32 devices in a mesh: expert: 4 (over y, x), shard: 8 (over z, core).
Axes of the slice: x: 2, y: 2, z: 4, core: 2. Of those that a mesh axis runs over, the one named last changes fastest.
Arguments:
- tokens: bfloat16 [32768, 768], P(('expert', 'shard')), may hold values from -6 to 6
- previous_logits: float32 [32768, 12], P(('expert', 'shard')), may hold values from -3 to 3
- routes: int32 [32768, 2], P(('expert', 'shard')), may hold values from 0 to 11, all different within a row
- prefix: int32 [32], P(('expert', 'shard')), may hold values from 1 to 1024
- slot_order: int32 [32, 1024], P(('expert', 'shard')), may hold values from 0 to 1023, each once within a row
- first_gain: bfloat16 [768], P('shard'), may hold values from 0.5 to 1.5
- query_weight: bfloat16 [768, 768], P('shard'), may hold values from -0.21875 to 0.21875
- key_weight: bfloat16 [768, 768], P('shard'), may hold values from -0.21875 to 0.21875
- value_weight: bfloat16 [768, 768], P('shard'), may hold values from -0.21875 to 0.21875
- output_weight: bfloat16 [768, 768], P('shard'), may hold values from -1.75 to 1.75
- second_gain: bfloat16 [768], P('shard'), may hold values from 0.5 to 1.5
- router_weight: bfloat16 [768, 12], P('shard'), may hold values from -0.109375 to 0.109375
- constant_mix: bfloat16 [768, 4], P('shard'), may hold values from -0.21875 to 0.21875
- constant_vectors: bfloat16 [2, 768], P(None, 'shard'), may hold values from -6 to 6
- gate_weight: bfloat16 [8, 768, 2048], P('expert', 'shard'), may hold values from -0.21875 to 0.21875
- up_weight: bfloat16 [8, 768, 2048], P('expert', 'shard'), may hold values from -0.21875 to 0.21875
- down_weight: bfloat16 [8, 2048, 768], P('expert', 'shard'), may hold values from -0.25 to 0.25
- cotangent: bfloat16 [32768, 768], P(('expert', 'shard')), may hold values from -6 to 6
Outputs:
- mixed: bfloat16 [32768, 768], P(('expert', 'shard'))
- tokens_grad: float32 [32768, 768], P(('expert', 'shard'))
- previous_grad: float32 [32768, 12], P(('expert', 'shard'))
- query_grad: float32 [768, 768], P('shard')
- key_grad: float32 [768, 768], P('shard')
- value_grad: float32 [768, 768], P('shard')
- output_grad: float32 [768, 768], P('shard')
- router_grad: float32 [768, 12], P('shard')
- mix_grad: float32 [768, 4], P('shard')
- vector_grad: float32 [2, 768], P(None, 'shard')
- first_grad: float32 [768], P('shard')
- second_grad: float32 [768], P('shard')
- gate_grad: float32 [8, 768, 2048], P('expert', 'shard')
- up_grad: float32 [8, 768, 2048], P('expert', 'shard')
- down_grad: float32 [8, 2048, 768], P('expert', 'shard')
The draws below stay inside these ranges and needn't reach their ends.
Inputs may be any that keep to these rules, and one draw needn't show every extreme that they name: `routes`: each token names two different experts; number 8 is the zero expert, 9 the copy expert, 10 and 11 the two constant experts. `slot_order`: each row is a permutation of its device's 1024 token indices.
All inputs are finite; a program needn't handle non-finite values.
Results may differ from the reference program's by a relative error of at most 0.022.
Values may be sent and summed in bfloat16 or wider, within the bound.
No kernel may reach another device: no remote copies, remote signals or barrier semaphores. Data moves between devices by JAX's collectives and lax.ppermute only.
A program may use at most 256 MiB of HBM per device.

```python
from functools import partial
import jax
import jax.numpy as jnp
from jax import lax

D = 768
HEADS = 12
HEAD_DIM = 64
FF = 2048
EXPERTS = 8
TOP = 2
ALL_EXP = 12
LEN = 1024
TOK_DEV = 1024
CAP = 168
SEQUENCES = 32
TOKENS = 32768
N_EXPERT = 4
N_SHARD = 8


def with_ends(entries, own_key, least, top_value):
    extent = entries.shape
    spot = [jax.random.randint(jax.random.fold_in(own_key, axis), (), 0, extent[axis]) for axis in range(len(extent))]
    entries = entries.at[tuple(spot)].set(least)
    longest = extent.index(max(extent))
    spot[longest] = (spot[longest] + 1) % extent[longest]
    return entries.at[tuple(spot)].set(top_value)


def strengthened(entries, rng, source, target, blocks, factor):
    def block_of(axis_at):
        return (jnp.arange(entries.shape[axis_at]) // (entries.shape[axis_at] // blocks)).reshape((-1,) + (1,) * (entries.ndim - 1 - axis_at))

    first = jax.random.permutation(rng, blocks)[block_of(target)]
    second = (block_of(target) + blocks // 2) % blocks
    return jnp.where((block_of(source) == first) | (block_of(source) == second), factor * entries, entries)


def block_scale(stream_key, extent, shards, least, top_value):
    level, own = 1.0, jax.random.fold_in(stream_key, 6)
    for dim, blocks in shards:
        steps = jnp.exp(jax.random.uniform(jax.random.fold_in(own, dim), (blocks,), jnp.float32, least / len(shards), top_value / len(shards)))
        level = level * jnp.repeat(steps, extent[dim] // blocks).reshape([-1 if axis == dim else 1 for axis in range(len(extent))])
    return level


def choose_distinct(key, rows, count, top, lift):
    order = jax.random.permutation(jax.random.fold_in(key, 1), count)
    boost = order
    for power in range(3):
        boost = boost * boost // count
    boost = boost * lift // count
    tickets = jax.random.randint(jax.random.fold_in(key, 2), (rows, count), 0, 4096) + boost
    sure = jax.random.permutation(jax.random.fold_in(key, 3), rows)[jnp.arange(count) % rows]
    tickets = jnp.where(jnp.arange(rows)[:, None] == sure[None, :], 1 << 14, tickets)
    merit = tickets * count + jnp.arange(count)
    return lax.top_k(merit.astype(jnp.int32), top)[1].astype(jnp.int32)


def centred(stream_key, shape, spread, bound, split=(), held_as=jnp.bfloat16):
    array = spread * jax.random.normal(stream_key, shape, jnp.float32)
    if split:
        array = array * block_scale(stream_key, shape, split, -0.22, 0.18)
    return jnp.clip(array, -bound, bound).astype(held_as)


def bell_draw_with(own_key, dims, width, reach, cuts, heavy, kind=jnp.bfloat16):
    array = width * jax.random.normal(own_key, dims, jnp.float32)
    if cuts:
        array = array * block_scale(own_key, dims, cuts, -0.22, 0.18)
    return jnp.clip(strengthened(array, jax.random.fold_in(own_key, 3), *heavy), -reach, reach).astype(kind)


def setup_inputs(seed: int = 0) -> dict:
    arg_keys = jax.random.split(jax.random.key(seed), 19)
    return {
        "tokens": bell_draw_with(arg_keys[0], (TOKENS, D), 1.0, 6.0, ((0, 32),), (0, 1, 32, 2.75)),
        "previous_logits": centred(arg_keys[1], (TOKENS, ALL_EXP), 0.5, 3.0, ((0, 32),), jnp.float32),
        "routes": choose_distinct(arg_keys[2], TOKENS, ALL_EXP, TOP, 1365),
        "prefix": with_ends(jax.random.randint(arg_keys[3], (SEQUENCES,), 1, LEN + 1), jax.random.fold_in(arg_keys[3], 1), 1, LEN).astype(jnp.int32),
        "slot_order": jax.vmap(lambda own: jax.random.permutation(own, TOK_DEV))(jax.random.split(arg_keys[4], (N_EXPERT * N_SHARD))).reshape((N_EXPERT * N_SHARD, TOK_DEV)).astype(jnp.int32),
        "first_gain": jnp.clip(1.0 + 0.1 * jax.random.normal(arg_keys[5], (D,), jnp.float32), 0.5, 1.5).astype(jnp.bfloat16),
        "query_weight": centred(arg_keys[6], (D, D), D ** -0.5, 0.21875, ((0, 8),)),
        "key_weight": centred(arg_keys[7], (D, D), D ** -0.5, 0.21875, ((0, 8),)),
        "value_weight": centred(arg_keys[8], (D, D), D ** -0.5, 0.21875, ((0, 8),)),
        "output_weight": centred(arg_keys[9], (D, D), (D // 64) ** -0.5, 1.75, ((0, 8),)),
        "second_gain": jnp.clip(1.0 + 0.1 * jax.random.normal(arg_keys[10], (D,), jnp.float32), 0.5, 1.5).astype(jnp.bfloat16),
        "router_weight": centred(arg_keys[11], (D, ALL_EXP), (4 * D) ** -0.5, 0.109375, ((0, 8),)),
        "constant_mix": centred(arg_keys[12], (D, 4), D ** -0.5, 0.21875, ((0, 8),)),
        "constant_vectors": centred(arg_keys[13], (2, D), 1.0, 6.0, ((1, 8),)),
        "gate_weight": centred(arg_keys[14], (EXPERTS, D, FF), D ** -0.5, 0.21875, ((0, 4), (1, 8))),
        "up_weight": centred(arg_keys[15], (EXPERTS, D, FF), D ** -0.5, 0.21875, ((0, 4), (1, 8))),
        "down_weight": centred(arg_keys[16], (EXPERTS, FF, D), (FF // 4) ** -0.5, 0.25, ((0, 4), (1, 8))),
        "cotangent": centred(arg_keys[17], (TOKENS, D), 1.0, 6.0, ((0, 32),)),
    }


EPS = 1e-05
NEG = -1e+30
highest = lax.Precision.HIGHEST

@jax.custom_vjp
def low(v):
    return lax.optimization_barrier(v.astype(jnp.bfloat16)).astype(jnp.float32)

@jax.custom_vjp
def low_back(v):
    return v

def low_keep(v):
    return (low(v), None)

def low_pass(kept, grad):
    return (grad,)

def back_keep(v):
    return (v, None)

def back_low(kept, grad):
    return (low(grad),)
low.defvjp(low_keep, low_pass)
low_back.defvjp(back_keep, back_low)

def matmul(left, right):
    return jnp.dot(left, right, precision=highest, preferred_element_type=jnp.float32)

def rms_norm(values, gain):
    scale_rows = lax.rsqrt(lax.optimization_barrier(jnp.mean(values * values, axis=-1, keepdims=True)) + EPS)
    return values * scale_rows * gain

def rotary_tables(length, head_dim):
    half_dim = head_dim // 2
    frequency = 10000.0 ** (-jnp.arange(half_dim, dtype=jnp.float32) * 2.0 / head_dim)
    angles = jnp.arange(length, dtype=jnp.float32)[:, None] * frequency[None, :]
    return (jnp.cos(angles), jnp.sin(angles))

def rotate(values, cosine_table, sine_table):
    half_dim = values.shape[-1] // 2
    first_half = values[..., :half_dim]
    second_half = values[..., half_dim:]
    cosine = cosine_table[:, None, :]
    sine_wave = sine_table[:, None, :]
    return jnp.concatenate([first_half * cosine - second_half * sine_wave, second_half * cosine + first_half * sine_wave], axis=-1)

def assign_slots(route_rows, turn_order, experts, capacity):
    tok_count = route_rows.shape[0]
    choices_count = route_rows.shape[1]
    ordered = route_rows[turn_order].reshape(-1)
    pair_ids = (turn_order[:, None] * choices_count + jnp.arange(choices_count, dtype=jnp.int32)[None, :]).reshape(-1)
    onehot = (ordered[:, None] == jnp.arange(experts, dtype=jnp.int32)[None, :]).astype(jnp.int32)
    earlier = jnp.cumsum(onehot, axis=0, dtype=jnp.int32) - onehot
    position = lax.optimization_barrier(jnp.sum(earlier * onehot, axis=1, dtype=jnp.int32))
    kept_pair = (ordered < experts) & (position < capacity)
    target = jnp.where(kept_pair, ordered * capacity + position, experts * capacity).astype(jnp.int32)
    slot_pair = jnp.full((experts * capacity,), choices_count * tok_count, jnp.int32).at[target].set(pair_ids, mode='drop')
    pair_dest = jnp.zeros((choices_count * tok_count,), jnp.int32).at[pair_ids].set(target)
    return (slot_pair, pair_dest.reshape(tok_count, choices_count))

def attend_sequence(operands):
    query_seq, keys_seq, values_seq, prefix_len = operands
    length = query_seq.shape[0]
    block_rows = min(512, length)
    key_pos = jnp.arange(length, dtype=jnp.int32)
    score_scale = HEAD_DIM ** (-0.5)

    def one_block(row_start):
        query_block = lax.dynamic_slice_in_dim(query_seq, row_start, block_rows, 0)
        query_pos = row_start + jnp.arange(block_rows, dtype=jnp.int32)
        visible = (key_pos[None, :] <= query_pos[:, None]) | (key_pos[None, :] < prefix_len)
        raw_scores = jnp.einsum('qhd,khd->hqk', query_block, keys_seq, precision=highest) * score_scale
        scores = low_back(jnp.where(visible[None], raw_scores, NEG))
        weights = low(jax.nn.softmax(scores, axis=-1))
        return jnp.einsum('hqk,khd->qhd', weights, values_seq, precision=highest)
    starts = jnp.arange(length // block_rows, dtype=jnp.int32) * block_rows
    outputs = lax.map(jax.checkpoint(one_block), starts)
    return outputs.reshape(length, -1)

def expert_block(operands):
    gate_in, up_in, down_in, rows_in = operands
    gate_pre = low_back(matmul(rows_in, gate_in))
    up_pre = low_back(matmul(rows_in, up_in))
    hidden = low(jax.nn.silu(gate_pre) * up_pre)
    return low_back(low(matmul(hidden, down_in)))

def forward(tokens, first_gain, query_weight, key_weight, value_weight, output_weight, second_gain, router_weight, constant_mix, constant_vectors, gate_weight, up_weight, down_weight, previous_logits, routes, prefix, slot_token, pair_dest):
    seq_count = tokens.shape[0] // LEN
    model_width = tokens.shape[1]
    normed_one = low(rms_norm(tokens, first_gain))
    query_lin = low_back(matmul(normed_one, query_weight))
    key_lin = low_back(matmul(normed_one, key_weight))
    values = low_back(low(matmul(normed_one, value_weight)))
    cosine_table, sine_table = rotary_tables(LEN, HEAD_DIM)
    head_shape = (seq_count, LEN, HEADS, HEAD_DIM)
    queries = low(rotate(query_lin.reshape(head_shape), cosine_table, sine_table))
    keys_rot = low(rotate(key_lin.reshape(head_shape), cosine_table, sine_table))
    mixed_heads = lax.map(jax.checkpoint(attend_sequence), (queries, keys_rot, values.reshape(head_shape), prefix))
    attn_mix = low_back(low(mixed_heads.reshape(-1, model_width)))
    residual = tokens + low_back(matmul(attn_mix, output_weight))
    normed_two = low(rms_norm(residual, second_gain))
    logits = matmul(normed_two, router_weight) + previous_logits
    chosen = jnp.take_along_axis(logits, routes, axis=1)
    gate_values = jax.nn.softmax(chosen, axis=-1)
    mix_weights = jax.nn.softmax(matmul(normed_two, constant_mix).reshape(-1, 2, 2), axis=-1)
    constant_out = mix_weights[..., 0:1] * normed_two[:, None, :] + mix_weights[..., 1:2] * constant_vectors[None]
    padded_rows = jnp.concatenate([normed_two, jnp.zeros((1, model_width), jnp.float32)], axis=0)
    device_count = slot_token.shape[0]
    expert_rows = low_back(padded_rows[slot_token])
    expert_rows = expert_rows.transpose(1, 0, 2, 3).reshape(EXPERTS, device_count * CAP, model_width)
    expert_out = lax.map(jax.checkpoint(expert_block), (gate_weight, up_weight, down_weight, expert_rows))
    expert_out = expert_out.reshape(EXPERTS, device_count, CAP, model_width).transpose(1, 0, 2, 3).reshape(-1, model_width)
    returned_pad = jnp.concatenate([expert_out, jnp.zeros((1, model_width), jnp.float32)], axis=0)
    expert_pair = returned_pad[pair_dest]
    route_col = routes[:, :, None]
    branch = jnp.where(route_col < EXPERTS, expert_pair, jnp.where(route_col == EXPERTS + 1, normed_two[:, None, :], jnp.where(route_col == EXPERTS + 2, constant_out[:, 0:1, :], jnp.where(route_col == EXPERTS + 3, constant_out[:, 1:2, :], 0.0))))
    return residual + lax.optimization_barrier(jnp.sum(gate_values[..., None] * branch, axis=1))

def reference(tokens, previous_logits, routes, prefix, slot_order, first_gain, query_weight, key_weight, value_weight, output_weight, second_gain, router_weight, constant_mix, constant_vectors, gate_weight, up_weight, down_weight, cotangent):
    device_count = N_EXPERT * N_SHARD
    tok_count = tokens.shape[0] // device_count
    slot_pair, pair_local = jax.vmap(partial(assign_slots, experts=EXPERTS, capacity=CAP))(routes.reshape(device_count, tok_count, 2), slot_order)
    device_ids = jnp.arange(device_count, dtype=jnp.int32)
    slot_token = jnp.where(slot_pair < 2 * tok_count, slot_pair // 2 + device_ids[:, None] * tok_count, device_count * tok_count)
    slot_token = slot_token.astype(jnp.int32).reshape(device_count, EXPERTS, CAP)
    per_device = EXPERTS * CAP
    pair_global = jnp.where(pair_local < per_device, pair_local + device_ids[:, None, None] * per_device, device_count * per_device)
    pair_global = pair_global.astype(jnp.int32).reshape(device_count * tok_count, 2)
    floats = tuple((argument.astype(jnp.float32) for argument in (tokens, first_gain, query_weight, key_weight, value_weight, output_weight, second_gain, router_weight, constant_mix, constant_vectors, gate_weight, up_weight, down_weight, previous_logits)))
    mixed_out, pullback = jax.vjp(partial(forward, routes=routes, prefix=prefix, slot_token=slot_token, pair_dest=pair_global), *floats)
    grads = pullback(cotangent.astype(jnp.float32))
    return (mixed_out.astype(jnp.bfloat16), grads[0], grads[13], grads[2], grads[3], grads[4], grads[5], grads[7], grads[8], grads[9], grads[1], grads[6], grads[10], grads[11], grads[12])
```

```python
import functools
import numpy as np
import jax
import jax.numpy as jnp
from jax import lax
from jax.experimental import pallas as pl
from jax.experimental.pallas import tpu as pltpu
from jax.sharding import PartitionSpec as P

HEADS = 12
HEAD_DIM = 64
ZC = 4
TOP = 2
LEN = 1024
EPS = 1e-05
NEG = -1e30
LANES = 128
BLOCK = 256
FTILE = 512
F32 = jnp.float32
BF16 = jnp.bfloat16
VMEM_LIMIT = 56 << 20


def call(body, name, grid, in_specs, out_specs, out_shape, scratch=(), flops=0, traffic=0, trans=0, prefetch=0):
    return pl.pallas_call(
        body,
        name=name,
        grid_spec=pltpu.PrefetchScalarGridSpec(
            num_scalar_prefetch=prefetch,
            grid=grid,
            in_specs=in_specs,
            out_specs=out_specs,
            scratch_shapes=scratch,
        ),
        out_shape=out_shape,
        compiler_params=pltpu.CompilerParams(
            dimension_semantics=("arbitrary",) * len(grid), vmem_limit_bytes=VMEM_LIMIT
        ),
        cost_estimate=pl.CostEstimate(flops=flops, transcendentals=trans, bytes_accessed=traffic),
    )


def mm(a, b):
    return lax.dot_general(a, b, (((1,), (0,)), ((), ())), preferred_element_type=F32)


def mm_nt(a, b):
    return lax.dot_general(a, b, (((1,), (1,)), ((), ())), preferred_element_type=F32)


def mm_tn(a, b):
    return lax.dot_general(a, b, (((0,), (0,)), ((), ())), preferred_element_type=F32)


def iota(shape, axis):
    return lax.broadcasted_iota(jnp.int32, shape, axis)


def whole(shape):
    return pl.BlockSpec(shape, lambda *idx: (0,) * len(shape))


def rows_of(block, width):
    return pl.BlockSpec((block, width), lambda i, *rest: (i, 0))


def split_high_low(values):
    high = values.astype(BF16)
    low = (values - high.astype(F32)).astype(BF16)
    return high, low


def pack_kernel(q, k, v, gain1, gain2, router, mix, vectors, out, scratch):
    rows, width = q.shape
    out[:, 0:width] = q[...]
    out[:, width : 2 * width] = k[...]
    out[:, 2 * width : 3 * width] = v[...]
    base = 3 * width
    out[:, base : base + LANES] = jnp.zeros((rows, LANES), BF16)
    scratch[...] = jnp.zeros_like(scratch)
    scratch[0:1, 0:rows] = gain1[...].astype(F32)
    scratch[1:2, 0:rows] = gain2[...].astype(F32)
    scratch[2:4, 0:rows] = vectors[...].astype(F32)
    columns = scratch[...].T
    n_router = router.shape[1]
    n_mix = mix.shape[1]
    out[:, base : base + n_router] = router[...]
    out[:, base + n_router : base + n_router + n_mix] = mix[...]
    out[:, base + 16 : base + 24] = columns[0:rows, 0:8].astype(BF16)


def slots_kernel(experts, capacity, stride, routes, order_row, order_col, dest_col, dest_row):
    tokens = routes.shape[0]
    r0 = routes[:, 0:1]
    r1 = routes[:, 1:2]
    lane = iota((tokens, LANES), 1)
    hot = jnp.where((lane == r0) | (lane == r1), 1.0, 0.0)
    hot = jnp.where(lane < experts, hot, 0.0).astype(BF16)
    row = iota((tokens, tokens), 0)
    col = iota((tokens, tokens), 1)
    to_turn = jnp.where(order_col[...] == col, 1.0, 0.0).astype(BF16)
    hot_turn = mm(to_turn, hot).astype(BF16)
    earlier = mm(jnp.where(col < row, 1.0, 0.0).astype(BF16), hot_turn)
    earlier = jnp.minimum(earlier, 255.0).astype(BF16)
    to_token = jnp.where(order_row[...] == row, 1.0, 0.0).astype(BF16)
    position = mm(to_token, earlier)
    p0 = jnp.sum(jnp.where(lane == r0, position, 0.0), axis=1, keepdims=True)
    p1 = jnp.sum(jnp.where(lane == r1, position, 0.0), axis=1, keepdims=True)
    d0 = jnp.where((r0 < experts) & (p0 < capacity), r0.astype(F32) * stride + p0, -1.0)
    d1 = jnp.where((r1 < experts) & (p1 < capacity), r1.astype(F32) * stride + p1, -1.0)
    both = jnp.where(lane == 0, d0, jnp.where(lane == 1, d1, 0.0))
    dest_col[...] = both.astype(jnp.int32)
    dest_row[...] = both.T[0:8, :].astype(jnp.int32)


def half_swap(values):
    lane = iota(values.shape, 1) % HEAD_DIM
    half = HEAD_DIM // 2
    return jnp.where(
        lane < half, pltpu.roll(values, LANES - half, 1), pltpu.roll(values, half, 1)
    )


def project_kernel(x, wq, wk, wv, small, cosine, sine, q_out, k_out, v_out, n_out, small_t):
    @pl.when(pl.program_id(0) == 0)
    def _():
        small_t[...] = small[...].astype(F32).T

    width = x.shape[1]
    rows = x[...].astype(F32)
    scale = lax.rsqrt(jnp.mean(rows * rows, axis=1, keepdims=True) + EPS)
    normed = (rows * scale * small_t[16:17, :]).astype(BF16)
    n_out[...] = normed
    cos = cosine[...]
    sin = sine[...]
    for weight, out, factor in ((wq, q_out, HEAD_DIM**-0.5), (wk, k_out, None)):
        lin = mm(normed, weight[...])
        for c in range(width // LANES):
            part = lin[:, c * LANES : (c + 1) * LANES]
            turned = part * cos + half_swap(part) * sin
            if factor is not None:
                turned = turned * factor
            out[:, c * LANES : (c + 1) * LANES] = turned.astype(BF16)
    v_out[...] = mm(normed, wv[...]).astype(BF16)


def attend_kernel(
    prefix, q, k, v, x, wo, small, small_t, prev, routes,
    mix_out, lse_out, res_out, n_out, tok_out, bias, mixed, lse,
):
    block, width = q.shape
    length = k.shape[0]
    start = pl.program_id(0) * block
    limit = jnp.maximum(start + iota((block, 1), 0) + 1, prefix[0])
    bias[...] = jnp.where(iota((block, length), 1) < limit, 0.0, NEG)
    lane = iota((block, LANES), 1)
    first = lane < HEAD_DIM
    lse[...] = jnp.zeros_like(lse)

    def one_pair(pair, carry):
        columns = pl.ds(pl.multiple_of(pair * LANES, LANES), LANES)
        q_pair = q[:, columns]
        k_pair = k[:, columns]
        v_pair = v[:, columns]
        outs = []
        for head in range(2):
            mine = first if head == 0 else jnp.logical_not(first)
            q_head = jnp.where(mine, q_pair, jnp.zeros_like(q_pair))
            scores = mm_nt(q_head, k_pair) + bias[...]
            top = jnp.max(scores, axis=1, keepdims=True)
            weights = jnp.exp(scores - top)
            total = jnp.sum(weights, axis=1, keepdims=True)
            outs.append(mm(weights.astype(BF16), v_pair) / total)
            lse[...] = jnp.where(lane == 2 * pair + head, top + jnp.log(total), lse[...])
        mixed[:, columns] = jnp.where(first, outs[0], outs[1]).astype(BF16)
        return carry

    lax.fori_loop(0, width // LANES, one_pair, 0)
    mix_out[...] = mixed[...]
    lse_out[...] = lse[...].T[0:16, :]
    residual = x[...].astype(F32) + mm(mixed[...], wo[...])
    res_out[...] = residual
    scale = lax.rsqrt(jnp.mean(residual * residual, axis=1, keepdims=True) + EPS)
    normed = (residual * scale * small_t[17:18, :]).astype(BF16)
    n_out[...] = normed
    lin = mm(normed, small[...])
    kinds = prev.shape[1]
    logits = lin[:, 0:kinds] + prev[...]
    kind = iota((block, kinds), 1)
    c0 = jnp.sum(jnp.where(kind == routes[:, 0:1], logits, 0.0), axis=1, keepdims=True)
    c1 = jnp.sum(jnp.where(kind == routes[:, 1:2], logits, 0.0), axis=1, keepdims=True)

    def pair_softmax(a, b):
        top = jnp.maximum(a, b)
        ea = jnp.exp(a - top)
        eb = jnp.exp(b - top)
        total = ea + eb
        return ea / total, eb / total

    g0, g1 = pair_softmax(c0, c1)
    m00, m01 = pair_softmax(lin[:, kinds : kinds + 1], lin[:, kinds + 1 : kinds + 2])
    m10, m11 = pair_softmax(lin[:, kinds + 2 : kinds + 3], lin[:, kinds + 3 : kinds + 4])
    packed = jnp.zeros((block, LANES), F32)
    for index, column in enumerate((g0, g1, m00, m01, m10, m11, scale)):
        packed = jnp.where(lane == index, column, packed)
    tok_out[...] = packed


def dispatch_kernel(normed, grad, tok, routes, dest_row, out, gates):
    expert = pl.program_id(0)
    tokens = normed.shape[0]
    stride = out.shape[3]

    @pl.when(expert == 0)
    def _():
        lane = iota((tokens, LANES), 1)
        kind = lane % HEAD_DIM
        value = jnp.where(kind == routes[:, 0:1], tok[:, 0:1], 0.0)
        value = value + jnp.where(kind == routes[:, 1:2], tok[:, 1:2], 0.0)
        high = value.astype(BF16).astype(F32)
        gates[...] = jnp.where(lane < HEAD_DIM, high, value - high).astype(BF16)

    slot = expert * stride + iota((stride, tokens), 0)
    hit = (dest_row[0:1, :] == slot) | (dest_row[1:2, :] == slot)
    take = jnp.where(hit, 1.0, 0.0).astype(BF16)
    out[0, 0, 0] = mm(take, normed[...]).astype(BF16)
    slot_gates = mm(take, gates[...])
    mine = iota((stride, LANES), 1) % HEAD_DIM == expert
    slot_gate = jnp.sum(jnp.where(mine, slot_gates, 0.0), axis=1, keepdims=True)
    out[0, 1, 0] = (mm(take, grad[...]) * slot_gate).astype(BF16)


def expert_up_kernel(rows, grads, gate, up, hidden, slope, silu_out, down_grad):
    n_src, stride, width = rows.shape[0], rows.shape[3], rows.shape[4]
    r = rows[...].reshape(n_src * stride, width)
    s = grads[...].reshape(n_src * stride, width)
    ftile = gate.shape[-1]
    gate_pre = mm(r, gate[...].reshape(width, ftile))
    up_pre = mm(r, up[...].reshape(width, ftile))
    sig = jax.nn.sigmoid(gate_pre)
    silu = gate_pre * sig
    hid = (silu * up_pre).astype(BF16)
    hidden[0] = hid
    silu_out[0] = silu.astype(BF16)
    slope[0] = (up_pre * (sig + silu * (1.0 - sig))).astype(BF16)
    down_grad[...] = mm_tn(hid, s).astype(BF16).reshape(down_grad.shape)


def expert_down_kernel(
    rows, grads, gate, up, down, hidden, slope, silu, back, grad_out, out_acc, row_acc
):
    step = pl.program_id(0)
    n_src, stride, width = rows.shape[0], rows.shape[3], rows.shape[4]
    count = n_src * stride
    ftile = gate.shape[-1]

    @pl.when(step == 0)
    def _():
        out_acc[...] = jnp.zeros_like(out_acc)
        row_acc[...] = jnp.zeros_like(row_acc)

    r = rows[...].reshape(count, width)
    s = grads[...].reshape(count, width)
    d = down[...].reshape(ftile, width)
    hidden_g = mm_nt(s, d)
    out_acc[...] += mm(hidden[0], d)
    gate_g = (hidden_g * slope[0].astype(F32)).astype(BF16)
    up_g = (hidden_g * silu[0].astype(F32)).astype(BF16)
    row_acc[...] += mm_nt(gate_g, gate[...].reshape(width, ftile)) + mm_nt(
        up_g, up[...].reshape(width, ftile)
    )
    shape = (grad_out.shape[0], grad_out.shape[2], ftile)
    grad_out[:, 0] = mm_tn(r, gate_g).astype(BF16).reshape(shape)
    grad_out[:, 1] = mm_tn(r, up_g).astype(BF16).reshape(shape)

    @pl.when(step == pl.num_programs(0) - 1)
    def _():
        back[:, 0] = out_acc[...].astype(BF16).reshape(n_src, stride, width)
        back[:, 1] = row_acc[...].astype(BF16).reshape(n_src, stride, width)


def combine_kernel(
    experts, eo0, rg0, eo1, rg1, residual, normed, grad, tok, routes, dest, mix, wo, small_t,
    mixed_out, prev_out, resg_out, headg_out, delta_out, wo_out, small_out, wo_acc, small_acc, second_acc,
):
    step = pl.program_id(0)
    block, width = residual.shape
    n_src, stride = eo0.shape[0], eo0.shape[2]
    local = n_src * stride

    @pl.when(step == 0)
    def _():
        wo_acc[...] = jnp.zeros_like(wo_acc)
        small_acc[...] = jnp.zeros_like(small_acc)
        second_acc[...] = jnp.zeros_like(second_acc)

    slot = iota((block, local), 1)
    owner_slot = slot // stride * (2 * stride) + slot % stride

    ep = [None, None]
    back = None
    for l, (eo_ref, rg_ref) in enumerate(((eo0, rg0), (eo1, rg1))):
        ident = owner_slot + l * stride
        t0 = jnp.where(dest[:, 0:1] == ident, 1.0, 0.0)
        t1 = jnp.where(dest[:, 1:2] == ident, 1.0, 0.0)
        eo = eo_ref[...].reshape(local, width)
        rg = rg_ref[...].reshape(local, width)
        e0 = mm(t0.astype(BF16), eo)
        e1 = mm(t1.astype(BF16), eo)
        b = mm((t0 + t1).astype(BF16), rg)
        ep[0] = e0 if ep[0] is None else ep[0] + e0
        ep[1] = e1 if ep[1] is None else ep[1] + e1
        back = b if back is None else back + b

    res = residual[...]
    n_low = normed[...]
    nf = n_low.astype(F32)
    g_low = grad[...]
    g = g_low.astype(F32)
    gate = [tok[:, 0:1], tok[:, 1:2]]
    mw = [[tok[:, 2:3], tok[:, 3:4]], [tok[:, 4:5], tok[:, 5:6]]]
    scale = tok[:, 6:7]
    vec = [small_t[18:19, :], small_t[19:20, :]]
    along_n = jnp.sum(g * nf, axis=1, keepdims=True)
    along_vec = [jnp.sum(g * vec[c], axis=1, keepdims=True) for c in range(2)]
    gate_g = []
    on_n = 0.0
    sel = [0.0, 0.0]
    copy_weight = 0.0
    for t in range(TOP):
        route = routes[:, t : t + 1]
        is_copy = jnp.where(route == experts + 1, 1.0, 0.0)
        is_const = [jnp.where(route == experts + 2 + c, 1.0, 0.0) for c in range(2)]
        a = is_copy + is_const[0] * mw[0][0] + is_const[1] * mw[1][0]
        b = [is_const[c] * mw[c][1] for c in range(2)]
        gate_g.append(
            jnp.sum(g * ep[t], axis=1, keepdims=True)
            + a * along_n
            + b[0] * along_vec[0]
            + b[1] * along_vec[1]
        )
        on_n = on_n + gate[t] * a
        copy_weight = copy_weight + gate[t] * is_copy
        sel = [sel[c] + gate[t] * is_const[c] for c in range(2)]
    vec_w = [sel[c] * mw[c][1] for c in range(2)]
    mixed_out[...] = (
        res + gate[0] * ep[0] + gate[1] * ep[1] + on_n * nf + vec_w[0] * vec[0] + vec_w[1] * vec[1]
    ).astype(BF16)

    centre = gate[0] * gate_g[0] + gate[1] * gate_g[1]
    pair_g = [gate[t] * (gate_g[t] - centre) for t in range(TOP)]
    lane = iota((block, LANES), 1)
    logit_g = jnp.where(lane == routes[:, 0:1], pair_g[0], 0.0)
    logit_g = logit_g + jnp.where(lane == routes[:, 1:2], pair_g[1], 0.0)
    kinds = prev_out.shape[1]
    prev_out[...] = logit_g[:, 0:kinds]
    for c in range(2):
        w0 = sel[c] * along_n
        w1 = sel[c] * along_vec[c]
        mid = mw[c][0] * w0 + mw[c][1] * w1
        logit_g = jnp.where(lane == kinds + 2 * c, mw[c][0] * (w0 - mid), logit_g)
        logit_g = jnp.where(lane == kinds + 2 * c + 1, mw[c][1] * (w1 - mid), logit_g)
    high, low = split_high_low(logit_g)
    table = small_t[...]
    table = jnp.where(iota(table.shape, 0) < 16, table, 0.0).astype(BF16)
    direct = copy_weight + sel[0] * mw[0][0] + sel[1] * mw[1][0]
    normed_g = back + direct * g + mm(high, table) + mm(low, table)
    gain = small_t[17:18, :]
    scaled = normed_g * gain
    second_acc[...] += jnp.sum(
        (normed_g * res * scale).reshape(block // 8, 8, width), axis=0
    )
    resg = g + scale * scaled - res * (scale * scale * scale) * jnp.mean(
        scaled * res, axis=1, keepdims=True
    )
    resg_out[...] = resg
    attn_g = resg.astype(BF16)
    am = mix[...]
    wo_acc[...] += mm_tn(am, attn_g)
    heads_g = mm_nt(attn_g, wo[...]).astype(BF16)
    headg_out[...] = heads_g
    product = heads_g.astype(F32) * am.astype(F32)
    p_high, p_low = split_high_low(product)
    head_of = jnp.where(
        iota((16, width), 1) // HEAD_DIM == iota((16, width), 0), 1.0, 0.0
    ).astype(BF16)
    delta_out[...] = mm_nt(head_of, p_high) + mm_nt(head_of, p_low)
    small_acc[...] += mm_tn(n_low, high) + mm_tn(n_low, low)
    coefficient = jnp.where(lane == 18, vec_w[0], jnp.where(lane == 19, vec_w[1], 0.0))
    c_high, c_low = split_high_low(coefficient)
    small_acc[...] += mm_tn(g_low, c_high) + mm_tn(g_low, c_low)

    @pl.when(step == pl.num_programs(0) - 1)
    def _():
        wo_out[...] = wo_acc[...].astype(BF16)
        second = jnp.sum(second_acc[...], axis=0, keepdims=True)
        row = iota((LANES, width), 0)
        small_out[...] = small_acc[...] + jnp.where(row == 17, second, 0.0).T


def attend_back_kernel(
    prefix, q, k, v, grad, lse, delta, cosine, sine, dq_out, dk_out, dv_out, bias, dq_acc
):
    length = q.shape[0]
    pair = pl.program_id(0)
    block = BLOCK
    lane_all = iota((length, LANES), 1)
    lane = iota((block, LANES), 1)

    @pl.when(pair == 0)
    def _():
        limit = jnp.maximum(iota((1, length), 1) + 1, prefix[0])
        bias[...] = jnp.where(iota((length, length), 0) < limit, 0.0, NEG).astype(BF16)

    q_pair = q[...]
    g_pair = grad[...]
    zero = jnp.zeros_like(q_pair)
    q_head = []
    g_head = []
    for head in range(2):
        mine = (lane_all // HEAD_DIM) == head
        q_head.append(jnp.where(mine, q_pair, zero))
        g_head.append(jnp.where(mine, g_pair, zero))
    dq_acc[...] = jnp.zeros_like(dq_acc)

    def one_block(index, carry):
        place = pl.ds(pl.multiple_of(index * block, block), block)
        k_pair = k[place, :]
        v_pair = v[place, :]
        dk = None
        dv = None
        for head in range(2):
            mine = (lane // HEAD_DIM) == head
            k_head = jnp.where(mine, k_pair, jnp.zeros_like(k_pair))
            lse_row = lse[pl.ds(2 * pair + head, 1), :]
            delta_row = delta[pl.ds(2 * pair + head, 1), :]
            scores = mm_nt(k_pair, q_head[head]) + bias[place, :].astype(F32)
            weights = jnp.exp(scores - lse_row)
            probs_g = mm_nt(v_pair, g_head[head])
            one_dv = mm(weights.astype(BF16), g_head[head])
            scores_g = (weights * (probs_g - delta_row)).astype(BF16)
            one_dk = mm(scores_g, q_head[head])
            dq_acc[...] += mm_tn(scores_g, k_head)
            dk = one_dk if dk is None else dk + one_dk
            dv = one_dv if dv is None else dv + one_dv
        cos = cosine[place, :]
        sin = sine[place, :]
        dk_out[place, :] = (dk * cos - half_swap(dk) * sin).astype(BF16)
        dv_out[place, :] = dv.astype(BF16)
        return carry

    lax.fori_loop(0, length // block, one_block, 0)
    dq = dq_acc[...] * (HEAD_DIM**-0.5)
    dq_out[...] = (dq * cosine[...] - half_swap(dq) * sine[...]).astype(BF16)


def project_back_kernel(
    x, normed, dq, dk, dv, resg, wq, wk, wv, small_t, small_g, tok_out, grad_out, acc, first_acc
):
    step = pl.program_id(0)
    block, width = x.shape

    @pl.when(step == 0)
    def _():
        acc[...] = jnp.zeros_like(acc)
        first_acc[...] = jnp.zeros_like(first_acc)

    rows = x[...].astype(F32)
    scale = lax.rsqrt(jnp.mean(rows * rows, axis=1, keepdims=True) + EPS)
    normed_g = mm_nt(dq[...], wq[...]) + mm_nt(dk[...], wk[...]) + mm_nt(dv[...], wv[...])
    n_low = normed[...]
    for index, part in enumerate((dq, dk, dv)):
        acc[:, index * width : (index + 1) * width] += mm_tn(n_low, part[...])
    first_acc[...] += jnp.sum(
        (normed_g * rows * scale).reshape(block // 8, 8, width), axis=0
    )
    scaled = normed_g * small_t[16:17, :]
    tok_out[...] = resg[...] + scale * scaled - rows * (scale * scale * scale) * jnp.mean(
        scaled * rows, axis=1, keepdims=True
    )

    @pl.when(step == pl.num_programs(0) - 1)
    def _():
        grad_out[:, 0 : 3 * width] = acc[...].astype(BF16)
        first = jnp.sum(first_acc[...], axis=0, keepdims=True)
        row = iota((LANES, width), 0)
        extra = small_g[...] + jnp.where(row == 16, first, 0.0).T
        grad_out[:, 3 * width : 3 * width + LANES] = extra.astype(BF16)


def rotary_tables():
    half = HEAD_DIM // 2
    frequency = np.float32(10000.0) ** (
        -np.arange(half, dtype=np.float32) * np.float32(2.0) / np.float32(HEAD_DIM)
    )
    angles = np.arange(LEN, dtype=np.float32)[:, None] * frequency[None, :].astype(np.float32)
    cos = np.cos(angles.astype(np.float64)).astype(np.float32)
    sin = np.sin(angles.astype(np.float64)).astype(np.float32)
    return np.tile(cos, (1, 4)), np.tile(np.concatenate([-sin, sin], axis=1), (1, 2))


def body(
    tokens, previous_logits, routes, prefix, slot_order, first_gain, query_weight, key_weight,
    value_weight, output_weight, second_gain, router_weight, constant_mix, constant_vectors,
    gate_weight, up_weight, down_weight, cotangent,
):
    owners = lax.axis_size("expert")
    shards = lax.axis_size("shard")
    local_experts, shard_rows, ff = gate_weight.shape
    experts = local_experts * owners
    count, width = tokens.shape
    kinds = experts + ZC
    capacity = count * TOP // kinds // 8 * 8
    stride = -(-capacity // 16) * 16
    ftile = FTILE
    fsteps = ff // ftile
    down_rows = down_weight.shape[1]
    per_tile = ftile // down_rows
    packed_width = 3 * width + LANES
    cosine, sine = (jnp.asarray(t) for t in rotary_tables())
    struct = jax.ShapeDtypeStruct

    packed = call(
        pack_kernel, "pack", (1,),
        [whole((shard_rows, width))] * 3
        + [whole((1, shard_rows))] * 2
        + [whole((shard_rows, kinds)), whole((shard_rows, 4)), whole((2, shard_rows))],
        whole((shard_rows, packed_width)),
        struct((shard_rows, packed_width), BF16),
        scratch=[pltpu.VMEM((8, LANES), F32)],
        traffic=1 << 20,
    )(
        query_weight, key_weight, value_weight, first_gain[None], second_gain[None],
        router_weight, constant_mix, constant_vectors,
    )
    qkv_full = lax.all_gather(packed, "shard", axis=0, tiled=True)
    output_full = lax.all_gather(output_weight, "shard", axis=0, tiled=True)
    gate_up = jnp.stack([gate_weight, up_weight], axis=1)
    gate_up_full = lax.all_gather(gate_up, "shard", axis=0, tiled=False)
    down_full = lax.all_gather(down_weight, "shard", axis=0, tiled=False)

    dest_col, dest_row = call(
        functools.partial(slots_kernel, experts, capacity, stride), "slots", (1,),
        [whole((count, TOP)), whole((1, count)), whole((count, 1))],
        [whole((count, LANES)), whole((8, count))],
        [struct((count, LANES), jnp.int32), struct((8, count), jnp.int32)],
        flops=2 * 3 * count * count * LANES, traffic=1 << 20,
    )(routes, slot_order, slot_order.reshape(count, 1))

    steps = count // BLOCK
    weight_block = [
        pl.BlockSpec((width, width), lambda i, *rest, j=j: (0, j)) for j in range(3)
    ]
    small_block = pl.BlockSpec((width, LANES), lambda i, *rest: (0, 3 * width // LANES))
    wide = rows_of(BLOCK, width)
    table = rows_of(BLOCK, LANES)
    act = struct((count, width), BF16)
    queries, keys, values, normed_one, small_t = call(
        project_kernel, "project", (steps,),
        [wide] + weight_block + [small_block, table, table],
        [wide] * 4 + [whole((LANES, width))],
        [act] * 4 + [struct((LANES, width), F32)],
        flops=6 * count * width * width, traffic=12 << 20,
    )(tokens, qkv_full, qkv_full, qkv_full, qkv_full, cosine, sine)

    attn_mix, lse, residual, normed_two, tok = call(
        attend_kernel, "attend", (steps,),
        [wide, whole((count, width)), whole((count, width)), wide, whole((width, width)),
         small_block, whole((LANES, width)), rows_of(BLOCK, kinds), rows_of(BLOCK, TOP)],
        [wide, pl.BlockSpec((16, BLOCK), lambda i, *rest: (0, i)), wide, wide, table],
        [act, struct((16, count), F32), struct((count, width), F32), act,
         struct((count, LANES), F32)],
        scratch=[pltpu.VMEM((BLOCK, count), F32), pltpu.VMEM((BLOCK, width), BF16),
                 pltpu.VMEM((BLOCK, LANES), F32)],
        flops=30 << 30, traffic=16 << 20, trans=HEADS * count * count, prefetch=1,
    )(prefix, queries, keys, values, tokens, output_full, qkv_full, small_t,
      previous_logits, routes)

    send = call(
        dispatch_kernel, "dispatch", (experts,),
        [whole((count, width)), whole((count, width)), whole((count, LANES)),
         whole((count, TOP)), whole((8, count))],
        pl.BlockSpec(
            (1, 2, 1, stride, width),
            lambda e: (e // local_experts, 0, e % local_experts, 0, 0),
        ),
        struct((owners, 2, local_experts, stride, width), BF16),
        scratch=[pltpu.VMEM((count, LANES), BF16)],
        flops=4 * experts * stride * count * width, traffic=8 << 20,
    )(normed_two, cotangent, tok, routes, dest_row)
    received = lax.all_to_all(send, "expert", split_axis=0, concat_axis=0, tiled=True)

    aligned = shard_rows % 16 == 0
    if aligned:
        chunks, chunk_rows = shards, shard_rows
        gate_up_kernel = gate_up_full
    else:
        chunks, chunk_rows = 1, width
        gate_up_kernel = gate_up_full.transpose(1, 2, 0, 3, 4).reshape(
            1, local_experts, 2, width, ff
        )
    local = owners * stride

    def part(kind, pick):
        return pl.BlockSpec(
            (owners, 1, 1, stride, width), lambda *idx: (0, kind, pick(*idx), 0, 0)
        )

    expert_flops = 2 * local * width * ff
    hidden_block = pl.BlockSpec((1, local, ftile), lambda l, f: (l, 0, f))
    hidden_shape = struct((local_experts, local, ff), BF16)
    hidden, slope, silu, down_grad = call(
        expert_up_kernel, "expert_up", (local_experts, fsteps),
        [part(0, lambda l, f: l), part(1, lambda l, f: l)]
        + [
            pl.BlockSpec((chunks, 1, 1, chunk_rows, ftile), lambda l, f, j=j: (0, l, j, 0, f))
            for j in range(2)
        ],
        [hidden_block] * 3
        + [pl.BlockSpec((per_tile, 1, down_rows, width), lambda l, f: (f, l, 0, 0))],
        [hidden_shape] * 3 + [struct((shards, local_experts, down_rows, width), BF16)],
        flops=3 * local_experts * expert_flops, traffic=35 << 20,
        trans=local_experts * local * ff,
    )(received, received, gate_up_kernel, gate_up_kernel)
    down_sum = lax.psum_scatter(down_grad, "shard", scatter_dimension=0, tiled=False)

    returned = []
    gate_up_sums = []
    for l in range(local_experts):
        pick = lambda f, l=l: l
        hid = pl.BlockSpec((1, local, ftile), lambda f, l=l: (l, 0, f))
        back, gu_grad = call(
            expert_down_kernel, "expert_down", (fsteps,),
            [part(0, pick), part(1, pick)]
            + [
                pl.BlockSpec(
                    (chunks, 1, 1, chunk_rows, ftile), lambda f, j=j, l=l: (0, l, j, 0, f)
                )
                for j in range(2)
            ]
            + [pl.BlockSpec((per_tile, 1, down_rows, width), lambda f, l=l: (f, l, 0, 0))]
            + [hid] * 3,
            [whole((owners, 2, stride, width)),
             pl.BlockSpec((chunks, 2, chunk_rows, ftile), lambda f: (0, 0, 0, f))],
            [struct((owners, 2, stride, width), BF16),
             struct((chunks, 2, chunk_rows, ff), BF16)],
            scratch=[pltpu.VMEM((local, width), F32)] * 2,
            flops=6 * expert_flops, traffic=30 << 20,
        )(received, received, gate_up_kernel, gate_up_kernel, down_full, hidden, slope, silu)
        if not aligned:
            gu_grad = gu_grad.reshape(2, shards, shard_rows, ff).transpose(1, 0, 2, 3)
        gate_up_sums.append(
            lax.psum_scatter(gu_grad, "shard", scatter_dimension=0, tiled=False)
        )
        returned.append(
            lax.all_to_all(back, "expert", split_axis=0, concat_axis=0, tiled=True)
        )

    def kind_block(kind):
        return pl.BlockSpec((owners, 1, stride, width), lambda i: (0, kind, 0, 0))

    mixed, previous_grad, residual_grad, heads_grad, delta, output_grad, small_grad = call(
        functools.partial(combine_kernel, experts), "combine", (steps,),
        [kind_block(0), kind_block(1)] * 2
        + [wide, wide, wide, table, rows_of(BLOCK, TOP), table, wide, whole((width, width)),
           whole((LANES, width))],
        [wide, rows_of(BLOCK, kinds), wide, wide, pl.BlockSpec((16, BLOCK), lambda i: (0, i)),
         whole((width, width)), whole((width, LANES))],
        [act, struct((count, kinds), F32), struct((count, width), F32), act,
         struct((16, count), F32), struct((width, width), BF16), struct((width, LANES), F32)],
        scratch=[pltpu.VMEM((width, width), F32), pltpu.VMEM((width, LANES), F32),
                 pltpu.VMEM((8, width), F32)],
        flops=6 * count * 2 * local * width + 4 * count * width * width, traffic=24 << 20,
    )(returned[0], returned[0], returned[1], returned[1], residual, normed_two, cotangent, tok,
      routes, dest_col, attn_mix, output_full, small_t)
    output_sum = lax.psum_scatter(output_grad, "shard", scatter_dimension=0, tiled=True)

    pair_block = pl.BlockSpec((count, LANES), lambda i, *rest: (0, i))
    dq, dk, dv = call(
        attend_back_kernel, "attend_back", (width // LANES,),
        [pair_block] * 4
        + [whole((16, count))] * 2
        + [whole((count, LANES))] * 2,
        [pair_block] * 3,
        [act] * 3,
        scratch=[pltpu.VMEM((count, count), BF16), pltpu.VMEM((count, LANES), F32)],
        flops=60 << 30, traffic=12 << 20, trans=HEADS * count * count, prefetch=1,
    )(prefix, queries, keys, values, heads_grad, lse, delta, cosine, sine)

    tokens_grad, dense_grad = call(
        project_back_kernel, "project_back", (steps,),
        [wide] * 6 + weight_block + [whole((LANES, width)), whole((width, LANES))],
        [wide, whole((width, packed_width))],
        [struct((count, width), F32), struct((width, packed_width), BF16)],
        scratch=[pltpu.VMEM((width, 3 * width), F32), pltpu.VMEM((8, width), F32)],
        flops=12 * count * width * width, traffic=24 << 20,
    )(tokens, normed_one, dq, dk, dv, residual_grad, qkv_full, qkv_full, qkv_full, small_t,
      small_grad)
    dense_sum = lax.psum_scatter(dense_grad, "shard", scatter_dimension=0, tiled=True)
    dense_all = lax.all_gather(
        jnp.concatenate([dense_sum, output_sum], axis=1), "expert", axis=0, tiled=False
    )
    dense = jnp.sum(dense_all.astype(F32), axis=0)
    small = dense[:, 3 * width : 3 * width + LANES]
    gate_sum = jnp.stack([s[0] for s in gate_up_sums]).astype(F32)
    up_sum = jnp.stack([s[1] for s in gate_up_sums]).astype(F32)
    return (
        mixed,
        tokens_grad,
        previous_grad,
        dense[:, 0:width],
        dense[:, width : 2 * width],
        dense[:, 2 * width : 3 * width],
        dense[:, packed_width:],
        small[:, 0:kinds],
        small[:, kinds : kinds + 4],
        small[:, 18:20].T,
        small[:, 16],
        small[:, 17],
        gate_sum,
        up_sum,
        down_sum.astype(F32),
    )


def solution(mesh):
    rows = P(("expert", "shard"), None)
    expert = P("expert", "shard", None)
    flat = P("shard", None)
    return jax.shard_map(
        body,
        mesh=mesh,
        in_specs=(
            rows, rows, rows, P(("expert", "shard")), rows, P("shard"), flat, flat, flat, flat,
            P("shard"), flat, flat, P(None, "shard"), expert, expert, expert, rows,
        ),
        out_specs=(
            rows, rows, rows, flat, flat, flat, flat, flat, flat, P(None, "shard"), P("shard"),
            P("shard"), expert, expert, expert,
        ),
        check_vma=False,
    )
```

```python
import functools
import numpy as np
import jax
import jax.numpy as jnp
from jax import lax
from jax.experimental import pallas as pl
from jax.experimental.pallas import tpu as pltpu
from jax.sharding import PartitionSpec as P

HEADS = 12
HEAD_DIM = 64
ZC = 4
TOP = 2
LEN = 1024
EPS = 1e-05
NEG = -1e30
LANES = 128
BLOCK = 256
TILE = 256
F32 = jnp.float32
BF16 = jnp.bfloat16
VMEM_LIMIT = 56 << 20


def call(body, name, grid, in_specs, out_specs, out_shape, scratch=(), flops=0, traffic=0, trans=0, prefetch=0):
    return pl.pallas_call(
        body,
        name=name,
        grid_spec=pltpu.PrefetchScalarGridSpec(
            num_scalar_prefetch=prefetch,
            grid=grid,
            in_specs=in_specs,
            out_specs=out_specs,
            scratch_shapes=scratch,
        ),
        out_shape=out_shape,
        compiler_params=pltpu.CompilerParams(
            dimension_semantics=("arbitrary",) * len(grid), vmem_limit_bytes=VMEM_LIMIT
        ),
        cost_estimate=pl.CostEstimate(flops=flops, transcendentals=trans, bytes_accessed=traffic),
    )


def mm(a, b):
    return lax.dot_general(a, b, (((1,), (0,)), ((), ())), preferred_element_type=F32)


def mm_nt(a, b):
    return lax.dot_general(a, b, (((1,), (1,)), ((), ())), preferred_element_type=F32)


def mm_tn(a, b):
    return lax.dot_general(a, b, (((0,), (0,)), ((), ())), preferred_element_type=F32)


def iota(shape, axis):
    return lax.broadcasted_iota(jnp.int32, shape, axis)


def whole(shape):
    return pl.BlockSpec(shape, lambda *idx: (0,) * len(shape))


def rows_of(block, width):
    return pl.BlockSpec((block, width), lambda i, *rest: (i, 0))


def split_high_low(values):
    high = values.astype(BF16)
    low = (values - high.astype(F32)).astype(BF16)
    return high, low


def pack_kernel(q, k, v, gain1, gain2, router, mix, vectors, out, scratch):
    rows, width = q.shape
    out[:, 0:width] = q[...]
    out[:, width : 2 * width] = k[...]
    out[:, 2 * width : 3 * width] = v[...]
    base = 3 * width
    out[:, base : base + LANES] = jnp.zeros((rows, LANES), BF16)
    scratch[...] = jnp.zeros_like(scratch)
    scratch[0:1, 0:rows] = gain1[...].astype(F32)
    scratch[1:2, 0:rows] = gain2[...].astype(F32)
    scratch[2:4, 0:rows] = vectors[...].astype(F32)
    columns = scratch[...].T
    n_router = router.shape[1]
    n_mix = mix.shape[1]
    out[:, base : base + n_router] = router[...]
    out[:, base + n_router : base + n_router + n_mix] = mix[...]
    out[:, base + 16 : base + 24] = columns[0:rows, 0:8].astype(BF16)


def slots_kernel(experts, capacity, stride, routes, order_row, order_col, dest_col, dest_row):
    tokens = routes.shape[0]
    r0 = routes[:, 0:1]
    r1 = routes[:, 1:2]
    lane = iota((tokens, LANES), 1)
    hot = jnp.where((lane == r0) | (lane == r1), 1.0, 0.0)
    hot = jnp.where(lane < experts, hot, 0.0).astype(BF16)
    row = iota((tokens, tokens), 0)
    col = iota((tokens, tokens), 1)
    to_turn = jnp.where(order_col[...] == col, 1.0, 0.0).astype(BF16)
    hot_turn = mm(to_turn, hot).astype(BF16)
    earlier = mm(jnp.where(col < row, 1.0, 0.0).astype(BF16), hot_turn)
    earlier = jnp.minimum(earlier, 255.0).astype(BF16)
    to_token = jnp.where(order_row[...] == row, 1.0, 0.0).astype(BF16)
    position = mm(to_token, earlier)
    p0 = jnp.sum(jnp.where(lane == r0, position, 0.0), axis=1, keepdims=True)
    p1 = jnp.sum(jnp.where(lane == r1, position, 0.0), axis=1, keepdims=True)
    d0 = jnp.where((r0 < experts) & (p0 < capacity), r0.astype(F32) * stride + p0, -1.0)
    d1 = jnp.where((r1 < experts) & (p1 < capacity), r1.astype(F32) * stride + p1, -1.0)
    both = jnp.where(lane == 0, d0, jnp.where(lane == 1, d1, 0.0))
    dest_col[...] = both.astype(jnp.int32)
    dest_row[...] = both.T[0:8, :].astype(jnp.int32)


def half_swap(values):
    lane = iota(values.shape, 1) % HEAD_DIM
    half = HEAD_DIM // 2
    return jnp.where(
        lane < half, pltpu.roll(values, LANES - half, 1), pltpu.roll(values, half, 1)
    )


def project_kernel(x, wq, wk, wv, small, cosine, sine, q_out, k_out, v_out, n_out, small_t):
    @pl.when(pl.program_id(0) == 0)
    def _():
        small_t[...] = small[...].astype(F32).T

    width = x.shape[1]
    rows = x[...].astype(F32)
    scale = lax.rsqrt(jnp.mean(rows * rows, axis=1, keepdims=True) + EPS)
    normed = (rows * scale * small_t[16:17, :]).astype(BF16)
    n_out[...] = normed
    cos = cosine[...]
    sin = sine[...]
    for weight, out, factor in ((wq, q_out, HEAD_DIM**-0.5), (wk, k_out, None)):
        lin = mm(normed, weight[...])
        for c in range(width // LANES):
            part = lin[:, c * LANES : (c + 1) * LANES]
            turned = part * cos + half_swap(part) * sin
            if factor is not None:
                turned = turned * factor
            out[:, c * LANES : (c + 1) * LANES] = turned.astype(BF16)
    v_out[...] = mm(normed, wv[...]).astype(BF16)


def attend_kernel(
    prefix, q, k, v, x, wo, small, small_t, prev, routes,
    mix_out, lse_out, res_out, n_out, tok_out, bias, mixed, lse,
):
    block, width = q.shape
    length = k.shape[0]
    start = pl.program_id(0) * block
    limit = jnp.maximum(start + iota((block, 1), 0) + 1, prefix[0])
    bias[...] = jnp.where(iota((block, length), 1) < limit, 0.0, NEG)
    lane = iota((block, LANES), 1)
    first = lane < HEAD_DIM
    lse[...] = jnp.zeros_like(lse)

    def one_pair(pair, carry):
        columns = pl.ds(pl.multiple_of(pair * LANES, LANES), LANES)
        q_pair = q[:, columns]
        k_pair = k[:, columns]
        v_pair = v[:, columns]
        outs = []
        for head in range(2):
            mine = first if head == 0 else jnp.logical_not(first)
            q_head = jnp.where(mine, q_pair, jnp.zeros_like(q_pair))
            scores = mm_nt(q_head, k_pair) + bias[...]
            top = jnp.max(scores, axis=1, keepdims=True)
            weights = jnp.exp(scores - top)
            total = jnp.sum(weights, axis=1, keepdims=True)
            outs.append(mm(weights.astype(BF16), v_pair) / total)
            lse[...] = jnp.where(lane == 2 * pair + head, top + jnp.log(total), lse[...])
        mixed[:, columns] = jnp.where(first, outs[0], outs[1]).astype(BF16)
        return carry

    lax.fori_loop(0, width // LANES, one_pair, 0)
    mix_out[...] = mixed[...]
    lse_out[...] = lse[...].T[0:16, :]
    residual = x[...].astype(F32) + mm(mixed[...], wo[...])
    res_out[...] = residual
    scale = lax.rsqrt(jnp.mean(residual * residual, axis=1, keepdims=True) + EPS)
    normed = (residual * scale * small_t[17:18, :]).astype(BF16)
    n_out[...] = normed
    lin = mm(normed, small[...])
    kinds = prev.shape[1]
    logits = lin[:, 0:kinds] + prev[...]
    kind = iota((block, kinds), 1)
    c0 = jnp.sum(jnp.where(kind == routes[:, 0:1], logits, 0.0), axis=1, keepdims=True)
    c1 = jnp.sum(jnp.where(kind == routes[:, 1:2], logits, 0.0), axis=1, keepdims=True)

    def pair_softmax(a, b):
        top = jnp.maximum(a, b)
        ea = jnp.exp(a - top)
        eb = jnp.exp(b - top)
        total = ea + eb
        return ea / total, eb / total

    g0, g1 = pair_softmax(c0, c1)
    m00, m01 = pair_softmax(lin[:, kinds : kinds + 1], lin[:, kinds + 1 : kinds + 2])
    m10, m11 = pair_softmax(lin[:, kinds + 2 : kinds + 3], lin[:, kinds + 3 : kinds + 4])
    packed = jnp.zeros((block, LANES), F32)
    for index, column in enumerate((g0, g1, m00, m01, m10, m11, scale)):
        packed = jnp.where(lane == index, column, packed)
    tok_out[...] = packed


def pack_expert_kernel(gate, up, down, out):
    rows, ff = gate.shape[1:]
    down_rows, width = down.shape[1:]
    tiles = ff // TILE
    for index, ref in enumerate((gate, up)):
        for f in range(tiles):
            start = (index * tiles + f) * rows
            out[start : start + rows, :] = ref[0, :, f * TILE : (f + 1) * TILE]
    base = 2 * tiles * rows
    for c in range(width // TILE):
        out[base + c * down_rows : base + (c + 1) * down_rows, :] = down[
            0, :, c * TILE : (c + 1) * TILE
        ]


def unpack_expert_kernel(*refs):
    gate, up, down = refs[-3:]
    rows, ff = gate.shape[1:]
    down_rows, width = down.shape[1:]
    tiles = ff // TILE
    base = 2 * tiles * rows
    for l, ref in enumerate(refs[:-3]):
        for index, out in enumerate((gate, up)):
            for f in range(tiles):
                start = (index * tiles + f) * rows
                out[l, :, f * TILE : (f + 1) * TILE] = ref[start : start + rows, :].astype(F32)
        for c in range(width // TILE):
            down[l, :, c * TILE : (c + 1) * TILE] = ref[
                base + c * down_rows : base + (c + 1) * down_rows, :
            ].astype(F32)


def dispatch_kernel(local_experts, l, me, normed, grad, tok, routes, dest_row, *rest):
    outs, gates = rest[:-1], rest[-1]
    step = pl.program_id(0)
    tokens = normed.shape[0]
    stride = outs[0].shape[1]
    expert = (me[0] ^ step) * local_experts + l

    @pl.when(step == 0)
    def _():
        lane = iota((tokens, LANES), 1)
        kind = lane % HEAD_DIM
        value = jnp.where(kind == routes[:, 0:1], tok[:, 0:1], 0.0)
        value = value + jnp.where(kind == routes[:, 1:2], tok[:, 1:2], 0.0)
        high = value.astype(BF16).astype(F32)
        gates[...] = jnp.where(lane < HEAD_DIM, high, value - high).astype(BF16)

    slot = expert * stride + iota((stride, tokens), 0)
    hit = (dest_row[0:1, :] == slot) | (dest_row[1:2, :] == slot)
    take = jnp.where(hit, 1.0, 0.0).astype(BF16)
    row = mm(take, normed[...]).astype(BF16)
    slot_gates = mm(take, gates[...])
    mine = iota((stride, LANES), 1) % HEAD_DIM == expert
    slot_gate = jnp.sum(jnp.where(mine, slot_gates, 0.0), axis=1, keepdims=True)
    slot_g = (mm(take, grad[...]) * slot_gate).astype(BF16)
    for k, out in enumerate(outs):

        @pl.when(step == k)
        def _():
            out[0] = row
            out[1] = slot_g


def expert_kernel(owners, merged, *refs):
    sent = refs[:owners]
    weights = refs[owners : owners + 6]
    backs = refs[owners + 6 : 2 * owners + 6]
    grads = refs[2 * owners + 6 : -4]
    r_all, s_all, out_acc, row_acc = refs[-4:]
    step = pl.program_id(0)
    steps = pl.num_programs(0)
    stride, width = sent[0].shape[1:]
    chunks, chunk_rows = weights[0].shape[:2]

    @pl.when(step == 0)
    def _():
        for k, ref in enumerate(sent):
            r_all[k * stride : (k + 1) * stride, :] = ref[0]
            s_all[k * stride : (k + 1) * stride, :] = ref[1]
        out_acc[...] = jnp.zeros_like(out_acc)
        row_acc[...] = jnp.zeros_like(row_acc)

    def tile_pair(a, b):
        return jnp.concatenate([t[...].reshape(width, TILE) for t in (a, b)], axis=1)

    def down_tile(ref):
        parts = [ref[0, c * TILE : (c + 1) * TILE, :] for c in range(width // TILE)]
        return jnp.concatenate(parts, axis=1)

    r = r_all[...]
    s = s_all[...]
    gate = tile_pair(weights[0], weights[1])
    up = tile_pair(weights[2], weights[3])
    d = jnp.concatenate([down_tile(weights[4]), down_tile(weights[5])], axis=0)
    gate_pre = mm(r, gate)
    up_pre = mm(r, up)
    sig = jax.nn.sigmoid(gate_pre)
    silu = gate_pre * sig
    hid = (silu * up_pre).astype(BF16)
    hidden_g = mm_nt(s, d)
    out_acc[...] += mm(hid, d)
    gate_g = (hidden_g * (up_pre * (sig + silu * (1.0 - sig)))).astype(BF16)
    up_g = (hidden_g * silu).astype(BF16)
    row_acc[...] += mm_nt(gate_g, gate) + mm_nt(up_g, up)
    down_grad = mm_tn(hid, s).astype(BF16)
    gate_grad = mm_tn(r, gate_g).astype(BF16)
    up_grad = mm_tn(r, up_g).astype(BF16)
    base = 4 * steps * chunk_rows if merged else 0
    for i in range(2):
        tile = 2 * step + i
        for index, value in enumerate((gate_grad, up_grad)):
            start = pl.multiple_of((index * 2 * steps + tile) * chunk_rows, 16)
            grads[0][:, pl.ds(start, chunk_rows), :] = value[:, i * TILE : (i + 1) * TILE].reshape(
                chunks, chunk_rows, TILE
            )
        for c in range(width // TILE):
            grads[-1][tile, base + c * TILE : base + (c + 1) * TILE, :] = down_grad[
                i * TILE : (i + 1) * TILE, c * TILE : (c + 1) * TILE
            ]

    @pl.when(step == steps - 1)
    def _():
        for k, ref in enumerate(backs):
            ref[0] = out_acc[k * stride : (k + 1) * stride, :].astype(BF16)
            ref[1] = row_acc[k * stride : (k + 1) * stride, :].astype(BF16)


def combine_kernel(experts, owners, local_experts, me, *refs):
    backs = refs[: owners * local_experts]
    (
        residual, normed, grad, tok, routes, dest, mix, wo, small_t,
        mixed_out, prev_out, resg_out, headg_out, delta_out, wo_out, small_out,
        wo_acc, small_acc, second_acc, eo_all, rg_all,
    ) = refs[owners * local_experts :]
    step = pl.program_id(0)
    block, width = residual.shape
    stride = backs[0].shape[1]
    local = owners * stride

    @pl.when(step == 0)
    def _():
        wo_acc[...] = jnp.zeros_like(wo_acc)
        small_acc[...] = jnp.zeros_like(small_acc)
        second_acc[...] = jnp.zeros_like(second_acc)
        for l in range(local_experts):
            for k in range(owners):
                place = slice(k * stride, (k + 1) * stride)
                eo_all[l, place, :] = backs[l * owners + k][0]
                rg_all[l, place, :] = backs[l * owners + k][1]

    slot = iota((1, local), 1)
    owner_slot = ((slot // stride) ^ me[0]) * (local_experts * stride) + slot % stride

    ep = [None, None]
    back = None
    for l in range(local_experts):
        ident = owner_slot + l * stride
        t0 = jnp.where(dest[:, 0:1] == ident, 1.0, 0.0)
        t1 = jnp.where(dest[:, 1:2] == ident, 1.0, 0.0)
        eo = eo_all[l]
        rg = rg_all[l]
        e0 = mm(t0.astype(BF16), eo)
        e1 = mm(t1.astype(BF16), eo)
        b = mm((t0 + t1).astype(BF16), rg)
        ep[0] = e0 if ep[0] is None else ep[0] + e0
        ep[1] = e1 if ep[1] is None else ep[1] + e1
        back = b if back is None else back + b

    res = residual[...]
    n_low = normed[...]
    nf = n_low.astype(F32)
    g_low = grad[...]
    g = g_low.astype(F32)
    gate = [tok[:, 0:1], tok[:, 1:2]]
    mw = [[tok[:, 2:3], tok[:, 3:4]], [tok[:, 4:5], tok[:, 5:6]]]
    scale = tok[:, 6:7]
    vec = [small_t[18:19, :], small_t[19:20, :]]
    along_n = jnp.sum(g * nf, axis=1, keepdims=True)
    along_vec = [jnp.sum(g * vec[c], axis=1, keepdims=True) for c in range(2)]
    gate_g = []
    on_n = 0.0
    sel = [0.0, 0.0]
    copy_weight = 0.0
    for t in range(TOP):
        route = routes[:, t : t + 1]
        is_copy = jnp.where(route == experts + 1, 1.0, 0.0)
        is_const = [jnp.where(route == experts + 2 + c, 1.0, 0.0) for c in range(2)]
        a = is_copy + is_const[0] * mw[0][0] + is_const[1] * mw[1][0]
        b = [is_const[c] * mw[c][1] for c in range(2)]
        gate_g.append(
            jnp.sum(g * ep[t], axis=1, keepdims=True)
            + a * along_n
            + b[0] * along_vec[0]
            + b[1] * along_vec[1]
        )
        on_n = on_n + gate[t] * a
        copy_weight = copy_weight + gate[t] * is_copy
        sel = [sel[c] + gate[t] * is_const[c] for c in range(2)]
    vec_w = [sel[c] * mw[c][1] for c in range(2)]
    mixed_out[...] = (
        res + gate[0] * ep[0] + gate[1] * ep[1] + on_n * nf + vec_w[0] * vec[0] + vec_w[1] * vec[1]
    ).astype(BF16)

    centre = gate[0] * gate_g[0] + gate[1] * gate_g[1]
    pair_g = [gate[t] * (gate_g[t] - centre) for t in range(TOP)]
    lane = iota((block, LANES), 1)
    logit_g = jnp.where(lane == routes[:, 0:1], pair_g[0], 0.0)
    logit_g = logit_g + jnp.where(lane == routes[:, 1:2], pair_g[1], 0.0)
    kinds = prev_out.shape[1]
    prev_out[...] = logit_g[:, 0:kinds]
    for c in range(2):
        w0 = sel[c] * along_n
        w1 = sel[c] * along_vec[c]
        mid = mw[c][0] * w0 + mw[c][1] * w1
        logit_g = jnp.where(lane == kinds + 2 * c, mw[c][0] * (w0 - mid), logit_g)
        logit_g = jnp.where(lane == kinds + 2 * c + 1, mw[c][1] * (w1 - mid), logit_g)
    high, low = split_high_low(logit_g)
    table = small_t[...]
    table = jnp.where(iota(table.shape, 0) < 16, table, 0.0).astype(BF16)
    direct = copy_weight + sel[0] * mw[0][0] + sel[1] * mw[1][0]
    normed_g = back + direct * g + mm(high, table) + mm(low, table)
    gain = small_t[17:18, :]
    scaled = normed_g * gain
    second_acc[...] += jnp.sum(
        (normed_g * res * scale).reshape(block // 8, 8, width), axis=0
    )
    resg = g + scale * scaled - res * (scale * scale * scale) * jnp.mean(
        scaled * res, axis=1, keepdims=True
    )
    resg_out[...] = resg
    attn_g = resg.astype(BF16)
    am = mix[...]
    wo_acc[...] += mm_tn(am, attn_g)
    heads_g = mm_nt(attn_g, wo[...]).astype(BF16)
    headg_out[...] = heads_g
    product = heads_g.astype(F32) * am.astype(F32)
    p_high, p_low = split_high_low(product)
    head_of = jnp.where(
        iota((16, width), 1) // HEAD_DIM == iota((16, width), 0), 1.0, 0.0
    ).astype(BF16)
    delta_out[...] = mm_nt(head_of, p_high) + mm_nt(head_of, p_low)
    small_acc[...] += mm_tn(n_low, high) + mm_tn(n_low, low)
    coefficient = jnp.where(lane == 18, vec_w[0], jnp.where(lane == 19, vec_w[1], 0.0))
    c_high, c_low = split_high_low(coefficient)
    small_acc[...] += mm_tn(g_low, c_high) + mm_tn(g_low, c_low)

    @pl.when(step == pl.num_programs(0) - 1)
    def _():
        wo_out[...] = wo_acc[...].astype(BF16)
        second = jnp.sum(second_acc[...], axis=0, keepdims=True)
        row = iota((LANES, width), 0)
        small_out[...] = small_acc[...] + jnp.where(row == 17, second, 0.0).T


def attend_back_kernel(
    prefix, q, k, v, grad, lse, delta, cosine, sine, dq_out, dk_out, dv_out, bias, dq_acc
):
    length = q.shape[0]
    pair = pl.program_id(0)
    block = BLOCK
    lane_all = iota((length, LANES), 1)
    lane = iota((block, LANES), 1)

    @pl.when(pair == 0)
    def _():
        limit = jnp.maximum(iota((1, length), 1) + 1, prefix[0])
        bias[...] = jnp.where(iota((length, length), 0) < limit, 0.0, NEG).astype(BF16)

    q_pair = q[...]
    g_pair = grad[...]
    zero = jnp.zeros_like(q_pair)
    q_head = []
    g_head = []
    for head in range(2):
        mine = (lane_all // HEAD_DIM) == head
        q_head.append(jnp.where(mine, q_pair, zero))
        g_head.append(jnp.where(mine, g_pair, zero))
    dq_acc[...] = jnp.zeros_like(dq_acc)

    def one_block(index, carry):
        place = pl.ds(pl.multiple_of(index * block, block), block)
        k_pair = k[place, :]
        v_pair = v[place, :]
        dk = None
        dv = None
        for head in range(2):
            mine = (lane // HEAD_DIM) == head
            k_head = jnp.where(mine, k_pair, jnp.zeros_like(k_pair))
            lse_row = lse[pl.ds(2 * pair + head, 1), :]
            delta_row = delta[pl.ds(2 * pair + head, 1), :]
            scores = mm_nt(k_pair, q_head[head]) + bias[place, :].astype(F32)
            weights = jnp.exp(scores - lse_row)
            probs_g = mm_nt(v_pair, g_head[head])
            one_dv = mm(weights.astype(BF16), g_head[head])
            scores_g = (weights * (probs_g - delta_row)).astype(BF16)
            one_dk = mm(scores_g, q_head[head])
            dq_acc[...] += mm_tn(scores_g, k_head)
            dk = one_dk if dk is None else dk + one_dk
            dv = one_dv if dv is None else dv + one_dv
        cos = cosine[place, :]
        sin = sine[place, :]
        dk_out[place, :] = (dk * cos - half_swap(dk) * sin).astype(BF16)
        dv_out[place, :] = dv.astype(BF16)
        return carry

    lax.fori_loop(0, length // block, one_block, 0)
    dq = dq_acc[...] * (HEAD_DIM**-0.5)
    dq_out[...] = (dq * cosine[...] - half_swap(dq) * sine[...]).astype(BF16)


def project_back_kernel(
    x, normed, dq, dk, dv, resg, wq, wk, wv, small_t, small_g, tok_out, grad_out, acc, first_acc
):
    step = pl.program_id(0)
    block, width = x.shape

    @pl.when(step == 0)
    def _():
        acc[...] = jnp.zeros_like(acc)
        first_acc[...] = jnp.zeros_like(first_acc)

    rows = x[...].astype(F32)
    scale = lax.rsqrt(jnp.mean(rows * rows, axis=1, keepdims=True) + EPS)
    normed_g = mm_nt(dq[...], wq[...]) + mm_nt(dk[...], wk[...]) + mm_nt(dv[...], wv[...])
    n_low = normed[...]
    for index, part in enumerate((dq, dk, dv)):
        acc[:, index * width : (index + 1) * width] += mm_tn(n_low, part[...])
    first_acc[...] += jnp.sum(
        (normed_g * rows * scale).reshape(block // 8, 8, width), axis=0
    )
    scaled = normed_g * small_t[16:17, :]
    tok_out[...] = resg[...] + scale * scaled - rows * (scale * scale * scale) * jnp.mean(
        scaled * rows, axis=1, keepdims=True
    )

    @pl.when(step == pl.num_programs(0) - 1)
    def _():
        grad_out[:, 0 : 3 * width] = acc[...].astype(BF16)
        first = jnp.sum(first_acc[...], axis=0, keepdims=True)
        row = iota((LANES, width), 0)
        extra = small_g[...] + jnp.where(row == 16, first, 0.0).T
        grad_out[:, 3 * width : 3 * width + LANES] = extra.astype(BF16)


def rotary_tables():
    half = HEAD_DIM // 2
    frequency = np.float32(10000.0) ** (
        -np.arange(half, dtype=np.float32) * np.float32(2.0) / np.float32(HEAD_DIM)
    )
    angles = np.arange(LEN, dtype=np.float32)[:, None] * frequency[None, :].astype(np.float32)
    cos = np.cos(angles.astype(np.float64)).astype(np.float32)
    sin = np.sin(angles.astype(np.float64)).astype(np.float32)
    return np.tile(cos, (1, 4)), np.tile(np.concatenate([-sin, sin], axis=1), (1, 2))


def body(
    tokens, previous_logits, routes, prefix, slot_order, first_gain, query_weight, key_weight,
    value_weight, output_weight, second_gain, router_weight, constant_mix, constant_vectors,
    gate_weight, up_weight, down_weight, cotangent,
):
    owners = lax.axis_size("expert")
    shards = lax.axis_size("shard")
    local_experts, shard_rows, ff = gate_weight.shape
    experts = local_experts * owners
    count, width = tokens.shape
    kinds = experts + ZC
    capacity = count * TOP // kinds // 8 * 8
    stride = -(-capacity // 16) * 16
    tiles = ff // TILE
    down_rows = down_weight.shape[1]
    me = lax.axis_index("expert").astype(jnp.int32).reshape(1)
    packed_width = 3 * width + LANES
    cosine, sine = (jnp.asarray(t) for t in rotary_tables())
    struct = jax.ShapeDtypeStruct

    packed = call(
        pack_kernel, "pack", (1,),
        [whole((shard_rows, width))] * 3
        + [whole((1, shard_rows))] * 2
        + [whole((shard_rows, kinds)), whole((shard_rows, 4)), whole((2, shard_rows))],
        whole((shard_rows, packed_width)),
        struct((shard_rows, packed_width), BF16),
        scratch=[pltpu.VMEM((8, LANES), F32)],
        traffic=1 << 20,
    )(
        query_weight, key_weight, value_weight, first_gain[None], second_gain[None],
        router_weight, constant_mix, constant_vectors,
    )
    qkv_full = lax.all_gather(packed, "shard", axis=0, tiled=True)
    output_full = lax.all_gather(output_weight, "shard", axis=0, tiled=True)
    aligned = shard_rows % 16 == 0 and down_rows == TILE
    expert_rows = 2 * tiles * shard_rows + width // TILE * down_rows

    def gather_expert(l):
        if aligned:
            one = call(
                pack_expert_kernel, "pack_expert", (1,),
                [pl.BlockSpec((1,) + w.shape[1:], lambda i: (l, 0, 0))
                 for w in (gate_weight, up_weight, down_weight)],
                whole((expert_rows, TILE)), struct((expert_rows, TILE), BF16), traffic=5 << 20,
            )(gate_weight, up_weight, down_weight)
        else:
            one = jnp.concatenate([
                w[l].reshape(w.shape[1], -1, TILE).transpose(1, 0, 2).reshape(-1, TILE)
                for w in (gate_weight, up_weight, down_weight)
            ])
        full = lax.all_gather(one, "shard", axis=0, tiled=True)
        full = full.reshape(shards, expert_rows, TILE)
        if aligned:
            return full, full
        split = 2 * tiles * shard_rows
        gate_up = full[:, :split].reshape(shards, 2 * tiles, shard_rows, TILE)
        down = full[:, split:].reshape(shards, width // TILE, down_rows, TILE)
        down = down.transpose(1, 0, 2, 3).reshape(width // TILE, tiles, TILE, TILE)
        return (
            gate_up.transpose(1, 0, 2, 3).reshape(1, -1, TILE),
            down.transpose(1, 0, 2, 3).reshape(tiles, width, TILE),
        )

    expert_full = [gather_expert(l) for l in range(local_experts)]

    dest_col, dest_row = call(
        functools.partial(slots_kernel, experts, capacity, stride), "slots", (1,),
        [whole((count, TOP)), whole((1, count)), whole((count, 1))],
        [whole((count, LANES)), whole((8, count))],
        [struct((count, LANES), jnp.int32), struct((8, count), jnp.int32)],
        flops=2 * 3 * count * count * LANES, traffic=1 << 20,
    )(routes, slot_order, slot_order.reshape(count, 1))

    steps = count // BLOCK
    weight_block = [
        pl.BlockSpec((width, width), lambda i, *rest, j=j: (0, j)) for j in range(3)
    ]
    small_block = pl.BlockSpec((width, LANES), lambda i, *rest: (0, 3 * width // LANES))
    wide = rows_of(BLOCK, width)
    table = rows_of(BLOCK, LANES)
    act = struct((count, width), BF16)
    queries, keys, values, normed_one, small_t = call(
        project_kernel, "project", (steps,),
        [wide] + weight_block + [small_block, table, table],
        [wide] * 4 + [whole((LANES, width))],
        [act] * 4 + [struct((LANES, width), F32)],
        flops=6 * count * width * width, traffic=12 << 20,
    )(tokens, qkv_full, qkv_full, qkv_full, qkv_full, cosine, sine)

    attn_mix, lse, residual, normed_two, tok = call(
        attend_kernel, "attend", (steps,),
        [wide, whole((count, width)), whole((count, width)), wide, whole((width, width)),
         small_block, whole((LANES, width)), rows_of(BLOCK, kinds), rows_of(BLOCK, TOP)],
        [wide, pl.BlockSpec((16, BLOCK), lambda i, *rest: (0, i)), wide, wide, table],
        [act, struct((16, count), F32), struct((count, width), F32), act,
         struct((count, LANES), F32)],
        scratch=[pltpu.VMEM((BLOCK, count), F32), pltpu.VMEM((BLOCK, width), BF16),
                 pltpu.VMEM((BLOCK, LANES), F32)],
        flops=30 << 30, traffic=16 << 20, trans=HEADS * count * count, prefetch=1,
    )(prefix, queries, keys, values, tokens, output_full, qkv_full, small_t,
      previous_logits, routes)

    def exchange(parts):
        return [parts[0]] + [
            lax.ppermute(part, "expert", [(i, i ^ k) for i in range(owners)])
            for k, part in list(enumerate(parts))[1:]
        ]

    pair = whole((2, stride, width))
    pair_shape = struct((2, stride, width), BF16)

    def dispatch(l):
        parts = call(
            functools.partial(dispatch_kernel, local_experts, l), "dispatch", (owners,),
            [whole((count, width)), whole((count, width)), whole((count, LANES)),
             whole((count, TOP)), whole((8, count))],
            [pair] * owners, [pair_shape] * owners,
            scratch=[pltpu.VMEM((count, LANES), BF16)],
            flops=4 * owners * stride * count * width, traffic=6 << 20, prefetch=1,
        )(me, normed_two, cotangent, tok, routes, dest_row)
        return exchange(parts)

    received = [dispatch(l) for l in range(local_experts)]

    chunks, chunk_rows = (shards, shard_rows) if aligned else (1, width)
    local = owners * stride

    def run_expert(l):
        gate_up, down = expert_full[l]
        weights = [
            pl.BlockSpec((chunks, chunk_rows, TILE), lambda f, j=j: (0, j // 2 * tiles + 2 * f + j % 2, 0))
            for j in range(4)
        ] + [
            pl.BlockSpec((1, width, TILE), lambda f, j=j: (2 * f + j, 2 if aligned else 0, 0))
            for j in range(2)
        ]
        if aligned:
            grad_shapes = [(shards, expert_rows, TILE)]
        else:
            grad_shapes = [(1, 2 * tiles * width, TILE), (tiles, width, TILE)]
        outs = call(
            functools.partial(expert_kernel, owners, aligned), "expert", (tiles // 2,),
            [pair] * owners + weights,
            [pair] * owners + [whole(g) for g in grad_shapes],
            [pair_shape] * owners + [struct(g, BF16) for g in grad_shapes],
            scratch=[pltpu.VMEM((local, width), BF16)] * 2 + [pltpu.VMEM((local, width), F32)] * 2,
            flops=16 * local * width * ff, traffic=24 << 20, trans=local * ff,
        )(*received[l], gate_up, gate_up, gate_up, gate_up, down, down)
        grads = outs[owners:]
        if aligned:
            grad = grads[0]
        else:
            gate_up_g = grads[0].reshape(2 * tiles, shards, shard_rows, TILE).transpose(1, 0, 2, 3)
            down_g = grads[1].reshape(tiles, width // TILE, TILE, TILE).transpose(1, 0, 2, 3)
            down_g = down_g.reshape(width // TILE, shards, down_rows, TILE).transpose(1, 0, 2, 3)
            grad = jnp.concatenate(
                [gate_up_g.reshape(shards, -1, TILE), down_g.reshape(shards, -1, TILE)], axis=1
            )
        total = lax.psum_scatter(
            grad.reshape(shards * expert_rows, TILE), "shard", scatter_dimension=0, tiled=True
        )
        return exchange(outs[:owners]), total

    returned = []
    expert_sums = []
    for l in range(local_experts):
        back, total = run_expert(l)
        returned += back
        expert_sums.append(total)

    mixed, previous_grad, residual_grad, heads_grad, delta, output_grad, small_grad = call(
        functools.partial(combine_kernel, experts, owners, local_experts), "combine", (steps,),
        [pair] * len(returned)
        + [wide, wide, wide, table, rows_of(BLOCK, TOP), table, wide, whole((width, width)),
           whole((LANES, width))],
        [wide, rows_of(BLOCK, kinds), wide, wide, pl.BlockSpec((16, BLOCK), lambda i, *rest: (0, i)),
         whole((width, width)), whole((width, LANES))],
        [act, struct((count, kinds), F32), struct((count, width), F32), act,
         struct((16, count), F32), struct((width, width), BF16), struct((width, LANES), F32)],
        scratch=[pltpu.VMEM((width, width), F32), pltpu.VMEM((width, LANES), F32),
                 pltpu.VMEM((8, width), F32)]
        + [pltpu.VMEM((local_experts, local, width), BF16)] * 2,
        flops=6 * count * 2 * local * width + 4 * count * width * width, traffic=24 << 20, prefetch=1,
    )(me, *returned, residual, normed_two, cotangent, tok,
      routes, dest_col, attn_mix, output_full, small_t)

    pair_block = pl.BlockSpec((count, LANES), lambda i, *rest: (0, i))
    dq, dk, dv = call(
        attend_back_kernel, "attend_back", (width // LANES,),
        [pair_block] * 4
        + [whole((16, count))] * 2
        + [whole((count, LANES))] * 2,
        [pair_block] * 3,
        [act] * 3,
        scratch=[pltpu.VMEM((count, count), BF16), pltpu.VMEM((count, LANES), F32)],
        flops=60 << 30, traffic=12 << 20, trans=HEADS * count * count, prefetch=1,
    )(prefix, queries, keys, values, heads_grad, lse, delta, cosine, sine)

    tokens_grad, dense_grad = call(
        project_back_kernel, "project_back", (steps,),
        [wide] * 6 + weight_block + [whole((LANES, width)), whole((width, LANES))],
        [wide, whole((width, packed_width))],
        [struct((count, width), F32), struct((width, packed_width), BF16)],
        scratch=[pltpu.VMEM((width, 3 * width), F32), pltpu.VMEM((8, width), F32)],
        flops=12 * count * width * width, traffic=24 << 20,
    )(tokens, normed_one, dq, dk, dv, residual_grad, qkv_full, qkv_full, qkv_full, small_t,
      small_grad)
    dense_grad = jnp.concatenate([dense_grad, output_grad], axis=1)
    dense_grad, expert_sums = lax.optimization_barrier((dense_grad, expert_sums))
    dense_sum = lax.psum_scatter(dense_grad, "shard", scatter_dimension=0, tiled=True)
    half = shard_rows // 2
    parts = [dense_sum[:half], dense_sum[half:]]
    moves = [[(i, i ^ k) for i in range(owners)] for k in (1, 2)]
    for turn in range(2):
        other = [lax.ppermute(parts[j], "expert", moves[(turn + j) % 2]) for j in range(2)]
        parts = [(a.astype(F32) + b.astype(F32)).astype(F32 if turn else BF16)
                 for a, b in zip(parts, other)]
    dense = jnp.concatenate(parts, axis=0)
    small = dense[:, 3 * width : 3 * width + LANES]
    if aligned:
        out_shapes = [w.shape for w in (gate_weight, up_weight, down_weight)]
        gate_sum, up_sum, down_sum = call(
            unpack_expert_kernel, "unpack", (1,),
            [whole((expert_rows, TILE))] * local_experts,
            [whole(o) for o in out_shapes], [struct(o, F32) for o in out_shapes],
            traffic=8 << 20,
        )(*expert_sums)
    else:
        split = 2 * tiles * shard_rows
        total = jnp.stack(expert_sums).astype(F32)
        gate_sum, up_sum = (
            part.reshape(local_experts, tiles, shard_rows, TILE).transpose(0, 2, 1, 3).reshape(
                local_experts, shard_rows, ff
            )
            for part in (total[:, : split // 2], total[:, split // 2 : split])
        )
        down_sum = total[:, split:].reshape(local_experts, width // TILE, down_rows, TILE)
        down_sum = down_sum.transpose(0, 2, 1, 3).reshape(local_experts, down_rows, width)
    return (
        mixed,
        tokens_grad,
        previous_grad,
        dense[:, 0:width],
        dense[:, width : 2 * width],
        dense[:, 2 * width : 3 * width],
        dense[:, packed_width:],
        small[:, 0:kinds],
        small[:, kinds : kinds + 4],
        small[:, 18:20].T,
        small[:, 16],
        small[:, 17],
        gate_sum,
        up_sum,
        down_sum,
    )


def solution(mesh):
    rows = P(("expert", "shard"), None)
    expert = P("expert", "shard", None)
    flat = P("shard", None)
    return jax.shard_map(
        body,
        mesh=mesh,
        in_specs=(
            rows, rows, rows, P(("expert", "shard")), rows, P("shard"), flat, flat, flat, flat,
            P("shard"), flat, flat, P(None, "shard"), expert, expert, expert, rows,
        ),
        out_specs=(
            rows, rows, rows, flat, flat, flat, flat, flat, flat, P(None, "shard"), P("shard"),
            P("shard"), expert, expert, expert,
        ),
        check_vma=False,
    )
```

```python
import functools
import numpy as np
import jax
import jax.numpy as jnp
from jax import lax
from jax.experimental import pallas as pl
from jax.experimental.pallas import tpu as pltpu
from jax.sharding import PartitionSpec as P

HEADS = 12
HEAD_DIM = 64
ZC = 4
TOP = 2
LEN = 1024
EPS = 1e-05
NEG = -1e30
LANES = 128
BLOCK = 256
TILE = 256
F32 = jnp.float32
BF16 = jnp.bfloat16
VMEM_LIMIT = 56 << 20


def call(body, name, grid, in_specs, out_specs, out_shape, scratch=(), flops=0, traffic=0, trans=0, prefetch=0):
    return pl.pallas_call(
        body,
        name=name,
        grid_spec=pltpu.PrefetchScalarGridSpec(
            num_scalar_prefetch=prefetch,
            grid=grid,
            in_specs=in_specs,
            out_specs=out_specs,
            scratch_shapes=scratch,
        ),
        out_shape=out_shape,
        compiler_params=pltpu.CompilerParams(
            dimension_semantics=("arbitrary",) * len(grid), vmem_limit_bytes=VMEM_LIMIT
        ),
        cost_estimate=pl.CostEstimate(flops=flops, transcendentals=trans, bytes_accessed=traffic),
    )


def mm(a, b):
    return lax.dot_general(a, b, (((1,), (0,)), ((), ())), preferred_element_type=F32)


def mm_nt(a, b):
    return lax.dot_general(a, b, (((1,), (1,)), ((), ())), preferred_element_type=F32)


def mm_tn(a, b):
    return lax.dot_general(a, b, (((0,), (0,)), ((), ())), preferred_element_type=F32)


def iota(shape, axis):
    return lax.broadcasted_iota(jnp.int32, shape, axis)


def whole(shape):
    return pl.BlockSpec(shape, lambda *idx: (0,) * len(shape))


def rows_of(block, width):
    return pl.BlockSpec((block, width), lambda i, *rest: (i, 0))


def split_high_low(values):
    high = values.astype(BF16)
    low = (values - high.astype(F32)).astype(BF16)
    return high, low


def pack_kernel(q, k, v, gain1, gain2, router, mix, vectors, out, scratch):
    rows, width = q.shape
    out[:, 0:width] = q[...]
    out[:, width : 2 * width] = k[...]
    out[:, 2 * width : 3 * width] = v[...]
    base = 3 * width
    out[:, base : base + LANES] = jnp.zeros((rows, LANES), BF16)
    scratch[...] = jnp.zeros_like(scratch)
    scratch[0:1, 0:rows] = gain1[...].astype(F32)
    scratch[1:2, 0:rows] = gain2[...].astype(F32)
    scratch[2:4, 0:rows] = vectors[...].astype(F32)
    columns = scratch[...].T
    n_router = router.shape[1]
    n_mix = mix.shape[1]
    out[:, base : base + n_router] = router[...]
    out[:, base + n_router : base + n_router + n_mix] = mix[...]
    out[:, base + 16 : base + 24] = columns[0:rows, 0:8].astype(BF16)


def slots_kernel(experts, capacity, stride, routes, order_row, order_col, dest_col, dest_row):
    tokens = routes.shape[0]
    r0 = routes[:, 0:1]
    r1 = routes[:, 1:2]
    lane = iota((tokens, LANES), 1)
    hot = jnp.where((lane == r0) | (lane == r1), 1.0, 0.0)
    hot = jnp.where(lane < experts, hot, 0.0).astype(BF16)
    row = iota((tokens, tokens), 0)
    col = iota((tokens, tokens), 1)
    to_turn = jnp.where(order_col[...] == col, 1.0, 0.0).astype(BF16)
    hot_turn = mm(to_turn, hot).astype(BF16)
    earlier = mm(jnp.where(col < row, 1.0, 0.0).astype(BF16), hot_turn)
    earlier = jnp.minimum(earlier, 255.0).astype(BF16)
    to_token = jnp.where(order_row[...] == row, 1.0, 0.0).astype(BF16)
    position = mm(to_token, earlier)
    p0 = jnp.sum(jnp.where(lane == r0, position, 0.0), axis=1, keepdims=True)
    p1 = jnp.sum(jnp.where(lane == r1, position, 0.0), axis=1, keepdims=True)
    d0 = jnp.where((r0 < experts) & (p0 < capacity), r0.astype(F32) * stride + p0, -1.0)
    d1 = jnp.where((r1 < experts) & (p1 < capacity), r1.astype(F32) * stride + p1, -1.0)
    both = jnp.where(lane == 0, d0, jnp.where(lane == 1, d1, 0.0))
    dest_col[...] = both.astype(jnp.int32)
    dest_row[...] = both.T[0:8, :].astype(jnp.int32)


def half_swap(values):
    lane = iota(values.shape, 1) % HEAD_DIM
    half = HEAD_DIM // 2
    return jnp.where(
        lane < half, pltpu.roll(values, LANES - half, 1), pltpu.roll(values, half, 1)
    )


def project_kernel(x, wq, wk, wv, small, cosine, sine, q_out, k_out, v_out, n_out, small_t):
    @pl.when(pl.program_id(0) == 0)
    def _():
        small_t[...] = small[...].astype(F32).T

    width = x.shape[1]
    rows = x[...].astype(F32)
    scale = lax.rsqrt(jnp.mean(rows * rows, axis=1, keepdims=True) + EPS)
    normed = (rows * scale * small_t[16:17, :]).astype(BF16)
    n_out[...] = normed
    cos = cosine[...]
    sin = sine[...]
    for weight, out, factor in ((wq, q_out, HEAD_DIM**-0.5), (wk, k_out, None)):
        lin = mm(normed, weight[...])
        for c in range(width // LANES):
            part = lin[:, c * LANES : (c + 1) * LANES]
            turned = part * cos + half_swap(part) * sin
            if factor is not None:
                turned = turned * factor
            out[:, c * LANES : (c + 1) * LANES] = turned.astype(BF16)
    v_out[...] = mm(normed, wv[...]).astype(BF16)


def attend_kernel(
    prefix, q, k, v, x, wo, small, small_t, prev, routes,
    mix_out, lse_out, res_out, n_out, tok_out, bias, mixed, lse,
):
    block, width = q.shape
    length = k.shape[0]
    start = pl.program_id(0) * block
    limit = jnp.maximum(start + iota((block, 1), 0) + 1, prefix[0])
    bias[...] = jnp.where(iota((block, length), 1) < limit, 0.0, NEG)
    lane = iota((block, LANES), 1)
    first = lane < HEAD_DIM
    lse[...] = jnp.zeros_like(lse)

    def one_pair(pair, carry):
        columns = pl.ds(pl.multiple_of(pair * LANES, LANES), LANES)
        q_pair = q[:, columns]
        k_pair = k[:, columns]
        v_pair = v[:, columns]
        outs = []
        for head in range(2):
            mine = first if head == 0 else jnp.logical_not(first)
            q_head = jnp.where(mine, q_pair, jnp.zeros_like(q_pair))
            scores = mm_nt(q_head, k_pair) + bias[...]
            top = jnp.max(scores, axis=1, keepdims=True)
            weights = jnp.exp(scores - top)
            total = jnp.sum(weights, axis=1, keepdims=True)
            outs.append(mm(weights.astype(BF16), v_pair) / total)
            lse[...] = jnp.where(lane == 2 * pair + head, top + jnp.log(total), lse[...])
        mixed[:, columns] = jnp.where(first, outs[0], outs[1]).astype(BF16)
        return carry

    lax.fori_loop(0, width // LANES, one_pair, 0)
    mix_out[...] = mixed[...]
    lse_out[...] = lse[...].T[0:16, :]
    residual = x[...].astype(F32) + mm(mixed[...], wo[...])
    res_out[...] = residual
    scale = lax.rsqrt(jnp.mean(residual * residual, axis=1, keepdims=True) + EPS)
    normed = (residual * scale * small_t[17:18, :]).astype(BF16)
    n_out[...] = normed
    lin = mm(normed, small[...])
    kinds = prev.shape[1]
    logits = lin[:, 0:kinds] + prev[...]
    kind = iota((block, kinds), 1)
    c0 = jnp.sum(jnp.where(kind == routes[:, 0:1], logits, 0.0), axis=1, keepdims=True)
    c1 = jnp.sum(jnp.where(kind == routes[:, 1:2], logits, 0.0), axis=1, keepdims=True)

    def pair_softmax(a, b):
        top = jnp.maximum(a, b)
        ea = jnp.exp(a - top)
        eb = jnp.exp(b - top)
        total = ea + eb
        return ea / total, eb / total

    g0, g1 = pair_softmax(c0, c1)
    m00, m01 = pair_softmax(lin[:, kinds : kinds + 1], lin[:, kinds + 1 : kinds + 2])
    m10, m11 = pair_softmax(lin[:, kinds + 2 : kinds + 3], lin[:, kinds + 3 : kinds + 4])
    packed = jnp.zeros((block, LANES), F32)
    for index, column in enumerate((g0, g1, m00, m01, m10, m11, scale)):
        packed = jnp.where(lane == index, column, packed)
    tok_out[...] = packed


def pack_expert_kernel(gate, up, down, out):
    rows, ff = gate.shape[1:]
    down_rows, width = down.shape[1:]
    tiles = ff // TILE
    for index, ref in enumerate((gate, up)):
        for f in range(tiles):
            start = (index * tiles + f) * rows
            out[start : start + rows, :] = ref[0, :, f * TILE : (f + 1) * TILE]
    base = 2 * tiles * rows
    for c in range(width // TILE):
        out[base + c * down_rows : base + (c + 1) * down_rows, :] = down[
            0, :, c * TILE : (c + 1) * TILE
        ]


def unpack_expert_kernel(*refs):
    gate, up, down = refs[-3:]
    rows, ff = gate.shape[1:]
    down_rows, width = down.shape[1:]
    tiles = ff // TILE
    base = 2 * tiles * rows
    for l, ref in enumerate(refs[:-3]):
        for index, out in enumerate((gate, up)):
            for f in range(tiles):
                start = (index * tiles + f) * rows
                out[l, :, f * TILE : (f + 1) * TILE] = ref[start : start + rows, :].astype(F32)
        for c in range(width // TILE):
            down[l, :, c * TILE : (c + 1) * TILE] = ref[
                base + c * down_rows : base + (c + 1) * down_rows, :
            ].astype(F32)


def dispatch_kernel(local_experts, l, me, normed, grad, tok, routes, dest_row, *rest):
    outs, gates = rest[:-1], rest[-1]
    step = pl.program_id(0)
    tokens = normed.shape[0]
    stride = outs[0].shape[1]
    expert = (me[0] ^ step) * local_experts + l

    @pl.when(step == 0)
    def _():
        lane = iota((tokens, LANES), 1)
        kind = lane % HEAD_DIM
        value = jnp.where(kind == routes[:, 0:1], tok[:, 0:1], 0.0)
        value = value + jnp.where(kind == routes[:, 1:2], tok[:, 1:2], 0.0)
        high = value.astype(BF16).astype(F32)
        gates[...] = jnp.where(lane < HEAD_DIM, high, value - high).astype(BF16)

    slot = expert * stride + iota((stride, tokens), 0)
    hit = (dest_row[0:1, :] == slot) | (dest_row[1:2, :] == slot)
    take = jnp.where(hit, 1.0, 0.0).astype(BF16)
    row = mm(take, normed[...]).astype(BF16)
    slot_gates = mm(take, gates[...])
    mine = iota((stride, LANES), 1) % HEAD_DIM == expert
    slot_gate = jnp.sum(jnp.where(mine, slot_gates, 0.0), axis=1, keepdims=True)
    slot_g = (mm(take, grad[...]) * slot_gate).astype(BF16)
    for k, out in enumerate(outs):

        @pl.when(step == k)
        def _():
            out[0] = row
            out[1] = slot_g


def expert_kernel(owners, merged, *refs):
    sent = refs[:owners]
    weights = refs[owners : owners + 6]
    backs = refs[owners + 6 : 2 * owners + 6]
    grads = refs[2 * owners + 6 : -4]
    r_all, s_all, out_acc, row_acc = refs[-4:]
    step = pl.program_id(0)
    steps = pl.num_programs(0)
    stride, width = sent[0].shape[1:]
    chunks, chunk_rows = weights[0].shape[:2]

    @pl.when(step == 0)
    def _():
        for k, ref in enumerate(sent):
            r_all[k * stride : (k + 1) * stride, :] = ref[0]
            s_all[k * stride : (k + 1) * stride, :] = ref[1]
        out_acc[...] = jnp.zeros_like(out_acc)
        row_acc[...] = jnp.zeros_like(row_acc)

    def tile_pair(a, b):
        return jnp.concatenate([t[...].reshape(width, TILE) for t in (a, b)], axis=1)

    def down_tile(ref):
        parts = [ref[0, c * TILE : (c + 1) * TILE, :] for c in range(width // TILE)]
        return jnp.concatenate(parts, axis=1)

    r = r_all[...]
    s = s_all[...]
    gate = tile_pair(weights[0], weights[1])
    up = tile_pair(weights[2], weights[3])
    d = jnp.concatenate([down_tile(weights[4]), down_tile(weights[5])], axis=0)
    gate_pre = mm(r, gate)
    up_pre = mm(r, up)
    sig = jax.nn.sigmoid(gate_pre)
    silu = gate_pre * sig
    hid = (silu * up_pre).astype(BF16)
    hidden_g = mm_nt(s, d)
    out_acc[...] += mm(hid, d)
    gate_g = (hidden_g * (up_pre * (sig + silu * (1.0 - sig)))).astype(BF16)
    up_g = (hidden_g * silu).astype(BF16)
    row_acc[...] += mm_nt(gate_g, gate) + mm_nt(up_g, up)
    down_grad = mm_tn(hid, s).astype(BF16)
    gate_grad = mm_tn(r, gate_g).astype(BF16)
    up_grad = mm_tn(r, up_g).astype(BF16)
    base = 4 * steps * chunk_rows if merged else 0
    for i in range(2):
        tile = 2 * step + i
        for index, value in enumerate((gate_grad, up_grad)):
            start = pl.multiple_of((index * 2 * steps + tile) * chunk_rows, 16)
            grads[0][:, pl.ds(start, chunk_rows), :] = value[:, i * TILE : (i + 1) * TILE].reshape(
                chunks, chunk_rows, TILE
            )
        for c in range(width // TILE):
            grads[-1][tile, base + c * TILE : base + (c + 1) * TILE, :] = down_grad[
                i * TILE : (i + 1) * TILE, c * TILE : (c + 1) * TILE
            ]

    @pl.when(step == steps - 1)
    def _():
        for k, ref in enumerate(backs):
            ref[0] = out_acc[k * stride : (k + 1) * stride, :].astype(BF16)
            ref[1] = row_acc[k * stride : (k + 1) * stride, :].astype(BF16)


def combine_kernel(experts, owners, local_experts, me, *refs):
    backs = refs[: owners * local_experts]
    (
        residual, normed, grad, tok, routes, dest, mix, wo, small_t,
        mixed_out, prev_out, resg_out, headg_out, delta_out, wo_out, small_out,
        wo_acc, small_acc, second_acc, eo_all, rg_all,
    ) = refs[owners * local_experts :]
    step = pl.program_id(0)
    block, width = residual.shape
    stride = backs[0].shape[1]
    local = owners * stride

    @pl.when(step == 0)
    def _():
        wo_acc[...] = jnp.zeros_like(wo_acc)
        small_acc[...] = jnp.zeros_like(small_acc)
        second_acc[...] = jnp.zeros_like(second_acc)
        for l in range(local_experts):
            for k in range(owners):
                place = slice(k * stride, (k + 1) * stride)
                eo_all[l, place, :] = backs[l * owners + k][0]
                rg_all[l, place, :] = backs[l * owners + k][1]

    slot = iota((1, local), 1)
    owner_slot = ((slot // stride) ^ me[0]) * (local_experts * stride) + slot % stride

    ep = [None, None]
    back = None
    for l in range(local_experts):
        ident = owner_slot + l * stride
        t0 = jnp.where(dest[:, 0:1] == ident, 1.0, 0.0)
        t1 = jnp.where(dest[:, 1:2] == ident, 1.0, 0.0)
        eo = eo_all[l]
        rg = rg_all[l]
        e0 = mm(t0.astype(BF16), eo)
        e1 = mm(t1.astype(BF16), eo)
        b = mm((t0 + t1).astype(BF16), rg)
        ep[0] = e0 if ep[0] is None else ep[0] + e0
        ep[1] = e1 if ep[1] is None else ep[1] + e1
        back = b if back is None else back + b

    res = residual[...]
    n_low = normed[...]
    nf = n_low.astype(F32)
    g_low = grad[...]
    g = g_low.astype(F32)
    gate = [tok[:, 0:1], tok[:, 1:2]]
    mw = [[tok[:, 2:3], tok[:, 3:4]], [tok[:, 4:5], tok[:, 5:6]]]
    scale = tok[:, 6:7]
    vec = [small_t[18:19, :], small_t[19:20, :]]
    along_n = jnp.sum(g * nf, axis=1, keepdims=True)
    along_vec = [jnp.sum(g * vec[c], axis=1, keepdims=True) for c in range(2)]
    gate_g = []
    on_n = 0.0
    sel = [0.0, 0.0]
    copy_weight = 0.0
    for t in range(TOP):
        route = routes[:, t : t + 1]
        is_copy = jnp.where(route == experts + 1, 1.0, 0.0)
        is_const = [jnp.where(route == experts + 2 + c, 1.0, 0.0) for c in range(2)]
        a = is_copy + is_const[0] * mw[0][0] + is_const[1] * mw[1][0]
        b = [is_const[c] * mw[c][1] for c in range(2)]
        gate_g.append(
            jnp.sum(g * ep[t], axis=1, keepdims=True)
            + a * along_n
            + b[0] * along_vec[0]
            + b[1] * along_vec[1]
        )
        on_n = on_n + gate[t] * a
        copy_weight = copy_weight + gate[t] * is_copy
        sel = [sel[c] + gate[t] * is_const[c] for c in range(2)]
    vec_w = [sel[c] * mw[c][1] for c in range(2)]
    mixed_out[...] = (
        res + gate[0] * ep[0] + gate[1] * ep[1] + on_n * nf + vec_w[0] * vec[0] + vec_w[1] * vec[1]
    ).astype(BF16)

    centre = gate[0] * gate_g[0] + gate[1] * gate_g[1]
    pair_g = [gate[t] * (gate_g[t] - centre) for t in range(TOP)]
    lane = iota((block, LANES), 1)
    logit_g = jnp.where(lane == routes[:, 0:1], pair_g[0], 0.0)
    logit_g = logit_g + jnp.where(lane == routes[:, 1:2], pair_g[1], 0.0)
    kinds = prev_out.shape[1]
    prev_out[...] = logit_g[:, 0:kinds]
    for c in range(2):
        w0 = sel[c] * along_n
        w1 = sel[c] * along_vec[c]
        mid = mw[c][0] * w0 + mw[c][1] * w1
        logit_g = jnp.where(lane == kinds + 2 * c, mw[c][0] * (w0 - mid), logit_g)
        logit_g = jnp.where(lane == kinds + 2 * c + 1, mw[c][1] * (w1 - mid), logit_g)
    high, low = split_high_low(logit_g)
    table = small_t[...]
    table = jnp.where(iota(table.shape, 0) < 16, table, 0.0).astype(BF16)
    direct = copy_weight + sel[0] * mw[0][0] + sel[1] * mw[1][0]
    normed_g = back + direct * g + mm(high, table) + mm(low, table)
    gain = small_t[17:18, :]
    scaled = normed_g * gain
    second_acc[...] += jnp.sum(
        (normed_g * res * scale).reshape(block // 8, 8, width), axis=0
    )
    resg = g + scale * scaled - res * (scale * scale * scale) * jnp.mean(
        scaled * res, axis=1, keepdims=True
    )
    resg_out[...] = resg
    attn_g = resg.astype(BF16)
    am = mix[...]
    wo_acc[...] += mm_tn(am, attn_g)
    heads_g = mm_nt(attn_g, wo[...]).astype(BF16)
    headg_out[...] = heads_g
    product = heads_g.astype(F32) * am.astype(F32)
    p_high, p_low = split_high_low(product)
    head_of = jnp.where(
        iota((16, width), 1) // HEAD_DIM == iota((16, width), 0), 1.0, 0.0
    ).astype(BF16)
    delta_out[...] = mm_nt(head_of, p_high) + mm_nt(head_of, p_low)
    small_acc[...] += mm_tn(n_low, high) + mm_tn(n_low, low)
    coefficient = jnp.where(lane == 18, vec_w[0], jnp.where(lane == 19, vec_w[1], 0.0))
    c_high, c_low = split_high_low(coefficient)
    small_acc[...] += mm_tn(g_low, c_high) + mm_tn(g_low, c_low)

    @pl.when(step == pl.num_programs(0) - 1)
    def _():
        wo_out[...] = wo_acc[...].astype(BF16)
        second = jnp.sum(second_acc[...], axis=0, keepdims=True)
        row = iota((LANES, width), 0)
        small_out[...] = small_acc[...] + jnp.where(row == 17, second, 0.0).T


def attend_back_kernel(
    prefix, q, k, v, grad, lse, delta, cosine, sine, dq_out, dk_out, dv_out, bias, dq_acc
):
    length = q.shape[0]
    pair = pl.program_id(0)
    block = BLOCK
    lane_all = iota((length, LANES), 1)
    lane = iota((block, LANES), 1)

    @pl.when(pair == 0)
    def _():
        limit = jnp.maximum(iota((1, length), 1) + 1, prefix[0])
        bias[...] = jnp.where(iota((length, length), 0) < limit, 0.0, NEG).astype(BF16)

    q_pair = q[...]
    g_pair = grad[...]
    zero = jnp.zeros_like(q_pair)
    q_head = []
    g_head = []
    for head in range(2):
        mine = (lane_all // HEAD_DIM) == head
        q_head.append(jnp.where(mine, q_pair, zero))
        g_head.append(jnp.where(mine, g_pair, zero))
    dq_acc[...] = jnp.zeros_like(dq_acc)

    def one_block(index, carry):
        place = pl.ds(pl.multiple_of(index * block, block), block)
        k_pair = k[place, :]
        v_pair = v[place, :]
        dk = None
        dv = None
        for head in range(2):
            mine = (lane // HEAD_DIM) == head
            k_head = jnp.where(mine, k_pair, jnp.zeros_like(k_pair))
            lse_row = lse[pl.ds(2 * pair + head, 1), :]
            delta_row = delta[pl.ds(2 * pair + head, 1), :]
            scores = mm_nt(k_pair, q_head[head]) + bias[place, :].astype(F32)
            weights = jnp.exp(scores - lse_row)
            probs_g = mm_nt(v_pair, g_head[head])
            one_dv = mm(weights.astype(BF16), g_head[head])
            scores_g = (weights * (probs_g - delta_row)).astype(BF16)
            one_dk = mm(scores_g, q_head[head])
            dq_acc[...] += mm_tn(scores_g, k_head)
            dk = one_dk if dk is None else dk + one_dk
            dv = one_dv if dv is None else dv + one_dv
        cos = cosine[place, :]
        sin = sine[place, :]
        dk_out[place, :] = (dk * cos - half_swap(dk) * sin).astype(BF16)
        dv_out[place, :] = dv.astype(BF16)
        return carry

    lax.fori_loop(0, length // block, one_block, 0)
    dq = dq_acc[...] * (HEAD_DIM**-0.5)
    dq_out[...] = (dq * cosine[...] - half_swap(dq) * sine[...]).astype(BF16)


def project_back_kernel(
    me, x, normed, dq, dk, dv, resg, wq, wk, wv, small_t, small_g, output_g,
    tok_out, grad_out, acc, first_acc,
):
    step = pl.program_id(0)
    block, width = x.shape

    @pl.when(step == 0)
    def _():
        acc[...] = jnp.zeros_like(acc)
        first_acc[...] = jnp.zeros_like(first_acc)

    rows = x[...].astype(F32)
    scale = lax.rsqrt(jnp.mean(rows * rows, axis=1, keepdims=True) + EPS)
    normed_g = mm_nt(dq[...], wq[...]) + mm_nt(dk[...], wk[...]) + mm_nt(dv[...], wv[...])
    n_low = normed[...]
    for index, part in enumerate((dq, dk, dv)):
        acc[:, index * width : (index + 1) * width] += mm_tn(n_low, part[...])
    first_acc[...] += jnp.sum(
        (normed_g * rows * scale).reshape(block // 8, 8, width), axis=0
    )
    scaled = normed_g * small_t[16:17, :]
    tok_out[...] = resg[...] + scale * scaled - rows * (scale * scale * scale) * jnp.mean(
        scaled * rows, axis=1, keepdims=True
    )

    @pl.when(step == pl.num_programs(0) - 1)
    def _():
        for j in range(3):
            grad_out[me[0] ^ j, :, 0:width] = acc[:, j * width : (j + 1) * width].astype(BF16)
            grad_out[me[0] ^ j, :, width : width + LANES] = jnp.zeros((width, LANES), BF16)
        first = jnp.sum(first_acc[...], axis=0, keepdims=True)
        row = iota((LANES, width), 0)
        extra = small_g[...] + jnp.where(row == 16, first, 0.0).T
        grad_out[me[0] ^ 3, :, 0:width] = output_g[...]
        grad_out[me[0] ^ 3, :, width : width + LANES] = extra.astype(BF16)


def rotary_tables():
    half = HEAD_DIM // 2
    frequency = np.float32(10000.0) ** (
        -np.arange(half, dtype=np.float32) * np.float32(2.0) / np.float32(HEAD_DIM)
    )
    angles = np.arange(LEN, dtype=np.float32)[:, None] * frequency[None, :].astype(np.float32)
    cos = np.cos(angles.astype(np.float64)).astype(np.float32)
    sin = np.sin(angles.astype(np.float64)).astype(np.float32)
    return np.tile(cos, (1, 4)), np.tile(np.concatenate([-sin, sin], axis=1), (1, 2))


def body(
    tokens, previous_logits, routes, prefix, slot_order, first_gain, query_weight, key_weight,
    value_weight, output_weight, second_gain, router_weight, constant_mix, constant_vectors,
    gate_weight, up_weight, down_weight, cotangent,
):
    owners = lax.axis_size("expert")
    shards = lax.axis_size("shard")
    local_experts, shard_rows, ff = gate_weight.shape
    experts = local_experts * owners
    count, width = tokens.shape
    kinds = experts + ZC
    capacity = count * TOP // kinds // 8 * 8
    stride = -(-capacity // 16) * 16
    tiles = ff // TILE
    down_rows = down_weight.shape[1]
    me = lax.axis_index("expert").astype(jnp.int32).reshape(1)
    packed_width = 3 * width + LANES
    cosine, sine = (jnp.asarray(t) for t in rotary_tables())
    struct = jax.ShapeDtypeStruct

    packed = call(
        pack_kernel, "pack", (1,),
        [whole((shard_rows, width))] * 3
        + [whole((1, shard_rows))] * 2
        + [whole((shard_rows, kinds)), whole((shard_rows, 4)), whole((2, shard_rows))],
        whole((shard_rows, packed_width)),
        struct((shard_rows, packed_width), BF16),
        scratch=[pltpu.VMEM((8, LANES), F32)],
        traffic=1 << 20,
    )(
        query_weight, key_weight, value_weight, first_gain[None], second_gain[None],
        router_weight, constant_mix, constant_vectors,
    )
    qkv_full = lax.all_gather(packed, "shard", axis=0, tiled=True)
    output_full = lax.all_gather(output_weight, "shard", axis=0, tiled=True)
    aligned = shard_rows % 16 == 0 and down_rows == TILE
    expert_rows = 2 * tiles * shard_rows + width // TILE * down_rows

    def gather_expert(l):
        if aligned:
            one = call(
                pack_expert_kernel, "pack_expert", (1,),
                [pl.BlockSpec((1,) + w.shape[1:], lambda i: (l, 0, 0))
                 for w in (gate_weight, up_weight, down_weight)],
                whole((expert_rows, TILE)), struct((expert_rows, TILE), BF16), traffic=5 << 20,
            )(gate_weight, up_weight, down_weight)
        else:
            one = jnp.concatenate([
                w[l].reshape(w.shape[1], -1, TILE).transpose(1, 0, 2).reshape(-1, TILE)
                for w in (gate_weight, up_weight, down_weight)
            ])
        full = lax.all_gather(one, "shard", axis=0, tiled=True)
        full = full.reshape(shards, expert_rows, TILE)
        if aligned:
            return full, full
        split = 2 * tiles * shard_rows
        gate_up = full[:, :split].reshape(shards, 2 * tiles, shard_rows, TILE)
        down = full[:, split:].reshape(shards, width // TILE, down_rows, TILE)
        down = down.transpose(1, 0, 2, 3).reshape(width // TILE, tiles, TILE, TILE)
        return (
            gate_up.transpose(1, 0, 2, 3).reshape(1, -1, TILE),
            down.transpose(1, 0, 2, 3).reshape(tiles, width, TILE),
        )

    expert_full = [gather_expert(l) for l in range(local_experts)]

    dest_col, dest_row = call(
        functools.partial(slots_kernel, experts, capacity, stride), "slots", (1,),
        [whole((count, TOP)), whole((1, count)), whole((count, 1))],
        [whole((count, LANES)), whole((8, count))],
        [struct((count, LANES), jnp.int32), struct((8, count), jnp.int32)],
        flops=2 * 3 * count * count * LANES, traffic=1 << 20,
    )(routes, slot_order, slot_order.reshape(count, 1))

    steps = count // BLOCK
    weight_block = [
        pl.BlockSpec((width, width), lambda i, *rest, j=j: (0, j)) for j in range(3)
    ]
    small_block = pl.BlockSpec((width, LANES), lambda i, *rest: (0, 3 * width // LANES))
    wide = rows_of(BLOCK, width)
    table = rows_of(BLOCK, LANES)
    act = struct((count, width), BF16)
    queries, keys, values, normed_one, small_t = call(
        project_kernel, "project", (steps,),
        [wide] + weight_block + [small_block, table, table],
        [wide] * 4 + [whole((LANES, width))],
        [act] * 4 + [struct((LANES, width), F32)],
        flops=6 * count * width * width, traffic=12 << 20,
    )(tokens, qkv_full, qkv_full, qkv_full, qkv_full, cosine, sine)

    attn_mix, lse, residual, normed_two, tok = call(
        attend_kernel, "attend", (steps,),
        [wide, whole((count, width)), whole((count, width)), wide, whole((width, width)),
         small_block, whole((LANES, width)), rows_of(BLOCK, kinds), rows_of(BLOCK, TOP)],
        [wide, pl.BlockSpec((16, BLOCK), lambda i, *rest: (0, i)), wide, wide, table],
        [act, struct((16, count), F32), struct((count, width), F32), act,
         struct((count, LANES), F32)],
        scratch=[pltpu.VMEM((BLOCK, count), F32), pltpu.VMEM((BLOCK, width), BF16),
                 pltpu.VMEM((BLOCK, LANES), F32)],
        flops=30 << 30, traffic=16 << 20, trans=HEADS * count * count, prefetch=1,
    )(prefix, queries, keys, values, tokens, output_full, qkv_full, small_t,
      previous_logits, routes)

    def exchange(parts):
        return [parts[0]] + [
            lax.ppermute(part, "expert", [(i, i ^ k) for i in range(owners)])
            for k, part in list(enumerate(parts))[1:]
        ]

    pair = whole((2, stride, width))
    pair_shape = struct((2, stride, width), BF16)

    def dispatch(l):
        parts = call(
            functools.partial(dispatch_kernel, local_experts, l), "dispatch", (owners,),
            [whole((count, width)), whole((count, width)), whole((count, LANES)),
             whole((count, TOP)), whole((8, count))],
            [pair] * owners, [pair_shape] * owners,
            scratch=[pltpu.VMEM((count, LANES), BF16)],
            flops=4 * owners * stride * count * width, traffic=6 << 20, prefetch=1,
        )(me, normed_two, cotangent, tok, routes, dest_row)
        return parts

    dispatched = [dispatch(l) for l in range(local_experts)]
    received = [exchange(parts) for parts in dispatched]

    chunks, chunk_rows = (shards, shard_rows) if aligned else (1, width)
    local = owners * stride

    def run_expert(l, rows):
        gate_up, down = expert_full[l]
        weights = [
            pl.BlockSpec((chunks, chunk_rows, TILE), lambda f, j=j: (0, j // 2 * tiles + 2 * f + j % 2, 0))
            for j in range(4)
        ] + [
            pl.BlockSpec((1, width, TILE), lambda f, j=j: (2 * f + j, 2 if aligned else 0, 0))
            for j in range(2)
        ]
        if aligned:
            grad_shapes = [(shards, expert_rows, TILE)]
        else:
            grad_shapes = [(1, 2 * tiles * width, TILE), (tiles, width, TILE)]
        outs = call(
            functools.partial(expert_kernel, owners, aligned), "expert", (tiles // 2,),
            [pair] * owners + weights,
            [pair] * owners + [whole(g) for g in grad_shapes],
            [pair_shape] * owners + [struct(g, BF16) for g in grad_shapes],
            scratch=[pltpu.VMEM((local, width), BF16)] * 2 + [pltpu.VMEM((local, width), F32)] * 2,
            flops=16 * local * width * ff, traffic=24 << 20, trans=local * ff,
        )(*rows, gate_up, gate_up, gate_up, gate_up, down, down)
        grads = outs[owners:]
        if aligned:
            grad = grads[0]
        else:
            gate_up_g = grads[0].reshape(2 * tiles, shards, shard_rows, TILE).transpose(1, 0, 2, 3)
            down_g = grads[1].reshape(tiles, width // TILE, TILE, TILE).transpose(1, 0, 2, 3)
            down_g = down_g.reshape(width // TILE, shards, down_rows, TILE).transpose(1, 0, 2, 3)
            grad = jnp.concatenate(
                [gate_up_g.reshape(shards, -1, TILE), down_g.reshape(shards, -1, TILE)], axis=1
            )
        total = lax.psum_scatter(
            grad.reshape(shards * expert_rows, TILE), "shard", scatter_dimension=0, tiled=True
        )
        return exchange(outs[:owners]), total

    returned = []
    expert_sums = []
    for l in range(local_experts):
        rows, ahead = lax.optimization_barrier((received[l], returned or dispatched[-1]))
        returned = ahead if returned else returned
        back, total = run_expert(l, rows)
        returned = returned + back
        expert_sums.append(total)

    mixed, previous_grad, residual_grad, heads_grad, delta, output_grad, small_grad = call(
        functools.partial(combine_kernel, experts, owners, local_experts), "combine", (steps,),
        [pair] * len(returned)
        + [wide, wide, wide, table, rows_of(BLOCK, TOP), table, wide, whole((width, width)),
           whole((LANES, width))],
        [wide, rows_of(BLOCK, kinds), wide, wide, pl.BlockSpec((16, BLOCK), lambda i, *rest: (0, i)),
         whole((width, width)), whole((width, LANES))],
        [act, struct((count, kinds), F32), struct((count, width), F32), act,
         struct((16, count), F32), struct((width, width), BF16), struct((width, LANES), F32)],
        scratch=[pltpu.VMEM((width, width), F32), pltpu.VMEM((width, LANES), F32),
                 pltpu.VMEM((8, width), F32)]
        + [pltpu.VMEM((local_experts, local, width), BF16)] * 2,
        flops=6 * count * 2 * local * width + 4 * count * width * width, traffic=24 << 20, prefetch=1,
    )(me, *returned, residual, normed_two, cotangent, tok,
      routes, dest_col, attn_mix, output_full, small_t)

    pair_block = pl.BlockSpec((count, LANES), lambda i, *rest: (0, i))
    dq, dk, dv = call(
        attend_back_kernel, "attend_back", (width // LANES,),
        [pair_block] * 4
        + [whole((16, count))] * 2
        + [whole((count, LANES))] * 2,
        [pair_block] * 3,
        [act] * 3,
        scratch=[pltpu.VMEM((count, count), BF16), pltpu.VMEM((count, LANES), F32)],
        flops=60 << 30, traffic=12 << 20, trans=HEADS * count * count, prefetch=1,
    )(prefix, queries, keys, values, heads_grad, lse, delta, cosine, sine)

    tokens_grad, dense_grad = call(
        project_back_kernel, "project_back", (steps,),
        [wide] * 6 + weight_block + [whole((LANES, width)), whole((width, LANES)), whole((width, width))],
        [wide, whole((owners, width, width + LANES))],
        [struct((count, width), F32), struct((owners, width, width + LANES), BF16)],
        scratch=[pltpu.VMEM((width, 3 * width), F32), pltpu.VMEM((8, width), F32)],
        flops=12 * count * width * width, traffic=24 << 20, prefetch=1,
    )(me, tokens, normed_one, dq, dk, dv, residual_grad, qkv_full, qkv_full, qkv_full, small_t,
      small_grad, output_grad)

    def send(part, k):
        return lax.ppermute(part, "expert", [(i, i ^ k) for i in range(owners)])

    def add(a, b):
        return (a.astype(F32) + b.astype(F32)).astype(BF16)

    half = width // 2
    top, low = dense_grad[:, :half], dense_grad[:, half:]
    top_in, low_in = send(top[1::2], 1), send(low[2:], 2)
    top, low = add(top[0::2], top_in), add(low[:2], low_in)
    top_in, low_in = send(top[1], 2), send(low[1], 1)
    quarter = jnp.concatenate([add(top[0], top_in), add(low[0], low_in)], axis=0)
    quarter, expert_sums = lax.optimization_barrier((quarter, expert_sums))
    quarter = lax.psum_scatter(quarter, "shard", scatter_dimension=0, tiled=True)
    dense = lax.all_gather(quarter, "expert", axis=0, tiled=False).astype(F32)
    small = dense[3, :, width:]
    if aligned:
        out_shapes = [w.shape for w in (gate_weight, up_weight, down_weight)]
        gate_sum, up_sum, down_sum = call(
            unpack_expert_kernel, "unpack", (1,),
            [whole((expert_rows, TILE))] * local_experts,
            [whole(o) for o in out_shapes], [struct(o, F32) for o in out_shapes],
            traffic=8 << 20,
        )(*expert_sums)
    else:
        split = 2 * tiles * shard_rows
        total = jnp.stack(expert_sums).astype(F32)
        gate_sum, up_sum = (
            part.reshape(local_experts, tiles, shard_rows, TILE).transpose(0, 2, 1, 3).reshape(
                local_experts, shard_rows, ff
            )
            for part in (total[:, : split // 2], total[:, split // 2 : split])
        )
        down_sum = total[:, split:].reshape(local_experts, width // TILE, down_rows, TILE)
        down_sum = down_sum.transpose(0, 2, 1, 3).reshape(local_experts, down_rows, width)
    return (
        mixed,
        tokens_grad,
        previous_grad,
        dense[0, :, :width],
        dense[1, :, :width],
        dense[2, :, :width],
        dense[3, :, :width],
        small[:, 0:kinds],
        small[:, kinds : kinds + 4],
        small[:, 18:20].T,
        small[:, 16],
        small[:, 17],
        gate_sum,
        up_sum,
        down_sum,
    )


def solution(mesh):
    rows = P(("expert", "shard"), None)
    expert = P("expert", "shard", None)
    flat = P("shard", None)
    return jax.shard_map(
        body,
        mesh=mesh,
        in_specs=(
            rows, rows, rows, P(("expert", "shard")), rows, P("shard"), flat, flat, flat, flat,
            P("shard"), flat, flat, P(None, "shard"), expert, expert, expert, rows,
        ),
        out_specs=(
            rows, rows, rows, flat, flat, flat, flat, flat, flat, P(None, "shard"), P("shard"),
            P("shard"), expert, expert, expert,
        ),
        check_vma=False,
    )
```

```python
import functools
import numpy as np
import jax
import jax.numpy as jnp
from jax import lax
from jax.experimental import pallas as pl
from jax.experimental.pallas import tpu as pltpu
from jax.sharding import PartitionSpec as P

HEADS = 12
HEAD_DIM = 64
ZC = 4
TOP = 2
LEN = 1024
EPS = 1e-05
NEG = -1e30
LANES = 128
BLOCK = 256
TILE = 256
F32 = jnp.float32
BF16 = jnp.bfloat16
VMEM_LIMIT = 56 << 20


def call(body, name, grid, in_specs, out_specs, out_shape, scratch=(), flops=0, traffic=0, trans=0, prefetch=0):
    return pl.pallas_call(
        body,
        name=name,
        grid_spec=pltpu.PrefetchScalarGridSpec(
            num_scalar_prefetch=prefetch,
            grid=grid,
            in_specs=in_specs,
            out_specs=out_specs,
            scratch_shapes=scratch,
        ),
        out_shape=out_shape,
        compiler_params=pltpu.CompilerParams(
            dimension_semantics=("arbitrary",) * len(grid), vmem_limit_bytes=VMEM_LIMIT
        ),
        cost_estimate=pl.CostEstimate(flops=flops, transcendentals=trans, bytes_accessed=traffic),
    )


def mm(a, b):
    return lax.dot_general(a, b, (((1,), (0,)), ((), ())), preferred_element_type=F32)


def mm_nt(a, b):
    return lax.dot_general(a, b, (((1,), (1,)), ((), ())), preferred_element_type=F32)


def mm_tn(a, b):
    return lax.dot_general(a, b, (((0,), (0,)), ((), ())), preferred_element_type=F32)


def iota(shape, axis):
    return lax.broadcasted_iota(jnp.int32, shape, axis)


def whole(shape):
    return pl.BlockSpec(shape, lambda *idx: (0,) * len(shape))


def rows_of(block, width):
    return pl.BlockSpec((block, width), lambda i, *rest: (i, 0))


def split_high_low(values):
    high = values.astype(BF16)
    low = (values - high.astype(F32)).astype(BF16)
    return high, low


def pack_kernel(me, q, k, v, o, gain1, gain2, router, mix, vectors, out, scratch):
    rows, width = q.shape
    for j, weight in enumerate((q, k, v, o)):

        @pl.when(me[0] == j)
        def _():
            out[:, 0:width] = weight[...]

    base = width
    out[:, base : base + LANES] = jnp.zeros((rows, LANES), BF16)
    scratch[...] = jnp.zeros_like(scratch)
    scratch[0:1, 0:rows] = gain1[...].astype(F32)
    scratch[1:2, 0:rows] = gain2[...].astype(F32)
    scratch[2:4, 0:rows] = vectors[...].astype(F32)
    columns = scratch[...].T
    n_router = router.shape[1]
    n_mix = mix.shape[1]
    out[:, base : base + n_router] = router[...]
    out[:, base + n_router : base + n_router + n_mix] = mix[...]
    out[:, base + 16 : base + 24] = columns[0:rows, 0:8].astype(BF16)


def slots_kernel(experts, capacity, stride, routes, order_row, order_col, dest_col, dest_row):
    tokens = routes.shape[0]
    r0 = routes[:, 0:1]
    r1 = routes[:, 1:2]
    lane = iota((tokens, LANES), 1)
    hot = jnp.where((lane == r0) | (lane == r1), 1.0, 0.0)
    hot = jnp.where(lane < experts, hot, 0.0).astype(BF16)
    row = iota((tokens, tokens), 0)
    col = iota((tokens, tokens), 1)
    to_turn = jnp.where(order_col[...] == col, 1.0, 0.0).astype(BF16)
    hot_turn = mm(to_turn, hot).astype(BF16)
    earlier = mm(jnp.where(col < row, 1.0, 0.0).astype(BF16), hot_turn)
    earlier = jnp.minimum(earlier, 255.0).astype(BF16)
    to_token = jnp.where(order_row[...] == row, 1.0, 0.0).astype(BF16)
    position = mm(to_token, earlier)
    p0 = jnp.sum(jnp.where(lane == r0, position, 0.0), axis=1, keepdims=True)
    p1 = jnp.sum(jnp.where(lane == r1, position, 0.0), axis=1, keepdims=True)
    d0 = jnp.where((r0 < experts) & (p0 < capacity), r0.astype(F32) * stride + p0, -1.0)
    d1 = jnp.where((r1 < experts) & (p1 < capacity), r1.astype(F32) * stride + p1, -1.0)
    both = jnp.where(lane == 0, d0, jnp.where(lane == 1, d1, 0.0))
    dest_col[...] = both.astype(jnp.int32)
    dest_row[...] = both.T[0:8, :].astype(jnp.int32)


def half_swap(values):
    lane = iota(values.shape, 1) % HEAD_DIM
    half = HEAD_DIM // 2
    return jnp.where(
        lane < half, pltpu.roll(values, LANES - half, 1), pltpu.roll(values, half, 1)
    )


def project_kernel(me, x, wq, wk, wv, small, cosine, sine, q_out, k_out, v_out, n_out, small_t):
    @pl.when(pl.program_id(0) == 0)
    def _():
        small_t[...] = small[...].astype(F32).T

    width = x.shape[1]
    rows = x[...].astype(F32)
    scale = lax.rsqrt(jnp.mean(rows * rows, axis=1, keepdims=True) + EPS)
    normed = (rows * scale * small_t[16:17, :]).astype(BF16)
    n_out[...] = normed
    cos = cosine[...]
    sin = sine[...]
    for weight, out, factor in ((wq, q_out, HEAD_DIM**-0.5), (wk, k_out, None)):
        lin = mm(normed, weight[0])
        for c in range(width // LANES):
            part = lin[:, c * LANES : (c + 1) * LANES]
            turned = part * cos + half_swap(part) * sin
            if factor is not None:
                turned = turned * factor
            out[:, c * LANES : (c + 1) * LANES] = turned.astype(BF16)
    v_out[...] = mm(normed, wv[0]).astype(BF16)


def attend_kernel(
    me, prefix, q, k, v, x, wo, small, small_t, prev, routes,
    mix_out, lse_out, res_out, n_out, tok_out, bias, mixed, lse,
):
    block, width = q.shape
    length = k.shape[0]
    start = pl.program_id(0) * block
    limit = jnp.maximum(start + iota((block, 1), 0) + 1, prefix[0])
    bias[...] = jnp.where(iota((block, length), 1) < limit, 0.0, NEG)
    lane = iota((block, LANES), 1)
    first = lane < HEAD_DIM
    lse[...] = jnp.zeros_like(lse)

    def one_pair(pair, carry):
        columns = pl.ds(pl.multiple_of(pair * LANES, LANES), LANES)
        q_pair = q[:, columns]
        k_pair = k[:, columns]
        v_pair = v[:, columns]
        outs = []
        for head in range(2):
            mine = first if head == 0 else jnp.logical_not(first)
            q_head = jnp.where(mine, q_pair, jnp.zeros_like(q_pair))
            scores = mm_nt(q_head, k_pair) + bias[...]
            top = jnp.max(scores, axis=1, keepdims=True)
            weights = jnp.exp(scores - top)
            total = jnp.sum(weights, axis=1, keepdims=True)
            outs.append(mm(weights.astype(BF16), v_pair) / total)
            lse[...] = jnp.where(lane == 2 * pair + head, top + jnp.log(total), lse[...])
        mixed[:, columns] = jnp.where(first, outs[0], outs[1]).astype(BF16)
        return carry

    lax.fori_loop(0, width // LANES, one_pair, 0)
    mix_out[...] = mixed[...]
    lse_out[...] = lse[...].T[0:16, :]
    residual = x[...].astype(F32) + mm(mixed[...], wo[0])
    res_out[...] = residual
    scale = lax.rsqrt(jnp.mean(residual * residual, axis=1, keepdims=True) + EPS)
    normed = (residual * scale * small_t[17:18, :]).astype(BF16)
    n_out[...] = normed
    lin = mm(normed, small[...])
    kinds = prev.shape[1]
    logits = lin[:, 0:kinds] + prev[...]
    kind = iota((block, kinds), 1)
    c0 = jnp.sum(jnp.where(kind == routes[:, 0:1], logits, 0.0), axis=1, keepdims=True)
    c1 = jnp.sum(jnp.where(kind == routes[:, 1:2], logits, 0.0), axis=1, keepdims=True)

    def pair_softmax(a, b):
        top = jnp.maximum(a, b)
        ea = jnp.exp(a - top)
        eb = jnp.exp(b - top)
        total = ea + eb
        return ea / total, eb / total

    g0, g1 = pair_softmax(c0, c1)
    m00, m01 = pair_softmax(lin[:, kinds : kinds + 1], lin[:, kinds + 1 : kinds + 2])
    m10, m11 = pair_softmax(lin[:, kinds + 2 : kinds + 3], lin[:, kinds + 3 : kinds + 4])
    packed = jnp.zeros((block, LANES), F32)
    for index, column in enumerate((g0, g1, m00, m01, m10, m11, scale)):
        packed = jnp.where(lane == index, column, packed)
    tok_out[...] = packed


def pack_expert_kernel(gate, up, down, out):
    rows, ff = gate.shape[1:]
    down_rows, width = down.shape[1:]
    tiles = ff // TILE
    for index, ref in enumerate((gate, up)):
        for f in range(tiles):
            start = (index * tiles + f) * rows
            out[start : start + rows, :] = ref[0, :, f * TILE : (f + 1) * TILE]
    base = 2 * tiles * rows
    for c in range(width // TILE):
        out[base + c * down_rows : base + (c + 1) * down_rows, :] = down[
            0, :, c * TILE : (c + 1) * TILE
        ]


def unpack_expert_kernel(*refs):
    gate, up, down = refs[-3:]
    rows, ff = gate.shape[1:]
    down_rows, width = down.shape[1:]
    tiles = ff // TILE
    base = 2 * tiles * rows
    for l, ref in enumerate(refs[:-3]):
        for index, out in enumerate((gate, up)):
            for f in range(tiles):
                start = (index * tiles + f) * rows
                out[l, :, f * TILE : (f + 1) * TILE] = ref[start : start + rows, :].astype(F32)
        for c in range(width // TILE):
            down[l, :, c * TILE : (c + 1) * TILE] = ref[
                base + c * down_rows : base + (c + 1) * down_rows, :
            ].astype(F32)


def dispatch_kernel(local_experts, l, me, normed, grad, tok, routes, dest_row, *rest):
    outs, gates = rest[:-1], rest[-1]
    step = pl.program_id(0)
    tokens = normed.shape[0]
    stride = outs[0].shape[1]
    expert = (me[0] ^ step) * local_experts + l

    @pl.when(step == 0)
    def _():
        lane = iota((tokens, LANES), 1)
        kind = lane % HEAD_DIM
        value = jnp.where(kind == routes[:, 0:1], tok[:, 0:1], 0.0)
        value = value + jnp.where(kind == routes[:, 1:2], tok[:, 1:2], 0.0)
        high = value.astype(BF16).astype(F32)
        gates[...] = jnp.where(lane < HEAD_DIM, high, value - high).astype(BF16)

    slot = expert * stride + iota((stride, tokens), 0)
    hit = (dest_row[0:1, :] == slot) | (dest_row[1:2, :] == slot)
    take = jnp.where(hit, 1.0, 0.0).astype(BF16)
    row = mm(take, normed[...]).astype(BF16)
    slot_gates = mm(take, gates[...])
    mine = iota((stride, LANES), 1) % HEAD_DIM == expert
    slot_gate = jnp.sum(jnp.where(mine, slot_gates, 0.0), axis=1, keepdims=True)
    slot_g = (mm(take, grad[...]) * slot_gate).astype(BF16)
    for k, out in enumerate(outs):

        @pl.when(step == k)
        def _():
            out[0] = row
            out[1] = slot_g


def expert_kernel(owners, merged, *refs):
    sent = refs[:owners]
    weights = refs[owners : owners + 6]
    backs = refs[owners + 6 : 2 * owners + 6]
    grads = refs[2 * owners + 6 : -4]
    r_all, s_all, out_acc, row_acc = refs[-4:]
    step = pl.program_id(0)
    steps = pl.num_programs(0)
    stride, width = sent[0].shape[1:]
    chunks, chunk_rows = weights[0].shape[:2]

    @pl.when(step == 0)
    def _():
        for k, ref in enumerate(sent):
            r_all[k * stride : (k + 1) * stride, :] = ref[0]
            s_all[k * stride : (k + 1) * stride, :] = ref[1]
        out_acc[...] = jnp.zeros_like(out_acc)
        row_acc[...] = jnp.zeros_like(row_acc)

    def tile_pair(a, b):
        return jnp.concatenate([t[...].reshape(width, TILE) for t in (a, b)], axis=1)

    def down_tile(ref):
        parts = [ref[0, c * TILE : (c + 1) * TILE, :] for c in range(width // TILE)]
        return jnp.concatenate(parts, axis=1)

    r = r_all[...]
    s = s_all[...]
    gate = tile_pair(weights[0], weights[1])
    up = tile_pair(weights[2], weights[3])
    d = jnp.concatenate([down_tile(weights[4]), down_tile(weights[5])], axis=0)
    gate_pre = mm(r, gate)
    up_pre = mm(r, up)
    sig = jax.nn.sigmoid(gate_pre)
    silu = gate_pre * sig
    hid = (silu * up_pre).astype(BF16)
    hidden_g = mm_nt(s, d)
    out_acc[...] += mm(hid, d)
    gate_g = (hidden_g * (up_pre * (sig + silu * (1.0 - sig)))).astype(BF16)
    up_g = (hidden_g * silu).astype(BF16)
    row_acc[...] += mm_nt(gate_g, gate) + mm_nt(up_g, up)
    down_grad = mm_tn(hid, s).astype(BF16)
    gate_grad = mm_tn(r, gate_g).astype(BF16)
    up_grad = mm_tn(r, up_g).astype(BF16)
    base = 4 * steps * chunk_rows if merged else 0
    for i in range(2):
        tile = 2 * step + i
        for index, value in enumerate((gate_grad, up_grad)):
            start = pl.multiple_of((index * 2 * steps + tile) * chunk_rows, 16)
            grads[0][:, pl.ds(start, chunk_rows), :] = value[:, i * TILE : (i + 1) * TILE].reshape(
                chunks, chunk_rows, TILE
            )
        for c in range(width // TILE):
            grads[-1][tile, base + c * TILE : base + (c + 1) * TILE, :] = down_grad[
                i * TILE : (i + 1) * TILE, c * TILE : (c + 1) * TILE
            ]

    @pl.when(step == steps - 1)
    def _():
        for k, ref in enumerate(backs):
            ref[0] = out_acc[k * stride : (k + 1) * stride, :].astype(BF16)
            ref[1] = row_acc[k * stride : (k + 1) * stride, :].astype(BF16)


def combine_kernel(experts, owners, local_experts, me, *refs):
    backs = refs[: owners * local_experts]
    (
        residual, normed, grad, tok, routes, dest, mix, wo, small_t,
        mixed_out, prev_out, resg_out, headg_out, delta_out, wo_out, small_out,
        wo_acc, small_acc, second_acc, eo_all, rg_all,
    ) = refs[owners * local_experts :]
    step = pl.program_id(0)
    block, width = residual.shape
    stride = backs[0].shape[1]
    local = owners * stride

    @pl.when(step == 0)
    def _():
        wo_acc[...] = jnp.zeros_like(wo_acc)
        small_acc[...] = jnp.zeros_like(small_acc)
        second_acc[...] = jnp.zeros_like(second_acc)
        for l in range(local_experts):
            for k in range(owners):
                place = slice(k * stride, (k + 1) * stride)
                eo_all[l, place, :] = backs[l * owners + k][0]
                rg_all[l, place, :] = backs[l * owners + k][1]

    slot = iota((1, local), 1)
    owner_slot = ((slot // stride) ^ me[0]) * (local_experts * stride) + slot % stride

    ep = [None, None]
    back = None
    for l in range(local_experts):
        ident = owner_slot + l * stride
        t0 = jnp.where(dest[:, 0:1] == ident, 1.0, 0.0)
        t1 = jnp.where(dest[:, 1:2] == ident, 1.0, 0.0)
        eo = eo_all[l]
        rg = rg_all[l]
        e0 = mm(t0.astype(BF16), eo)
        e1 = mm(t1.astype(BF16), eo)
        b = mm((t0 + t1).astype(BF16), rg)
        ep[0] = e0 if ep[0] is None else ep[0] + e0
        ep[1] = e1 if ep[1] is None else ep[1] + e1
        back = b if back is None else back + b

    res = residual[...]
    n_low = normed[...]
    nf = n_low.astype(F32)
    g_low = grad[...]
    g = g_low.astype(F32)
    gate = [tok[:, 0:1], tok[:, 1:2]]
    mw = [[tok[:, 2:3], tok[:, 3:4]], [tok[:, 4:5], tok[:, 5:6]]]
    scale = tok[:, 6:7]
    vec = [small_t[18:19, :], small_t[19:20, :]]
    along_n = jnp.sum(g * nf, axis=1, keepdims=True)
    along_vec = [jnp.sum(g * vec[c], axis=1, keepdims=True) for c in range(2)]
    gate_g = []
    on_n = 0.0
    sel = [0.0, 0.0]
    copy_weight = 0.0
    for t in range(TOP):
        route = routes[:, t : t + 1]
        is_copy = jnp.where(route == experts + 1, 1.0, 0.0)
        is_const = [jnp.where(route == experts + 2 + c, 1.0, 0.0) for c in range(2)]
        a = is_copy + is_const[0] * mw[0][0] + is_const[1] * mw[1][0]
        b = [is_const[c] * mw[c][1] for c in range(2)]
        gate_g.append(
            jnp.sum(g * ep[t], axis=1, keepdims=True)
            + a * along_n
            + b[0] * along_vec[0]
            + b[1] * along_vec[1]
        )
        on_n = on_n + gate[t] * a
        copy_weight = copy_weight + gate[t] * is_copy
        sel = [sel[c] + gate[t] * is_const[c] for c in range(2)]
    vec_w = [sel[c] * mw[c][1] for c in range(2)]
    mixed_out[...] = (
        res + gate[0] * ep[0] + gate[1] * ep[1] + on_n * nf + vec_w[0] * vec[0] + vec_w[1] * vec[1]
    ).astype(BF16)

    centre = gate[0] * gate_g[0] + gate[1] * gate_g[1]
    pair_g = [gate[t] * (gate_g[t] - centre) for t in range(TOP)]
    lane = iota((block, LANES), 1)
    logit_g = jnp.where(lane == routes[:, 0:1], pair_g[0], 0.0)
    logit_g = logit_g + jnp.where(lane == routes[:, 1:2], pair_g[1], 0.0)
    kinds = prev_out.shape[1]
    prev_out[...] = logit_g[:, 0:kinds]
    for c in range(2):
        w0 = sel[c] * along_n
        w1 = sel[c] * along_vec[c]
        mid = mw[c][0] * w0 + mw[c][1] * w1
        logit_g = jnp.where(lane == kinds + 2 * c, mw[c][0] * (w0 - mid), logit_g)
        logit_g = jnp.where(lane == kinds + 2 * c + 1, mw[c][1] * (w1 - mid), logit_g)
    high, low = split_high_low(logit_g)
    table = small_t[...]
    table = jnp.where(iota(table.shape, 0) < 16, table, 0.0).astype(BF16)
    direct = copy_weight + sel[0] * mw[0][0] + sel[1] * mw[1][0]
    normed_g = back + direct * g + mm(high, table) + mm(low, table)
    gain = small_t[17:18, :]
    scaled = normed_g * gain
    second_acc[...] += jnp.sum(
        (normed_g * res * scale).reshape(block // 8, 8, width), axis=0
    )
    resg = g + scale * scaled - res * (scale * scale * scale) * jnp.mean(
        scaled * res, axis=1, keepdims=True
    )
    resg_out[...] = resg
    attn_g = resg.astype(BF16)
    am = mix[...]
    wo_acc[...] += mm_tn(am, attn_g)
    heads_g = mm_nt(attn_g, wo[0]).astype(BF16)
    headg_out[...] = heads_g
    product = heads_g.astype(F32) * am.astype(F32)
    p_high, p_low = split_high_low(product)
    head_of = jnp.where(
        iota((16, width), 1) // HEAD_DIM == iota((16, width), 0), 1.0, 0.0
    ).astype(BF16)
    delta_out[...] = mm_nt(head_of, p_high) + mm_nt(head_of, p_low)
    small_acc[...] += mm_tn(n_low, high) + mm_tn(n_low, low)
    coefficient = jnp.where(lane == 18, vec_w[0], jnp.where(lane == 19, vec_w[1], 0.0))
    c_high, c_low = split_high_low(coefficient)
    small_acc[...] += mm_tn(g_low, c_high) + mm_tn(g_low, c_low)

    @pl.when(step == pl.num_programs(0) - 1)
    def _():
        wo_out[...] = wo_acc[...].astype(BF16)
        second = jnp.sum(second_acc[...], axis=0, keepdims=True)
        row = iota((LANES, width), 0)
        small_out[...] = small_acc[...] + jnp.where(row == 17, second, 0.0).T


def attend_back_kernel(
    prefix, q, k, v, grad, lse, delta, cosine, sine, dq_out, dk_out, dv_out, bias, dq_acc
):
    length = q.shape[0]
    pair = pl.program_id(0)
    block = BLOCK
    lane_all = iota((length, LANES), 1)
    lane = iota((block, LANES), 1)

    @pl.when(pair == 0)
    def _():
        limit = jnp.maximum(iota((1, length), 1) + 1, prefix[0])
        bias[...] = jnp.where(iota((length, length), 0) < limit, 0.0, NEG).astype(BF16)

    q_pair = q[...]
    g_pair = grad[...]
    zero = jnp.zeros_like(q_pair)
    q_head = []
    g_head = []
    for head in range(2):
        mine = (lane_all // HEAD_DIM) == head
        q_head.append(jnp.where(mine, q_pair, zero))
        g_head.append(jnp.where(mine, g_pair, zero))
    dq_acc[...] = jnp.zeros_like(dq_acc)

    def one_block(index, carry):
        place = pl.ds(pl.multiple_of(index * block, block), block)
        k_pair = k[place, :]
        v_pair = v[place, :]
        dk = None
        dv = None
        for head in range(2):
            mine = (lane // HEAD_DIM) == head
            k_head = jnp.where(mine, k_pair, jnp.zeros_like(k_pair))
            lse_row = lse[pl.ds(2 * pair + head, 1), :]
            delta_row = delta[pl.ds(2 * pair + head, 1), :]
            scores = mm_nt(k_pair, q_head[head]) + bias[place, :].astype(F32)
            weights = jnp.exp(scores - lse_row)
            probs_g = mm_nt(v_pair, g_head[head])
            one_dv = mm(weights.astype(BF16), g_head[head])
            scores_g = (weights * (probs_g - delta_row)).astype(BF16)
            one_dk = mm(scores_g, q_head[head])
            dq_acc[...] += mm_tn(scores_g, k_head)
            dk = one_dk if dk is None else dk + one_dk
            dv = one_dv if dv is None else dv + one_dv
        cos = cosine[place, :]
        sin = sine[place, :]
        dk_out[place, :] = (dk * cos - half_swap(dk) * sin).astype(BF16)
        dv_out[place, :] = dv.astype(BF16)
        return carry

    lax.fori_loop(0, length // block, one_block, 0)
    dq = dq_acc[...] * (HEAD_DIM**-0.5)
    dq_out[...] = (dq * cosine[...] - half_swap(dq) * sine[...]).astype(BF16)


def project_back_kernel(
    me, x, normed, dq, dk, dv, resg, wq, wk, wv, small_t, small_g, output_g,
    tok_out, grad_out, acc, first_acc,
):
    step = pl.program_id(0)
    block, width = x.shape

    @pl.when(step == 0)
    def _():
        acc[...] = jnp.zeros_like(acc)
        first_acc[...] = jnp.zeros_like(first_acc)

    rows = x[...].astype(F32)
    scale = lax.rsqrt(jnp.mean(rows * rows, axis=1, keepdims=True) + EPS)
    normed_g = mm_nt(dq[...], wq[0]) + mm_nt(dk[...], wk[0]) + mm_nt(dv[...], wv[0])
    n_low = normed[...]
    for index, part in enumerate((dq, dk, dv)):
        acc[:, index * width : (index + 1) * width] += mm_tn(n_low, part[...])
    first_acc[...] += jnp.sum(
        (normed_g * rows * scale).reshape(block // 8, 8, width), axis=0
    )
    scaled = normed_g * small_t[16:17, :]
    tok_out[...] = resg[...] + scale * scaled - rows * (scale * scale * scale) * jnp.mean(
        scaled * rows, axis=1, keepdims=True
    )

    @pl.when(step == pl.num_programs(0) - 1)
    def _():
        for j in range(3):
            grad_out[me[0] ^ j, :, 0:width] = acc[:, j * width : (j + 1) * width].astype(BF16)
            grad_out[me[0] ^ j, :, width : width + LANES] = jnp.zeros((width, LANES), BF16)
        first = jnp.sum(first_acc[...], axis=0, keepdims=True)
        row = iota((LANES, width), 0)
        extra = small_g[...] + jnp.where(row == 16, first, 0.0).T
        grad_out[me[0] ^ 3, :, 0:width] = output_g[...]
        grad_out[me[0] ^ 3, :, width : width + LANES] = extra.astype(BF16)


def rotary_tables():
    half = HEAD_DIM // 2
    frequency = np.float32(10000.0) ** (
        -np.arange(half, dtype=np.float32) * np.float32(2.0) / np.float32(HEAD_DIM)
    )
    angles = np.arange(LEN, dtype=np.float32)[:, None] * frequency[None, :].astype(np.float32)
    cos = np.cos(angles.astype(np.float64)).astype(np.float32)
    sin = np.sin(angles.astype(np.float64)).astype(np.float32)
    return np.tile(cos, (1, 4)), np.tile(np.concatenate([-sin, sin], axis=1), (1, 2))


def body(
    tokens, previous_logits, routes, prefix, slot_order, first_gain, query_weight, key_weight,
    value_weight, output_weight, second_gain, router_weight, constant_mix, constant_vectors,
    gate_weight, up_weight, down_weight, cotangent,
):
    owners = lax.axis_size("expert")
    shards = lax.axis_size("shard")
    local_experts, shard_rows, ff = gate_weight.shape
    experts = local_experts * owners
    count, width = tokens.shape
    kinds = experts + ZC
    capacity = count * TOP // kinds // 8 * 8
    stride = -(-capacity // 16) * 16
    tiles = ff // TILE
    down_rows = down_weight.shape[1]
    me = lax.axis_index("expert").astype(jnp.int32).reshape(1)
    packed_width = width + LANES
    cosine, sine = (jnp.asarray(t) for t in rotary_tables())
    struct = jax.ShapeDtypeStruct

    packed = call(
        pack_kernel, "pack", (1,),
        [whole((shard_rows, width))] * 4
        + [whole((1, shard_rows))] * 2
        + [whole((shard_rows, kinds)), whole((shard_rows, 4)), whole((2, shard_rows))],
        whole((shard_rows, packed_width)),
        struct((shard_rows, packed_width), BF16),
        scratch=[pltpu.VMEM((8, LANES), F32)],
        traffic=1 << 20, prefetch=1,
    )(
        me, query_weight, key_weight, value_weight, output_weight, first_gain[None], second_gain[None],
        router_weight, constant_mix, constant_vectors,
    )

    def send(part, k):
        return lax.ppermute(part, "expert", [(i, i ^ k) for i in range(owners)])

    half = width // 2
    own = lax.all_gather(packed, "shard", axis=0, tiled=True)
    top, low = own[None, :half, :width], own[None, half:, :width]
    top = jnp.concatenate([top, send(top, 1)])
    low = jnp.concatenate([low, send(low, 2)])
    top_in, low_in = send(top, 2), send(low, 1)
    weights = jnp.concatenate([
        jnp.concatenate([top, top_in]),
        jnp.stack([low[0], low_in[0], low[1], low_in[1]]),
    ], axis=1)
    aligned = shard_rows % 16 == 0 and down_rows == TILE
    expert_rows = 2 * tiles * shard_rows + width // TILE * down_rows

    def gather_expert(l):
        if aligned:
            one = call(
                pack_expert_kernel, "pack_expert", (1,),
                [pl.BlockSpec((1,) + w.shape[1:], lambda i: (l, 0, 0))
                 for w in (gate_weight, up_weight, down_weight)],
                whole((expert_rows, TILE)), struct((expert_rows, TILE), BF16), traffic=5 << 20,
            )(gate_weight, up_weight, down_weight)
        else:
            one = jnp.concatenate([
                w[l].reshape(w.shape[1], -1, TILE).transpose(1, 0, 2).reshape(-1, TILE)
                for w in (gate_weight, up_weight, down_weight)
            ])
        full = lax.all_gather(one, "shard", axis=0, tiled=True)
        full = full.reshape(shards, expert_rows, TILE)
        if aligned:
            return full, full
        split = 2 * tiles * shard_rows
        gate_up = full[:, :split].reshape(shards, 2 * tiles, shard_rows, TILE)
        down = full[:, split:].reshape(shards, width // TILE, down_rows, TILE)
        down = down.transpose(1, 0, 2, 3).reshape(width // TILE, tiles, TILE, TILE)
        return (
            gate_up.transpose(1, 0, 2, 3).reshape(1, -1, TILE),
            down.transpose(1, 0, 2, 3).reshape(tiles, width, TILE),
        )

    expert_full = [gather_expert(l) for l in range(local_experts)]

    dest_col, dest_row = call(
        functools.partial(slots_kernel, experts, capacity, stride), "slots", (1,),
        [whole((count, TOP)), whole((1, count)), whole((count, 1))],
        [whole((count, LANES)), whole((8, count))],
        [struct((count, LANES), jnp.int32), struct((8, count), jnp.int32)],
        flops=2 * 3 * count * count * LANES, traffic=1 << 20,
    )(routes, slot_order, slot_order.reshape(count, 1))

    steps = count // BLOCK
    weight_block = [
        pl.BlockSpec((1, width, width), lambda i, me, *rest, j=j: (me[0] ^ j, 0, 0))
        for j in range(4)
    ]
    output_block = weight_block.pop()
    small_block = pl.BlockSpec((width, LANES), lambda i, *rest: (0, width // LANES))
    wide = rows_of(BLOCK, width)
    table = rows_of(BLOCK, LANES)
    act = struct((count, width), BF16)
    queries, keys, values, normed_one, small_t = call(
        project_kernel, "project", (steps,),
        [wide] + weight_block + [small_block, table, table],
        [wide] * 4 + [whole((LANES, width))],
        [act] * 4 + [struct((LANES, width), F32)],
        flops=6 * count * width * width, traffic=12 << 20, prefetch=1,
    )(me, tokens, weights, weights, weights, own, cosine, sine)

    attn_mix, lse, residual, normed_two, tok = call(
        attend_kernel, "attend", (steps,),
        [wide, whole((count, width)), whole((count, width)), wide, output_block,
         small_block, whole((LANES, width)), rows_of(BLOCK, kinds), rows_of(BLOCK, TOP)],
        [wide, pl.BlockSpec((16, BLOCK), lambda i, *rest: (0, i)), wide, wide, table],
        [act, struct((16, count), F32), struct((count, width), F32), act,
         struct((count, LANES), F32)],
        scratch=[pltpu.VMEM((BLOCK, count), F32), pltpu.VMEM((BLOCK, width), BF16),
                 pltpu.VMEM((BLOCK, LANES), F32)],
        flops=30 << 30, traffic=16 << 20, trans=HEADS * count * count, prefetch=2,
    )(me, prefix, queries, keys, values, tokens, weights, own, small_t,
      previous_logits, routes)

    def exchange(parts):
        return [parts[0]] + [
            lax.ppermute(part, "expert", [(i, i ^ k) for i in range(owners)])
            for k, part in list(enumerate(parts))[1:]
        ]

    pair = whole((2, stride, width))
    pair_shape = struct((2, stride, width), BF16)

    def dispatch(l):
        parts = call(
            functools.partial(dispatch_kernel, local_experts, l), "dispatch", (owners,),
            [whole((count, width)), whole((count, width)), whole((count, LANES)),
             whole((count, TOP)), whole((8, count))],
            [pair] * owners, [pair_shape] * owners,
            scratch=[pltpu.VMEM((count, LANES), BF16)],
            flops=4 * owners * stride * count * width, traffic=6 << 20, prefetch=1,
        )(me, normed_two, cotangent, tok, routes, dest_row)
        return parts

    dispatched = [dispatch(l) for l in range(local_experts)]
    received = [exchange(parts) for parts in dispatched]

    chunks, chunk_rows = (shards, shard_rows) if aligned else (1, width)
    local = owners * stride

    def run_expert(l, rows, after):
        gate_up, down = expert_full[l]
        weights = [
            pl.BlockSpec((chunks, chunk_rows, TILE), lambda f, j=j: (0, j // 2 * tiles + 2 * f + j % 2, 0))
            for j in range(4)
        ] + [
            pl.BlockSpec((1, width, TILE), lambda f, j=j: (2 * f + j, 2 if aligned else 0, 0))
            for j in range(2)
        ]
        if aligned:
            grad_shapes = [(shards, expert_rows, TILE)]
        else:
            grad_shapes = [(1, 2 * tiles * width, TILE), (tiles, width, TILE)]
        outs = call(
            functools.partial(expert_kernel, owners, aligned), "expert", (tiles // 2,),
            [pair] * owners + weights,
            [pair] * owners + [whole(g) for g in grad_shapes],
            [pair_shape] * owners + [struct(g, BF16) for g in grad_shapes],
            scratch=[pltpu.VMEM((local, width), BF16)] * 2 + [pltpu.VMEM((local, width), F32)] * 2,
            flops=16 * local * width * ff, traffic=24 << 20, trans=local * ff,
        )(*rows, gate_up, gate_up, gate_up, gate_up, down, down)
        grads = outs[owners:]
        if aligned:
            grad = grads[0]
        else:
            gate_up_g = grads[0].reshape(2 * tiles, shards, shard_rows, TILE).transpose(1, 0, 2, 3)
            down_g = grads[1].reshape(tiles, width // TILE, TILE, TILE).transpose(1, 0, 2, 3)
            down_g = down_g.reshape(width // TILE, shards, down_rows, TILE).transpose(1, 0, 2, 3)
            grad = jnp.concatenate(
                [gate_up_g.reshape(shards, -1, TILE), down_g.reshape(shards, -1, TILE)], axis=1
            )
        grad, after = lax.optimization_barrier((grad, after))
        total = lax.psum_scatter(
            grad.reshape(shards * expert_rows, TILE), "shard", scatter_dimension=0, tiled=True
        )
        return outs[:owners], total, after

    returned = []
    expert_sums = []
    for l in range(local_experts):
        rows, ahead = lax.optimization_barrier((received[l], returned or dispatched[-1]))
        returned = ahead if returned else returned
        back, total, received[l + 1 :] = run_expert(l, rows, received[l + 1 :])
        returned = returned + exchange(back)
        expert_sums.append(total)

    mixed, previous_grad, residual_grad, heads_grad, delta, output_grad, small_grad = call(
        functools.partial(combine_kernel, experts, owners, local_experts), "combine", (steps,),
        [pair] * len(returned)
        + [wide, wide, wide, table, rows_of(BLOCK, TOP), table, wide, output_block,
           whole((LANES, width))],
        [wide, rows_of(BLOCK, kinds), wide, wide, pl.BlockSpec((16, BLOCK), lambda i, *rest: (0, i)),
         whole((width, width)), whole((width, LANES))],
        [act, struct((count, kinds), F32), struct((count, width), F32), act,
         struct((16, count), F32), struct((width, width), BF16), struct((width, LANES), F32)],
        scratch=[pltpu.VMEM((width, width), F32), pltpu.VMEM((width, LANES), F32),
                 pltpu.VMEM((8, width), F32)]
        + [pltpu.VMEM((local_experts, local, width), BF16)] * 2,
        flops=6 * count * 2 * local * width + 4 * count * width * width, traffic=24 << 20, prefetch=1,
    )(me, *returned, residual, normed_two, cotangent, tok,
      routes, dest_col, attn_mix, weights, small_t)

    pair_block = pl.BlockSpec((count, LANES), lambda i, *rest: (0, i))
    dq, dk, dv = call(
        attend_back_kernel, "attend_back", (width // LANES,),
        [pair_block] * 4
        + [whole((16, count))] * 2
        + [whole((count, LANES))] * 2,
        [pair_block] * 3,
        [act] * 3,
        scratch=[pltpu.VMEM((count, count), BF16), pltpu.VMEM((count, LANES), F32)],
        flops=60 << 30, traffic=12 << 20, trans=HEADS * count * count, prefetch=1,
    )(prefix, queries, keys, values, heads_grad, lse, delta, cosine, sine)

    tokens_grad, dense_grad = call(
        project_back_kernel, "project_back", (steps,),
        [wide] * 6 + weight_block + [whole((LANES, width)), whole((width, LANES)), whole((width, width))],
        [wide, whole((owners, width, width + LANES))],
        [struct((count, width), F32), struct((owners, width, width + LANES), BF16)],
        scratch=[pltpu.VMEM((width, 3 * width), F32), pltpu.VMEM((8, width), F32)],
        flops=12 * count * width * width, traffic=24 << 20, prefetch=1,
    )(me, tokens, normed_one, dq, dk, dv, residual_grad, weights, weights, weights, small_t,
      small_grad, output_grad)

    def add(a, b):
        return (a.astype(F32) + b.astype(F32)).astype(BF16)

    top, low = dense_grad[:, :half], dense_grad[:, half:]
    top_in, low_in = send(top[1::2], 1), send(low[2:], 2)
    top, low = add(top[0::2], top_in), add(low[:2], low_in)
    top_in, low_in = send(top[1], 2), send(low[1], 1)
    quarter = jnp.concatenate([add(top[0], top_in), add(low[0], low_in)], axis=0)
    quarter, expert_sums = lax.optimization_barrier((quarter, expert_sums))
    quarter = lax.psum_scatter(quarter, "shard", scatter_dimension=0, tiled=True)
    dense = lax.all_gather(quarter, "expert", axis=0, tiled=False).astype(F32)
    small = dense[3, :, width:]
    if aligned:
        out_shapes = [w.shape for w in (gate_weight, up_weight, down_weight)]
        gate_sum, up_sum, down_sum = call(
            unpack_expert_kernel, "unpack", (1,),
            [whole((expert_rows, TILE))] * local_experts,
            [whole(o) for o in out_shapes], [struct(o, F32) for o in out_shapes],
            traffic=8 << 20,
        )(*expert_sums)
    else:
        split = 2 * tiles * shard_rows
        total = jnp.stack(expert_sums).astype(F32)
        gate_sum, up_sum = (
            part.reshape(local_experts, tiles, shard_rows, TILE).transpose(0, 2, 1, 3).reshape(
                local_experts, shard_rows, ff
            )
            for part in (total[:, : split // 2], total[:, split // 2 : split])
        )
        down_sum = total[:, split:].reshape(local_experts, width // TILE, down_rows, TILE)
        down_sum = down_sum.transpose(0, 2, 1, 3).reshape(local_experts, down_rows, width)
    return (
        mixed,
        tokens_grad,
        previous_grad,
        dense[0, :, :width],
        dense[1, :, :width],
        dense[2, :, :width],
        dense[3, :, :width],
        small[:, 0:kinds],
        small[:, kinds : kinds + 4],
        small[:, 18:20].T,
        small[:, 16],
        small[:, 17],
        gate_sum,
        up_sum,
        down_sum,
    )


def solution(mesh):
    rows = P(("expert", "shard"), None)
    expert = P("expert", "shard", None)
    flat = P("shard", None)
    return jax.shard_map(
        body,
        mesh=mesh,
        in_specs=(
            rows, rows, rows, P(("expert", "shard")), rows, P("shard"), flat, flat, flat, flat,
            P("shard"), flat, flat, P(None, "shard"), expert, expert, expert, rows,
        ),
        out_specs=(
            rows, rows, rows, flat, flat, flat, flat, flat, flat, P(None, "shard"), P("shard"),
            P("shard"), expert, expert, expert,
        ),
        check_vma=False,
    )
```

```python
import functools
import numpy as np
import jax
import jax.numpy as jnp
from jax import lax
from jax.experimental import pallas as pl
from jax.experimental.pallas import tpu as pltpu
from jax.sharding import PartitionSpec as P

HEADS = 12
HEAD_DIM = 64
ZC = 4
TOP = 2
LEN = 1024
EPS = 1e-05
NEG = -1e30
LANES = 128
BLOCK = 256
TILE = 256
STRIDE = 32
F32 = jnp.float32
BF16 = jnp.bfloat16
VMEM_LIMIT = 56 << 20


def call(body, name, grid, in_specs, out_specs, out_shape, scratch=(), flops=0, traffic=0, trans=0, prefetch=0):
    return pl.pallas_call(
        body,
        name=name,
        grid_spec=pltpu.PrefetchScalarGridSpec(
            num_scalar_prefetch=prefetch,
            grid=grid,
            in_specs=in_specs,
            out_specs=out_specs,
            scratch_shapes=scratch,
        ),
        out_shape=out_shape,
        compiler_params=pltpu.CompilerParams(
            dimension_semantics=("arbitrary",) * len(grid), vmem_limit_bytes=VMEM_LIMIT
        ),
        cost_estimate=pl.CostEstimate(flops=flops, transcendentals=trans, bytes_accessed=traffic),
    )


def mm(a, b):
    return lax.dot_general(a, b, (((1,), (0,)), ((), ())), preferred_element_type=F32)


def mm_nt(a, b):
    return lax.dot_general(a, b, (((1,), (1,)), ((), ())), preferred_element_type=F32)


def mm_tn(a, b):
    return lax.dot_general(a, b, (((0,), (0,)), ((), ())), preferred_element_type=F32)


def iota(shape, axis):
    return lax.broadcasted_iota(jnp.int32, shape, axis)


def whole(shape):
    return pl.BlockSpec(shape, lambda *idx: (0,) * len(shape))


def rows_of(block, width):
    return pl.BlockSpec((block, width), lambda i, *rest: (i, 0))


def split_high_low(values):
    high = values.astype(BF16)
    low = (values - high.astype(F32)).astype(BF16)
    return high, low


def pack_kernel(me, q, k, v, o, gain1, gain2, router, mix, vectors, out, scratch):
    rows, width = q.shape
    for j, weight in enumerate((q, k, v, o)):

        @pl.when(me[0] == j)
        def _():
            out[:, 0:width] = weight[...]

    base = width
    out[:, base : base + LANES] = jnp.zeros((rows, LANES), BF16)
    scratch[...] = jnp.zeros_like(scratch)
    scratch[0:1, 0:rows] = gain1[...].astype(F32)
    scratch[1:2, 0:rows] = gain2[...].astype(F32)
    scratch[2:4, 0:rows] = vectors[...].astype(F32)
    columns = scratch[...].T
    n_router = router.shape[1]
    n_mix = mix.shape[1]
    out[:, base : base + n_router] = router[...]
    out[:, base + n_router : base + n_router + n_mix] = mix[...]
    out[:, base + 16 : base + 24] = columns[0:rows, 0:8].astype(BF16)


def slots_kernel(experts, capacity, stride, routes, order_row, order_col, dest_col, dest_row):
    tokens = routes.shape[0]
    r0 = routes[:, 0:1]
    r1 = routes[:, 1:2]
    lane = iota((tokens, LANES), 1)
    hot = jnp.where((lane == r0) | (lane == r1), 1.0, 0.0)
    hot = jnp.where(lane < experts, hot, 0.0).astype(BF16)
    row = iota((tokens, tokens), 0)
    col = iota((tokens, tokens), 1)
    to_turn = jnp.where(order_col[...] == col, 1.0, 0.0).astype(BF16)
    hot_turn = mm(to_turn, hot).astype(BF16)
    earlier = mm(jnp.where(col < row, 1.0, 0.0).astype(BF16), hot_turn)
    earlier = jnp.minimum(earlier, 255.0).astype(BF16)
    to_token = jnp.where(order_row[...] == row, 1.0, 0.0).astype(BF16)
    position = mm(to_token, earlier)
    p0 = jnp.sum(jnp.where(lane == r0, position, 0.0), axis=1, keepdims=True)
    p1 = jnp.sum(jnp.where(lane == r1, position, 0.0), axis=1, keepdims=True)
    d0 = jnp.where((r0 < experts) & (p0 < capacity), r0.astype(F32) * stride + p0, -1.0)
    d1 = jnp.where((r1 < experts) & (p1 < capacity), r1.astype(F32) * stride + p1, -1.0)
    both = jnp.where(lane == 0, d0, jnp.where(lane == 1, d1, 0.0))
    dest_col[...] = both.astype(jnp.int32)
    dest_row[...] = both.T[0:8, :].astype(jnp.int32)


def half_swap(values):
    lane = iota(values.shape, 1) % HEAD_DIM
    half = HEAD_DIM // 2
    return jnp.where(
        lane < half, pltpu.roll(values, LANES - half, 1), pltpu.roll(values, half, 1)
    )


def project_kernel(me, x, wq, wk, wv, small, cosine, sine, q_out, k_out, v_out, n_out, small_t):
    @pl.when(pl.program_id(0) == 0)
    def _():
        small_t[...] = small[...].astype(F32).T

    width = x.shape[1]
    rows = x[...].astype(F32)
    scale = lax.rsqrt(jnp.mean(rows * rows, axis=1, keepdims=True) + EPS)
    normed = (rows * scale * small_t[16:17, :]).astype(BF16)
    n_out[...] = normed.T
    cos = cosine[...]
    sin = sine[...]
    for weight, out, factor in ((wq, q_out, HEAD_DIM**-0.5), (wk, k_out, None)):
        lin = mm(normed, weight[0])
        for c in range(width // LANES):
            part = lin[:, c * LANES : (c + 1) * LANES]
            turned = part * cos + half_swap(part) * sin
            if factor is not None:
                turned = turned * factor
            out[:, c * LANES : (c + 1) * LANES] = turned.astype(BF16)
    v_out[...] = mm(normed, wv[0]).astype(BF16)


def attend_kernel(
    me, prefix, q, k, v, x, wo, small, small_t, prev, routes,
    mix_out, lse_out, res_out, n_out, tok_out, bias, mixed, lse,
):
    block, width = q.shape
    length = k.shape[0]
    start = pl.program_id(0) * block
    limit = jnp.maximum(start + iota((block, 1), 0) + 1, prefix[0])
    bias[...] = jnp.where(iota((block, length), 1) < limit, 0.0, NEG)
    lane = iota((block, LANES), 1)
    first = lane < HEAD_DIM
    lse[...] = jnp.zeros_like(lse)

    def one_pair(pair, carry):
        columns = pl.ds(pl.multiple_of(pair * LANES, LANES), LANES)
        q_pair = q[:, columns]
        k_pair = k[:, columns]
        v_pair = v[:, columns]
        outs = []
        for head in range(2):
            mine = first if head == 0 else jnp.logical_not(first)
            q_head = jnp.where(mine, q_pair, jnp.zeros_like(q_pair))
            scores = mm_nt(q_head, k_pair) + bias[...]
            top = jnp.max(scores, axis=1, keepdims=True)
            weights = jnp.exp(scores - top)
            total = jnp.sum(weights, axis=1, keepdims=True)
            outs.append(mm(weights.astype(BF16), v_pair) / total)
            lse[...] = jnp.where(lane == 2 * pair + head, top + jnp.log(total), lse[...])
        mixed[:, columns] = jnp.where(first, outs[0], outs[1]).astype(BF16)
        return carry

    lax.fori_loop(0, width // LANES, one_pair, 0)
    mix_out[...] = mixed[...]
    lse_out[...] = lse[...].T[0:16, :]
    residual = x[...].astype(F32) + mm(mixed[...], wo[0])
    res_out[...] = residual
    scale = lax.rsqrt(jnp.mean(residual * residual, axis=1, keepdims=True) + EPS)
    normed = (residual * scale * small_t[17:18, :]).astype(BF16)
    n_out[...] = normed
    lin = mm(normed, small[...])
    kinds = prev.shape[1]
    logits = lin[:, 0:kinds] + prev[...]
    kind = iota((block, kinds), 1)
    c0 = jnp.sum(jnp.where(kind == routes[:, 0:1], logits, 0.0), axis=1, keepdims=True)
    c1 = jnp.sum(jnp.where(kind == routes[:, 1:2], logits, 0.0), axis=1, keepdims=True)

    def pair_softmax(a, b):
        top = jnp.maximum(a, b)
        ea = jnp.exp(a - top)
        eb = jnp.exp(b - top)
        total = ea + eb
        return ea / total, eb / total

    g0, g1 = pair_softmax(c0, c1)
    m00, m01 = pair_softmax(lin[:, kinds : kinds + 1], lin[:, kinds + 1 : kinds + 2])
    m10, m11 = pair_softmax(lin[:, kinds + 2 : kinds + 3], lin[:, kinds + 3 : kinds + 4])
    packed = jnp.zeros((block, LANES), F32)
    for index, column in enumerate((g0, g1, m00, m01, m10, m11, scale)):
        packed = jnp.where(lane == index, column, packed)
    tok_out[...] = packed


def pack_expert_kernel(gate, up, down, out):
    rows, ff = gate.shape[1:]
    down_rows, width = down.shape[1:]
    tiles = ff // TILE
    for index, ref in enumerate((gate, up)):
        for f in range(tiles):
            start = (index * tiles + f) * rows
            out[start : start + rows, :] = ref[0, :, f * TILE : (f + 1) * TILE]
    base = 2 * tiles * rows
    for c in range(width // TILE):
        out[base + c * down_rows : base + (c + 1) * down_rows, :] = down[
            0, :, c * TILE : (c + 1) * TILE
        ]


def unpack_expert_kernel(*refs):
    gate, up, down = refs[-3:]
    rows, ff = gate.shape[1:]
    down_rows, width = down.shape[1:]
    tiles = ff // TILE
    base = 2 * tiles * rows
    for l, ref in enumerate(refs[:-3]):
        for index, out in enumerate((gate, up)):
            for f in range(tiles):
                start = (index * tiles + f) * rows
                out[l, :, f * TILE : (f + 1) * TILE] = ref[start : start + rows, :].astype(F32)
        for c in range(width // TILE):
            down[l, :, c * TILE : (c + 1) * TILE] = ref[
                base + c * down_rows : base + (c + 1) * down_rows, :
            ].astype(F32)


def dispatch_kernel(local_experts, l, me, normed, grad, tok, routes, dest_row, *rest):
    outs, gates = rest[:-1], rest[-1]
    step = pl.program_id(0)
    tokens = normed.shape[0]
    stride = outs[0].shape[1]
    expert = (me[0] ^ step) * local_experts + l

    @pl.when(step == 0)
    def _():
        lane = iota((tokens, LANES), 1)
        kind = lane % HEAD_DIM
        value = jnp.where(kind == routes[:, 0:1], tok[:, 0:1], 0.0)
        value = value + jnp.where(kind == routes[:, 1:2], tok[:, 1:2], 0.0)
        high = value.astype(BF16).astype(F32)
        gates[...] = jnp.where(lane < HEAD_DIM, high, value - high).astype(BF16)

    slot = expert * stride + iota((stride, tokens), 0)
    hit = (dest_row[0:1, :] == slot) | (dest_row[1:2, :] == slot)
    take = jnp.where(hit, 1.0, 0.0).astype(BF16)
    row = mm(take, normed[...]).astype(BF16)
    slot_gates = mm(take, gates[...])
    mine = iota((stride, LANES), 1) % HEAD_DIM == expert
    slot_gate = jnp.sum(jnp.where(mine, slot_gates, 0.0), axis=1, keepdims=True)
    slot_g = (mm(take, grad[...]) * slot_gate).astype(BF16)
    for k, out in enumerate(outs):

        @pl.when(step == k)
        def _():
            out[0] = row
            out[1] = slot_g


def expert_kernel(owners, merged, halves, core, *refs):
    sent = refs[:owners]
    weights = refs[owners : owners + 6]
    backs = refs[owners + 6 : 2 * owners + 6]
    grads = refs[2 * owners + 6 : -4]
    r_all, s_all, out_acc, row_acc = refs[-4:]
    step = pl.program_id(0)
    steps = pl.num_programs(0)
    stride, width = sent[0].shape[1:]
    chunks, chunk_rows = weights[0].shape[:2]

    @pl.when(step == 0)
    def _():
        for k, ref in enumerate(sent):
            r_all[k * stride : (k + 1) * stride, :] = ref[0]
            s_all[k * stride : (k + 1) * stride, :] = ref[1]
        out_acc[...] = jnp.zeros_like(out_acc)
        row_acc[...] = jnp.zeros_like(row_acc)

    def tile_pair(a, b):
        return jnp.concatenate([t[...].reshape(width, TILE) for t in (a, b)], axis=1)

    def down_tile(ref):
        parts = [ref[0, c * TILE : (c + 1) * TILE, :] for c in range(width // TILE)]
        return jnp.concatenate(parts, axis=1)

    r = r_all[...]
    s = s_all[...]
    gate = tile_pair(weights[0], weights[1])
    up = tile_pair(weights[2], weights[3])
    d = jnp.concatenate([down_tile(weights[4]), down_tile(weights[5])], axis=0)
    gate_pre = mm(r, gate)
    up_pre = mm(r, up)
    sig = jax.nn.sigmoid(gate_pre)
    silu = gate_pre * sig
    hid = (silu * up_pre).astype(BF16)
    hidden_g = mm_nt(s, d)
    out_acc[...] += mm(hid, d)
    gate_g = (hidden_g * (up_pre * (sig + silu * (1.0 - sig)))).astype(BF16)
    up_g = (hidden_g * silu).astype(BF16)
    row_acc[...] += mm_nt(gate_g, gate) + mm_nt(up_g, up)
    down_grad = mm_tn(hid, s).astype(BF16)
    gate_grad = mm_tn(r, gate_g).astype(BF16)
    up_grad = mm_tn(r, up_g).astype(BF16)
    even = core[0] == 0
    for i in range(2):
        tile = 2 * step + i
        for index, value in enumerate((gate_grad, up_grad)):
            start = pl.multiple_of((index * 2 * steps + tile) * chunk_rows, 16)
            place = pl.ds(start, chunk_rows)
            value = value[:, i * TILE : (i + 1) * TILE]
            if halves:
                value = value.reshape(chunks // 2, 2, chunk_rows, TILE)
                for out, flag in zip(grads, (even, jnp.logical_not(even))):
                    out[:, place, :] = jnp.where(flag, value[:, 0], value[:, 1])
            else:
                grads[0][:, place, :] = value.reshape(chunks, chunk_rows, TILE)
    base = 4 * steps * chunk_rows if merged else 0
    for c in range(width // TILE):
        pair = [down_grad[i * TILE : (i + 1) * TILE, c * TILE : (c + 1) * TILE] for i in range(2)]
        place = slice(base + c * TILE, base + (c + 1) * TILE)
        if halves:
            for out, flag in zip(grads, (even, jnp.logical_not(even))):
                out[step, place, :] = jnp.where(flag, pair[0], pair[1])
        else:
            for i in range(2):
                grads[-1][2 * step + i, place, :] = pair[i]

    @pl.when(step == steps - 1)
    def _():
        for k, ref in enumerate(backs):
            ref[0] = out_acc[k * stride : (k + 1) * stride, :].astype(BF16)
            ref[1] = row_acc[k * stride : (k + 1) * stride, :].astype(BF16)


def combine_kernel(experts, owners, local_experts, me, *refs):
    backs = refs[: owners * local_experts]
    (
        residual, normed, grad, tok, routes, dest, mix, wo, small_t,
        mixed_out, prev_out, resg_out, headg_out, delta_out, wo_out, small_out,
        wo_acc, small_acc, second_acc, eo_all, rg_all,
    ) = refs[owners * local_experts :]
    step = pl.program_id(0)
    block, width = residual.shape
    stride = backs[0].shape[1]
    local = owners * stride

    @pl.when(step == 0)
    def _():
        wo_acc[...] = jnp.zeros_like(wo_acc)
        small_acc[...] = jnp.zeros_like(small_acc)
        second_acc[...] = jnp.zeros_like(second_acc)
        for l in range(local_experts):
            for k in range(owners):
                place = slice(k * stride, (k + 1) * stride)
                eo_all[l, place, :] = backs[l * owners + k][0]
                rg_all[l, place, :] = backs[l * owners + k][1]

    slot = iota((1, local), 1)
    owner_slot = ((slot // stride) ^ me[0]) * (local_experts * stride) + slot % stride

    ep = [None, None]
    back = None
    for l in range(local_experts):
        ident = owner_slot + l * stride
        t0 = jnp.where(dest[:, 0:1] == ident, 1.0, 0.0)
        t1 = jnp.where(dest[:, 1:2] == ident, 1.0, 0.0)
        eo = eo_all[l]
        rg = rg_all[l]
        e0 = mm(t0.astype(BF16), eo)
        e1 = mm(t1.astype(BF16), eo)
        b = mm((t0 + t1).astype(BF16), rg)
        ep[0] = e0 if ep[0] is None else ep[0] + e0
        ep[1] = e1 if ep[1] is None else ep[1] + e1
        back = b if back is None else back + b

    res = residual[...]
    n_low = normed[...]
    nf = n_low.astype(F32)
    g_low = grad[...]
    g = g_low.astype(F32)
    gate = [tok[:, 0:1], tok[:, 1:2]]
    mw = [[tok[:, 2:3], tok[:, 3:4]], [tok[:, 4:5], tok[:, 5:6]]]
    scale = tok[:, 6:7]
    vec = [small_t[18:19, :], small_t[19:20, :]]
    along_n = jnp.sum(g * nf, axis=1, keepdims=True)
    along_vec = [jnp.sum(g * vec[c], axis=1, keepdims=True) for c in range(2)]
    gate_g = []
    on_n = 0.0
    sel = [0.0, 0.0]
    copy_weight = 0.0
    for t in range(TOP):
        route = routes[:, t : t + 1]
        is_copy = jnp.where(route == experts + 1, 1.0, 0.0)
        is_const = [jnp.where(route == experts + 2 + c, 1.0, 0.0) for c in range(2)]
        a = is_copy + is_const[0] * mw[0][0] + is_const[1] * mw[1][0]
        b = [is_const[c] * mw[c][1] for c in range(2)]
        gate_g.append(
            jnp.sum(g * ep[t], axis=1, keepdims=True)
            + a * along_n
            + b[0] * along_vec[0]
            + b[1] * along_vec[1]
        )
        on_n = on_n + gate[t] * a
        copy_weight = copy_weight + gate[t] * is_copy
        sel = [sel[c] + gate[t] * is_const[c] for c in range(2)]
    vec_w = [sel[c] * mw[c][1] for c in range(2)]
    mixed_out[...] = (
        res + gate[0] * ep[0] + gate[1] * ep[1] + on_n * nf + vec_w[0] * vec[0] + vec_w[1] * vec[1]
    ).astype(BF16)

    centre = gate[0] * gate_g[0] + gate[1] * gate_g[1]
    pair_g = [gate[t] * (gate_g[t] - centre) for t in range(TOP)]
    lane = iota((block, LANES), 1)
    logit_g = jnp.where(lane == routes[:, 0:1], pair_g[0], 0.0)
    logit_g = logit_g + jnp.where(lane == routes[:, 1:2], pair_g[1], 0.0)
    kinds = prev_out.shape[1]
    prev_out[...] = logit_g[:, 0:kinds]
    for c in range(2):
        w0 = sel[c] * along_n
        w1 = sel[c] * along_vec[c]
        mid = mw[c][0] * w0 + mw[c][1] * w1
        logit_g = jnp.where(lane == kinds + 2 * c, mw[c][0] * (w0 - mid), logit_g)
        logit_g = jnp.where(lane == kinds + 2 * c + 1, mw[c][1] * (w1 - mid), logit_g)
    high, low = split_high_low(logit_g)
    table = small_t[...]
    table = jnp.where(iota(table.shape, 0) < 16, table, 0.0).astype(BF16)
    direct = copy_weight + sel[0] * mw[0][0] + sel[1] * mw[1][0]
    normed_g = back + direct * g + mm(high, table) + mm(low, table)
    gain = small_t[17:18, :]
    scaled = normed_g * gain
    second_acc[...] += jnp.sum(
        (normed_g * res * scale).reshape(block // 8, 8, width), axis=0
    )
    resg = g + scale * scaled - res * (scale * scale * scale) * jnp.mean(
        scaled * res, axis=1, keepdims=True
    )
    resg_out[...] = resg
    attn_g = resg.astype(BF16)
    am = mix[...]
    wo_acc[...] += mm_tn(am, attn_g)
    heads_g = mm_nt(attn_g, wo[0]).astype(BF16)
    headg_out[...] = heads_g
    product = heads_g.astype(F32) * am.astype(F32)
    p_high, p_low = split_high_low(product)
    head_of = jnp.where(
        iota((16, width), 1) // HEAD_DIM == iota((16, width), 0), 1.0, 0.0
    ).astype(BF16)
    delta_out[...] = mm_nt(head_of, p_high) + mm_nt(head_of, p_low)
    small_acc[...] += mm_tn(n_low, high) + mm_tn(n_low, low)
    coefficient = jnp.where(lane == 18, vec_w[0], jnp.where(lane == 19, vec_w[1], 0.0))
    c_high, c_low = split_high_low(coefficient)
    small_acc[...] += mm_tn(g_low, c_high) + mm_tn(g_low, c_low)

    @pl.when(step == pl.num_programs(0) - 1)
    def _():
        wo_out[...] = wo_acc[...].astype(BF16)
        second = jnp.sum(second_acc[...], axis=0, keepdims=True)
        row = iota((LANES, width), 0)
        small_out[...] = small_acc[...] + jnp.where(row == 17, second, 0.0).T


def attend_back_kernel(
    start, me, prefix, q, k, v, grad, lse, delta, cosine, sine, normed, output_g,
    dq_out, dk_out, dv_out, grad_out, bias, dq_acc,
):
    length = q.shape[0]
    step = pl.program_id(0)
    pair = step + start
    block = BLOCK
    lane_all = iota((length, LANES), 1)
    lane = iota((block, LANES), 1)

    @pl.when(step == 0)
    def _():
        limit = jnp.maximum(iota((1, length), 1) + 1, prefix[0])
        bias[...] = jnp.where(iota((length, length), 0) < limit, 0.0, NEG).astype(BF16)
        grad_out[me[0] ^ 3] = output_g[...]

    q_pair = q[...]
    g_pair = grad[...]
    zero = jnp.zeros_like(q_pair)
    q_head = []
    g_head = []
    for head in range(2):
        mine = (lane_all // HEAD_DIM) == head
        q_head.append(jnp.where(mine, q_pair, zero))
        g_head.append(jnp.where(mine, g_pair, zero))
    dq_acc[...] = jnp.zeros_like(dq_acc)

    def one_block(index, carry):
        place = pl.ds(pl.multiple_of(index * block, block), block)
        k_pair = k[place, :]
        v_pair = v[place, :]
        dk = None
        dv = None
        for head in range(2):
            mine = (lane // HEAD_DIM) == head
            k_head = jnp.where(mine, k_pair, jnp.zeros_like(k_pair))
            lse_row = lse[pl.ds(2 * pair + head, 1), :]
            delta_row = delta[pl.ds(2 * pair + head, 1), :]
            scores = mm_nt(k_pair, q_head[head]) + bias[place, :].astype(F32)
            weights = jnp.exp(scores - lse_row)
            probs_g = mm_nt(v_pair, g_head[head])
            one_dv = mm(weights.astype(BF16), g_head[head])
            scores_g = (weights * (probs_g - delta_row)).astype(BF16)
            one_dk = mm(scores_g, q_head[head])
            dq_acc[...] += mm_tn(scores_g, k_head)
            dk = one_dk if dk is None else dk + one_dk
            dv = one_dv if dv is None else dv + one_dv
        cos = cosine[place, :]
        sin = sine[place, :]
        dk_out[place, :] = (dk * cos - half_swap(dk) * sin).astype(BF16)
        dv_out[place, :] = dv.astype(BF16)
        return carry

    lax.fori_loop(0, length // block, one_block, 0)
    dq = dq_acc[...] * (HEAD_DIM**-0.5)
    dq_out[...] = (dq * cosine[...] - half_swap(dq) * sine[...]).astype(BF16)
    columns = pl.ds(pl.multiple_of(step * LANES, LANES), LANES)
    for j, part in enumerate((dq_out, dk_out, dv_out)):
        grad_out[me[0] ^ j, :, columns] = mm(normed[...], part[...]).astype(BF16)


def project_back_kernel(me, x, *refs):
    parts = refs[:-9]
    resg, wq, wk, wv, small_t, small_g, tok_out, small_out, first_acc = refs[-9:]
    step = pl.program_id(0)
    block, width = x.shape

    @pl.when(step == 0)
    def _():
        first_acc[...] = jnp.zeros_like(first_acc)

    rows = x[...].astype(F32)
    scale = lax.rsqrt(jnp.mean(rows * rows, axis=1, keepdims=True) + EPS)
    normed_g = None
    for j, weight in enumerate((wq, wk, wv)):
        part = jnp.concatenate([p[...] for p in parts[j::3]], axis=1)
        one = mm_nt(part, weight[0])
        normed_g = one if normed_g is None else normed_g + one
    first_acc[...] += jnp.sum(
        (normed_g * rows * scale).reshape(block // 8, 8, width), axis=0
    )
    scaled = normed_g * small_t[16:17, :]
    tok_out[...] = resg[...] + scale * scaled - rows * (scale * scale * scale) * jnp.mean(
        scaled * rows, axis=1, keepdims=True
    )

    @pl.when(step == pl.num_programs(0) - 1)
    def _():
        first = jnp.sum(first_acc[...], axis=0, keepdims=True)
        row = iota((LANES, width), 0)
        small_out[...] = (small_g[...] + jnp.where(row == 16, first, 0.0).T).astype(BF16)


def rotary_tables():
    half = HEAD_DIM // 2
    frequency = 10000.0 ** (-np.arange(half) * 2.0 / HEAD_DIM)
    sign = np.tile(np.repeat([-1.0, 1.0], half), LANES // HEAD_DIM)
    tables = []
    for positions in (np.arange(0, LEN, STRIDE), np.arange(STRIDE)):
        angles = np.tile(positions[:, None] * frequency[None, :], (1, LANES // half))
        tables += [np.cos(angles), np.sin(angles)]
    return [t.astype(np.float32) for t in tables + [sign]]


def body(
    tokens, previous_logits, routes, prefix, slot_order, first_gain, query_weight, key_weight,
    value_weight, output_weight, second_gain, router_weight, constant_mix, constant_vectors,
    gate_weight, up_weight, down_weight, cotangent,
):
    owners = lax.axis_size("expert")
    shards = lax.axis_size("shard")
    local_experts, shard_rows, ff = gate_weight.shape
    experts = local_experts * owners
    count, width = tokens.shape
    kinds = experts + ZC
    capacity = count * TOP // kinds // 8 * 8
    stride = -(-capacity // 16) * 16
    tiles = ff // TILE
    down_rows = down_weight.shape[1]
    me = lax.axis_index("expert").astype(jnp.int32).reshape(1)
    packed_width = width + LANES
    cos_a, sin_a, cos_b, sin_b, sign = (jnp.asarray(t) for t in rotary_tables())
    cos_a, sin_a, cos_b, sin_b, me = lax.optimization_barrier((cos_a, sin_a, cos_b, sin_b, me))
    cos_a, sin_a, cos_b, sin_b = cos_a[:, None], sin_a[:, None], cos_b[None], sin_b[None]
    cosine = (cos_a * cos_b - sin_a * sin_b).reshape(LEN, LANES)
    sine = ((sin_a * cos_b + cos_a * sin_b) * sign).reshape(LEN, LANES)
    struct = jax.ShapeDtypeStruct

    packed = call(
        pack_kernel, "pack", (1,),
        [whole((shard_rows, width))] * 4
        + [whole((1, shard_rows))] * 2
        + [whole((shard_rows, kinds)), whole((shard_rows, 4)), whole((2, shard_rows))],
        whole((shard_rows, packed_width)),
        struct((shard_rows, packed_width), BF16),
        scratch=[pltpu.VMEM((8, LANES), F32)],
        traffic=1 << 20, prefetch=1,
    )(
        me, query_weight, key_weight, value_weight, output_weight, first_gain[None], second_gain[None],
        router_weight, constant_mix, constant_vectors,
    )

    def send(part, k):
        return lax.ppermute(part, "expert", [(i, i ^ k) for i in range(owners)])

    def add(a, b):
        return (a.astype(F32) + b.astype(F32)).astype(BF16)

    core = (lax.axis_index("shard") % 2).astype(jnp.int32).reshape(1)
    half = width // 2
    own = lax.all_gather(packed, "shard", axis=0, tiled=True)
    top, low = own[None, :half, :width], own[None, half:, :width]
    top = jnp.concatenate([top, send(top, 1)])
    low = jnp.concatenate([low, send(low, 2)])
    top_in, low_in = send(top, 2), send(low, 1)
    weights = jnp.concatenate([
        jnp.concatenate([top, top_in]),
        jnp.stack([low[0], low_in[0], low[1], low_in[1]]),
    ], axis=1)
    aligned = shard_rows % 16 == 0 and down_rows == TILE
    expert_rows = 2 * tiles * shard_rows + width // TILE * down_rows

    def gather_expert(l):
        if aligned:
            one = call(
                pack_expert_kernel, "pack_expert", (1,),
                [pl.BlockSpec((1,) + w.shape[1:], lambda i: (l, 0, 0))
                 for w in (gate_weight, up_weight, down_weight)],
                whole((expert_rows, TILE)), struct((expert_rows, TILE), BF16), traffic=5 << 20,
            )(gate_weight, up_weight, down_weight)
        else:
            one = jnp.concatenate([
                w[l].reshape(w.shape[1], -1, TILE).transpose(1, 0, 2).reshape(-1, TILE)
                for w in (gate_weight, up_weight, down_weight)
            ])
        full = lax.all_gather(one, "shard", axis=0, tiled=True)
        full = full.reshape(shards, expert_rows, TILE)
        if aligned:
            return full, full
        split = 2 * tiles * shard_rows
        gate_up = full[:, :split].reshape(shards, 2 * tiles, shard_rows, TILE)
        down = full[:, split:].reshape(shards, width // TILE, down_rows, TILE)
        down = down.transpose(1, 0, 2, 3).reshape(width // TILE, tiles, TILE, TILE)
        return (
            gate_up.transpose(1, 0, 2, 3).reshape(1, -1, TILE),
            down.transpose(1, 0, 2, 3).reshape(tiles, width, TILE),
        )

    expert_full = [gather_expert(l) for l in range(local_experts)]

    dest_col, dest_row = call(
        functools.partial(slots_kernel, experts, capacity, stride), "slots", (1,),
        [whole((count, TOP)), whole((1, count)), whole((count, 1))],
        [whole((count, LANES)), whole((8, count))],
        [struct((count, LANES), jnp.int32), struct((8, count), jnp.int32)],
        flops=2 * 3 * count * count * LANES, traffic=1 << 20,
    )(routes, slot_order, slot_order.reshape(count, 1))

    steps = count // BLOCK
    weight_block = [
        pl.BlockSpec((1, width, width), lambda i, me, *rest, j=j: (me[0] ^ j, 0, 0))
        for j in range(4)
    ]
    output_block = weight_block.pop()
    small_block = pl.BlockSpec((width, LANES), lambda i, *rest: (0, width // LANES))
    wide = rows_of(BLOCK, width)
    table = rows_of(BLOCK, LANES)
    act = struct((count, width), BF16)
    queries, keys, values, normed_one, small_t = call(
        project_kernel, "project", (steps,),
        [wide] + weight_block + [small_block, table, table],
        [wide] * 3 + [pl.BlockSpec((width, BLOCK), lambda i, *rest: (0, i)), whole((LANES, width))],
        [act] * 3 + [struct((width, count), BF16), struct((LANES, width), F32)],
        flops=6 * count * width * width, traffic=12 << 20, prefetch=1,
    )(me, tokens, weights, weights, weights, own, cosine, sine)

    attn_mix, lse, residual, normed_two, tok = call(
        attend_kernel, "attend", (steps,),
        [wide, whole((count, width)), whole((count, width)), wide, output_block,
         small_block, whole((LANES, width)), rows_of(BLOCK, kinds), rows_of(BLOCK, TOP)],
        [wide, pl.BlockSpec((16, BLOCK), lambda i, *rest: (0, i)), wide, wide, table],
        [act, struct((16, count), F32), struct((count, width), F32), act,
         struct((count, LANES), F32)],
        scratch=[pltpu.VMEM((BLOCK, count), F32), pltpu.VMEM((BLOCK, width), BF16),
                 pltpu.VMEM((BLOCK, LANES), F32)],
        flops=30 << 30, traffic=16 << 20, trans=HEADS * count * count, prefetch=2,
    )(me, prefix, queries, keys, values, tokens, weights, own, small_t,
      previous_logits, routes)

    def exchange(parts):
        return [parts[0]] + [
            lax.ppermute(part, "expert", [(i, i ^ k) for i in range(owners)])
            for k, part in list(enumerate(parts))[1:]
        ]

    pair = whole((2, stride, width))
    pair_shape = struct((2, stride, width), BF16)

    def dispatch(l):
        parts = call(
            functools.partial(dispatch_kernel, local_experts, l), "dispatch", (owners,),
            [whole((count, width)), whole((count, width)), whole((count, LANES)),
             whole((count, TOP)), whole((8, count))],
            [pair] * owners, [pair_shape] * owners,
            scratch=[pltpu.VMEM((count, LANES), BF16)],
            flops=4 * owners * stride * count * width, traffic=6 << 20, prefetch=1,
        )(me, normed_two, cotangent, tok, routes, dest_row)
        return parts

    dispatched = [dispatch(l) for l in range(local_experts)]
    received = [exchange(parts) for parts in dispatched]

    chunks, chunk_rows = (shards, shard_rows) if aligned else (1, width)
    local = owners * stride

    def run_expert(l, rows, after):
        gate_up, down = expert_full[l]
        weights = [
            pl.BlockSpec((chunks, chunk_rows, TILE), lambda f, *rest, j=j: (0, j // 2 * tiles + 2 * f + j % 2, 0))
            for j in range(4)
        ] + [
            pl.BlockSpec((1, width, TILE), lambda f, *rest, j=j: (2 * f + j, 2 if aligned else 0, 0))
            for j in range(2)
        ]
        halves = aligned and l + 1 == local_experts
        if halves:
            grad_shapes = [(shards // 2, expert_rows, TILE)] * 2
        elif aligned:
            grad_shapes = [(shards, expert_rows, TILE)]
        else:
            grad_shapes = [(1, 2 * tiles * width, TILE), (tiles, width, TILE)]
        outs = call(
            functools.partial(expert_kernel, owners, aligned, halves), "expert", (tiles // 2,),
            [pair] * owners + weights,
            [pair] * owners + [whole(g) for g in grad_shapes],
            [pair_shape] * owners + [struct(g, BF16) for g in grad_shapes],
            scratch=[pltpu.VMEM((local, width), BF16)] * 2 + [pltpu.VMEM((local, width), F32)] * 2,
            flops=16 * local * width * ff, traffic=24 << 20, trans=local * ff, prefetch=1,
        )(core, *rows, gate_up, gate_up, gate_up, gate_up, down, down)
        grads = outs[owners:]
        if halves:
            keep, give = grads
        elif aligned:
            grad = grads[0]
        else:
            gate_up_g = grads[0].reshape(2 * tiles, shards, shard_rows, TILE).transpose(1, 0, 2, 3)
            down_g = grads[1].reshape(tiles, width // TILE, TILE, TILE).transpose(1, 0, 2, 3)
            down_g = down_g.reshape(width // TILE, shards, down_rows, TILE).transpose(1, 0, 2, 3)
            grad = jnp.concatenate(
                [gate_up_g.reshape(shards, -1, TILE), down_g.reshape(shards, -1, TILE)], axis=1
            )
        if halves:
            grad = add(keep, lax.ppermute(give, "shard", [(i, i ^ 1) for i in range(shards)]))
        grad, after = lax.optimization_barrier((grad, after))
        return outs[:owners], grad.reshape(-1, TILE), after

    def reduce_expert(grad):
        return lax.psum_scatter(
            grad, "shard", scatter_dimension=0, tiled=True,
            axis_index_groups=(
                None if len(grad) == shards * expert_rows
                else [list(range(c, shards, 2)) for c in range(2)]
            ),
        )

    returned = []
    expert_sums = []
    for l in range(local_experts):
        rows, ahead = lax.optimization_barrier((received[l], returned or dispatched[-1]))
        returned = ahead if returned else returned
        back, grad, received[l + 1 :] = run_expert(l, rows, received[l + 1 :])
        back = exchange(back)
        if l + 1 == local_experts:
            back, grad = lax.optimization_barrier((back, grad))
        returned = returned + back
        expert_sums.append(reduce_expert(grad))

    mixed, previous_grad, residual_grad, heads_grad, delta, output_grad, small_grad = call(
        functools.partial(combine_kernel, experts, owners, local_experts), "combine", (steps,),
        [pair] * len(returned)
        + [wide, wide, wide, table, rows_of(BLOCK, TOP), table, wide, output_block,
           whole((LANES, width))],
        [wide, rows_of(BLOCK, kinds), wide, wide, pl.BlockSpec((16, BLOCK), lambda i, *rest: (0, i)),
         whole((width, width)), whole((width, LANES))],
        [act, struct((count, kinds), F32), struct((count, width), F32), act,
         struct((16, count), F32), struct((width, width), BF16), struct((width, LANES), F32)],
        scratch=[pltpu.VMEM((width, width), F32), pltpu.VMEM((width, LANES), F32),
                 pltpu.VMEM((8, width), F32)]
        + [pltpu.VMEM((local_experts, local, width), BF16)] * 2,
        flops=6 * count * 2 * local * width + 4 * count * width * width, traffic=24 << 20, prefetch=1,
    )(me, *returned, residual, normed_two, cotangent, tok,
      routes, dest_col, attn_mix, weights, small_t)

    def first_turn(grad):
        return send(grad[1::2, :half], 1), send(grad[2:, half:], 2)

    def second_turn(grad, came):
        top, low = add(grad[0::2, :half], came[0]), add(grad[:2, half:], came[1])
        return (top[0], low[0]), (send(top[1], 2), send(low[1], 1))

    def join(mine, came):
        return jnp.concatenate([add(a, b) for a, b in zip(mine, came)], axis=0)

    pairs = width // LANES // 2
    columns = pairs * LANES
    half_out = pl.BlockSpec((count, LANES), lambda i, *rest: (0, i))
    parts = []
    dense_grads = []
    moved = ()
    for start in (0, pairs):
        pair_block = pl.BlockSpec((count, LANES), lambda i, *rest, start=start: (0, i + start))
        *three, dense_grad = call(
            functools.partial(attend_back_kernel, start), "attend_back", (pairs,),
            [pair_block] * 4
            + [whole((16, count))] * 2
            + [whole((count, LANES))] * 2
            + [whole((width, count)),
               pl.BlockSpec((width, columns), lambda i, *rest, start=start: (0, start // pairs))],
            [half_out] * 3 + [whole((owners, width, columns))],
            [struct((count, columns), BF16)] * 3 + [struct((owners, width, columns), BF16)],
            scratch=[pltpu.VMEM((count, count), BF16), pltpu.VMEM((count, LANES), F32)],
            flops=30 << 30, traffic=6 << 20, trans=HEADS // 2 * count * count, prefetch=2,
        )(me, prefix, queries, keys, values, heads_grad, lse, delta, cosine, sine, normed_one,
          output_grad)
        if start:
            three, moved, expert_sums[0] = lax.optimization_barrier((three, moved, expert_sums[0]))
        parts += three
        dense_grads.append(dense_grad)
        if start == 0:
            moved = first_turn(dense_grad)
    mine_a, moved_a = second_turn(dense_grads[0], moved)
    moved_b = first_turn(dense_grads[1])

    half_wide = rows_of(BLOCK, columns)
    tokens_grad, small_grad = call(
        project_back_kernel, "project_back", (steps,),
        [wide] + [half_wide] * 6 + [wide] + weight_block
        + [whole((LANES, width)), whole((width, LANES))],
        [wide, whole((width, LANES))],
        [struct((count, width), F32), struct((width, LANES), BF16)],
        scratch=[pltpu.VMEM((8, width), F32)],
        flops=6 * count * width * width, traffic=18 << 20, prefetch=1,
    )(me, tokens, *parts, residual_grad, weights, weights, weights, small_t, small_grad)
    small_grad, moved_a, moved_b = lax.optimization_barrier((small_grad, moved_a, moved_b))
    mine_b, moved_b = second_turn(dense_grads[1], moved_b)
    quarters = [join(mine_a, moved_a), join(mine_b, moved_b)]
    quarter = jnp.concatenate(quarters + [small_grad], axis=1)
    quarter, expert_sums = lax.optimization_barrier((quarter, expert_sums))
    quarter = lax.psum_scatter(quarter, "shard", scatter_dimension=0, tiled=True)
    gathered = lax.all_gather(quarter, "expert", axis=0, tiled=False).astype(F32)
    dense = gathered[:, :, :width]
    small = jnp.sum(gathered[:, :, width:], axis=0)
    if aligned:
        out_shapes = [w.shape for w in (gate_weight, up_weight, down_weight)]
        gate_sum, up_sum, down_sum = call(
            unpack_expert_kernel, "unpack", (1,),
            [whole((expert_rows, TILE))] * local_experts,
            [whole(o) for o in out_shapes], [struct(o, F32) for o in out_shapes],
            traffic=8 << 20,
        )(*expert_sums)
    else:
        split = 2 * tiles * shard_rows
        total = jnp.stack(expert_sums).astype(F32)
        gate_sum, up_sum = (
            part.reshape(local_experts, tiles, shard_rows, TILE).transpose(0, 2, 1, 3).reshape(
                local_experts, shard_rows, ff
            )
            for part in (total[:, : split // 2], total[:, split // 2 : split])
        )
        down_sum = total[:, split:].reshape(local_experts, width // TILE, down_rows, TILE)
        down_sum = down_sum.transpose(0, 2, 1, 3).reshape(local_experts, down_rows, width)
    return (
        mixed,
        tokens_grad,
        previous_grad,
        dense[0],
        dense[1],
        dense[2],
        dense[3],
        small[:, 0:kinds],
        small[:, kinds : kinds + 4],
        small[:, 18:20].T,
        small[:, 16],
        small[:, 17],
        gate_sum,
        up_sum,
        down_sum,
    )


def solution(mesh):
    rows = P(("expert", "shard"), None)
    expert = P("expert", "shard", None)
    flat = P("shard", None)
    return jax.shard_map(
        body,
        mesh=mesh,
        in_specs=(
            rows, rows, rows, P(("expert", "shard")), rows, P("shard"), flat, flat, flat, flat,
            P("shard"), flat, flat, P(None, "shard"), expert, expert, expert, rows,
        ),
        out_specs=(
            rows, rows, rows, flat, flat, flat, flat, flat, flat, P(None, "shard"), P("shard"),
            P("shard"), expert, expert, expert,
        ),
        check_vma=False,
    )
```

```python
import functools
import numpy as np
import jax
import jax.numpy as jnp
from jax import lax
from jax.experimental import pallas as pl
from jax.experimental.pallas import tpu as pltpu
from jax.sharding import PartitionSpec as P

HEADS = 12
HEAD_DIM = 64
ZC = 4
TOP = 2
LEN = 1024
EPS = 1e-05
NEG = -1e30
LANES = 128
BLOCK = 256
TILE = 256
STRIDE = 32
F32 = jnp.float32
BF16 = jnp.bfloat16
VMEM_LIMIT = 56 << 20


def call(body, name, grid, in_specs, out_specs, out_shape, scratch=(), flops=0, traffic=0, trans=0, prefetch=0):
    return pl.pallas_call(
        body,
        name=name,
        grid_spec=pltpu.PrefetchScalarGridSpec(
            num_scalar_prefetch=prefetch,
            grid=grid,
            in_specs=in_specs,
            out_specs=out_specs,
            scratch_shapes=scratch,
        ),
        out_shape=out_shape,
        compiler_params=pltpu.CompilerParams(
            dimension_semantics=("arbitrary",) * len(grid), vmem_limit_bytes=VMEM_LIMIT
        ),
        cost_estimate=pl.CostEstimate(flops=flops, transcendentals=trans, bytes_accessed=traffic),
    )


def mm(a, b):
    return lax.dot_general(a, b, (((1,), (0,)), ((), ())), preferred_element_type=F32)


def mm_nt(a, b):
    return lax.dot_general(a, b, (((1,), (1,)), ((), ())), preferred_element_type=F32)


def mm_tn(a, b):
    return lax.dot_general(a, b, (((0,), (0,)), ((), ())), preferred_element_type=F32)


def iota(shape, axis):
    return lax.broadcasted_iota(jnp.int32, shape, axis)


def whole(shape):
    return pl.BlockSpec(shape, lambda *idx: (0,) * len(shape))


def rows_of(block, width):
    return pl.BlockSpec((block, width), lambda i, *rest: (i, 0))


def split_high_low(values):
    high = values.astype(BF16)
    low = (values - high.astype(F32)).astype(BF16)
    return high, low


def pack_kernel(me, q, k, v, o, gain1, gain2, router, mix, vectors, out, scratch):
    rows, width = q.shape
    for j, weight in enumerate((q, k, v, o)):

        @pl.when(me[0] == j)
        def _():
            out[:, 0:width] = weight[...]

    scratch[...] = jnp.zeros_like(scratch)
    n_router = router.shape[0]
    scratch[0:n_router, 0:rows] = router[...].astype(F32)
    scratch[n_router : n_router + mix.shape[0], 0:rows] = mix[...].astype(F32)
    scratch[16:17, 0:rows] = gain1[...].astype(F32)
    scratch[17:18, 0:rows] = gain2[...].astype(F32)
    scratch[18:20, 0:rows] = vectors[...].astype(F32)
    out[:, width : width + LANES] = scratch[...].T[0:rows, :].astype(BF16)


def slots_kernel(experts, capacity, stride, routes, order_row, order_col, dest_col, dest_row):
    tokens = routes.shape[0]
    r0 = routes[:, 0:1]
    r1 = routes[:, 1:2]
    lane = iota((tokens, LANES), 1)
    hot = jnp.where((lane == r0) | (lane == r1), 1.0, 0.0)
    hot = jnp.where(lane < experts, hot, 0.0).astype(BF16)
    row = iota((tokens, tokens), 0)
    col = iota((tokens, tokens), 1)
    to_turn = jnp.where(order_col[...] == col, 1.0, 0.0).astype(BF16)
    hot_turn = mm(to_turn, hot).astype(BF16)
    earlier = mm(jnp.where(col < row, 1.0, 0.0).astype(BF16), hot_turn)
    earlier = jnp.minimum(earlier, 255.0).astype(BF16)
    to_token = jnp.where(order_row[...] == row, 1.0, 0.0).astype(BF16)
    position = mm(to_token, earlier)
    p0 = jnp.sum(jnp.where(lane == r0, position, 0.0), axis=1, keepdims=True)
    p1 = jnp.sum(jnp.where(lane == r1, position, 0.0), axis=1, keepdims=True)
    d0 = jnp.where((r0 < experts) & (p0 < capacity), r0.astype(F32) * stride + p0, -1.0)
    d1 = jnp.where((r1 < experts) & (p1 < capacity), r1.astype(F32) * stride + p1, -1.0)
    both = jnp.where(lane == 0, d0, jnp.where(lane == 1, d1, 0.0))
    dest_col[...] = both.astype(jnp.int32)
    dest_row[...] = both.T[0:8, :].astype(jnp.int32)


def half_swap(values):
    lane = iota(values.shape, 1) % HEAD_DIM
    half = HEAD_DIM // 2
    return jnp.where(
        lane < half, pltpu.roll(values, LANES - half, 1), pltpu.roll(values, half, 1)
    )


def project_kernel(me, x, wq, wk, wv, small, cosine, sine, q_out, k_out, v_out, n_out, small_t):
    @pl.when(pl.program_id(0) == 0)
    def _():
        small_t[...] = small[...].astype(F32).T

    width = x.shape[1]
    rows = x[...].astype(F32)
    scale = lax.rsqrt(jnp.mean(rows * rows, axis=1, keepdims=True) + EPS)
    normed = (rows * scale * small_t[16:17, :]).astype(BF16)
    n_out[...] = normed.T
    cos = cosine[...]
    sin = sine[...]
    for weight, out, factor in ((wq, q_out, HEAD_DIM**-0.5), (wk, k_out, None)):
        lin = mm(normed, weight[0])
        for c in range(width // LANES):
            part = lin[:, c * LANES : (c + 1) * LANES]
            turned = part * cos + half_swap(part) * sin
            if factor is not None:
                turned = turned * factor
            out[:, c * LANES : (c + 1) * LANES] = turned.astype(BF16)
    v_out[...] = mm(normed, wv[0]).astype(BF16)


def attend_kernel(
    me, prefix, q, k, v, x, wo, small, small_t, prev, routes,
    mix_out, lse_out, res_out, n_out, tok_out, bias, mixed, lse,
):
    block, width = q.shape
    length = k.shape[0]
    start = pl.program_id(0) * block
    limit = jnp.maximum(start + iota((block, 1), 0) + 1, prefix[0])
    bias[...] = jnp.where(iota((block, length), 1) < limit, 0.0, NEG)
    lane = iota((block, LANES), 1)
    first = lane < HEAD_DIM
    lse[...] = jnp.zeros_like(lse)

    def one_pair(pair, carry):
        columns = pl.ds(pl.multiple_of(pair * LANES, LANES), LANES)
        q_pair = q[:, columns]
        k_pair = k[:, columns]
        v_pair = v[:, columns]
        outs = []
        for head in range(2):
            mine = first if head == 0 else jnp.logical_not(first)
            q_head = jnp.where(mine, q_pair, jnp.zeros_like(q_pair))
            scores = mm_nt(q_head, k_pair) + bias[...]
            top = jnp.max(scores, axis=1, keepdims=True)
            weights = jnp.exp(scores - top)
            total = jnp.sum(weights, axis=1, keepdims=True)
            outs.append(mm(weights.astype(BF16), v_pair) / total)
            lse[...] = jnp.where(lane == 2 * pair + head, top + jnp.log(total), lse[...])
        mixed[:, columns] = jnp.where(first, outs[0], outs[1]).astype(BF16)
        return carry

    lax.fori_loop(0, width // LANES, one_pair, 0)
    mix_out[...] = mixed[...]
    lse_out[...] = lse[...].T[0:16, :]
    residual = x[...].astype(F32) + mm(mixed[...], wo[0])
    res_out[...] = residual
    scale = lax.rsqrt(jnp.mean(residual * residual, axis=1, keepdims=True) + EPS)
    normed = (residual * scale * small_t[17:18, :]).astype(BF16)
    n_out[...] = normed
    lin = mm(normed, small[...])
    kinds = prev.shape[1]
    logits = lin[:, 0:kinds] + prev[...]
    kind = iota((block, kinds), 1)
    c0 = jnp.sum(jnp.where(kind == routes[:, 0:1], logits, 0.0), axis=1, keepdims=True)
    c1 = jnp.sum(jnp.where(kind == routes[:, 1:2], logits, 0.0), axis=1, keepdims=True)

    def pair_softmax(a, b):
        top = jnp.maximum(a, b)
        ea = jnp.exp(a - top)
        eb = jnp.exp(b - top)
        total = ea + eb
        return ea / total, eb / total

    g0, g1 = pair_softmax(c0, c1)
    m00, m01 = pair_softmax(lin[:, kinds : kinds + 1], lin[:, kinds + 1 : kinds + 2])
    m10, m11 = pair_softmax(lin[:, kinds + 2 : kinds + 3], lin[:, kinds + 3 : kinds + 4])
    packed = jnp.zeros((block, LANES), F32)
    for index, column in enumerate((g0, g1, m00, m01, m10, m11, scale)):
        packed = jnp.where(lane == index, column, packed)
    tok_out[...] = packed


def pack_expert_kernel(gate, up, down, out):
    rows, ff = gate.shape[1:]
    down_rows, width = down.shape[1:]
    tiles = ff // TILE
    for index, ref in enumerate((gate, up)):
        for f in range(tiles):
            start = (index * tiles + f) * rows
            out[start : start + rows, :] = ref[0, :, f * TILE : (f + 1) * TILE]
    base = 2 * tiles * rows
    for c in range(width // TILE):
        out[base + c * down_rows : base + (c + 1) * down_rows, :] = down[
            0, :, c * TILE : (c + 1) * TILE
        ]


def unpack_expert_kernel(*refs):
    gate, up, down = refs[-3:]
    rows, ff = gate.shape[1:]
    down_rows, width = down.shape[1:]
    tiles = ff // TILE
    base = 2 * tiles * rows
    for l, ref in enumerate(refs[:-3]):
        for index, out in enumerate((gate, up)):
            for f in range(tiles):
                start = (index * tiles + f) * rows
                out[l, :, f * TILE : (f + 1) * TILE] = ref[start : start + rows, :].astype(F32)
        for c in range(width // TILE):
            down[l, :, c * TILE : (c + 1) * TILE] = ref[
                base + c * down_rows : base + (c + 1) * down_rows, :
            ].astype(F32)


def dispatch_kernel(local_experts, l, me, normed, grad, tok, routes, dest_row, *rest):
    outs, gates = rest[:-1], rest[-1]
    step = pl.program_id(0)
    tokens = normed.shape[0]
    stride = outs[0].shape[1]
    expert = (me[0] ^ step) * local_experts + l

    @pl.when(step == 0)
    def _():
        lane = iota((tokens, LANES), 1)
        kind = lane % HEAD_DIM
        value = jnp.where(kind == routes[:, 0:1], tok[:, 0:1], 0.0)
        value = value + jnp.where(kind == routes[:, 1:2], tok[:, 1:2], 0.0)
        high = value.astype(BF16).astype(F32)
        gates[...] = jnp.where(lane < HEAD_DIM, high, value - high).astype(BF16)

    slot = expert * stride + iota((stride, tokens), 0)
    hit = (dest_row[0:1, :] == slot) | (dest_row[1:2, :] == slot)
    take = jnp.where(hit, 1.0, 0.0).astype(BF16)
    row = mm(take, normed[...]).astype(BF16)
    slot_gates = mm(take, gates[...])
    mine = iota((stride, LANES), 1) % HEAD_DIM == expert
    slot_gate = jnp.sum(jnp.where(mine, slot_gates, 0.0), axis=1, keepdims=True)
    slot_g = (mm(take, grad[...]) * slot_gate).astype(BF16)
    for k, out in enumerate(outs):

        @pl.when(step == k)
        def _():
            out[0] = row
            out[1] = slot_g


def expert_kernel(owners, merged, halves, core, *refs):
    sent = refs[:owners]
    weights = refs[owners : owners + 6]
    backs = refs[owners + 6 : 2 * owners + 6]
    grads = refs[2 * owners + 6 : -5]
    r_all, s_all, r_turned, out_acc, row_acc = refs[-5:]
    step = pl.program_id(0)
    steps = pl.num_programs(0)
    stride, width = sent[0].shape[1:]
    chunks, chunk_rows = weights[0].shape[:2]

    @pl.when(step == 0)
    def _():
        for k, ref in enumerate(sent):
            r_all[k * stride : (k + 1) * stride, :] = ref[0]
            s_all[k * stride : (k + 1) * stride, :] = ref[1]
        r_turned[...] = r_all[...].T
        out_acc[...] = jnp.zeros_like(out_acc)
        row_acc[...] = jnp.zeros_like(row_acc)

    def tile_pair(a, b):
        return jnp.concatenate([t[...].reshape(width, TILE) for t in (a, b)], axis=1)

    def down_tile(ref):
        parts = [ref[0, c * TILE : (c + 1) * TILE, :] for c in range(width // TILE)]
        return jnp.concatenate(parts, axis=1)

    r = r_all[...]
    s = s_all[...]
    gate = tile_pair(weights[0], weights[1])
    up = tile_pair(weights[2], weights[3])
    d = jnp.concatenate([down_tile(weights[4]), down_tile(weights[5])], axis=0)
    gate_pre = mm(r, gate)
    up_pre = mm(r, up)
    sig = jax.nn.sigmoid(gate_pre)
    silu = gate_pre * sig
    hid = (silu * up_pre).astype(BF16)
    hidden_g = mm_nt(s, d)
    out_acc[...] += mm(hid, d)
    gate_g = (hidden_g * (up_pre * (sig + silu * (1.0 - sig)))).astype(BF16)
    up_g = (hidden_g * silu).astype(BF16)
    both_g = jnp.concatenate([gate_g, up_g], axis=1)
    row_acc[...] += mm_nt(both_g, jnp.concatenate([gate, up], axis=1))
    down_grad = mm_tn(hid, s).astype(BF16)
    gate_grad = mm(r_turned[...], gate_g).astype(BF16)
    up_grad = mm(r_turned[...], up_g).astype(BF16)
    even = core[0] == 0
    for i in range(2):
        tile = 2 * step + i
        for index, value in enumerate((gate_grad, up_grad)):
            start = pl.multiple_of((index * 2 * steps + tile) * chunk_rows, 16)
            place = pl.ds(start, chunk_rows)
            value = value[:, i * TILE : (i + 1) * TILE]
            if halves:
                value = value.reshape(chunks // 2, 2, chunk_rows, TILE)
                for out, flag in zip(grads, (even, jnp.logical_not(even))):
                    out[:, place, :] = jnp.where(flag, value[:, 0], value[:, 1])
            else:
                grads[0][:, place, :] = value.reshape(chunks, chunk_rows, TILE)
    base = 4 * steps * chunk_rows if merged else 0
    for c in range(width // TILE):
        pair = [down_grad[i * TILE : (i + 1) * TILE, c * TILE : (c + 1) * TILE] for i in range(2)]
        place = slice(base + c * TILE, base + (c + 1) * TILE)
        if halves:
            for out, flag in zip(grads, (even, jnp.logical_not(even))):
                out[step, place, :] = jnp.where(flag, pair[0], pair[1])
        else:
            for i in range(2):
                grads[-1][2 * step + i, place, :] = pair[i]

    @pl.when(step == steps - 1)
    def _():
        for k, ref in enumerate(backs):
            ref[0] = out_acc[k * stride : (k + 1) * stride, :].astype(BF16)
            ref[1] = row_acc[k * stride : (k + 1) * stride, :].astype(BF16)


def combine_kernel(experts, owners, local_experts, me, *refs):
    backs = refs[: owners * local_experts]
    (
        residual, normed, grad, tok, routes, dest, mix, wo, small_t,
        mixed_out, prev_out, resg_out, headg_out, delta_out, wo_out, small_out,
        wo_acc, small_acc, second_acc, eo_all, rg_all,
    ) = refs[owners * local_experts :]
    step = pl.program_id(0)
    block, width = residual.shape
    stride = backs[0].shape[1]
    local = owners * stride

    @pl.when(step == 0)
    def _():
        wo_acc[...] = jnp.zeros_like(wo_acc)
        small_acc[...] = jnp.zeros_like(small_acc)
        second_acc[...] = jnp.zeros_like(second_acc)
        for l in range(local_experts):
            for k in range(owners):
                place = slice(k * stride, (k + 1) * stride)
                eo_all[l, place, :] = backs[l * owners + k][0]
                rg_all[l, place, :] = backs[l * owners + k][1]

    slot = iota((1, local), 1)
    owner_slot = ((slot // stride) ^ me[0]) * (local_experts * stride) + slot % stride

    ep = [None, None]
    back = None
    for l in range(local_experts):
        ident = owner_slot + l * stride
        t0 = jnp.where(dest[:, 0:1] == ident, 1.0, 0.0)
        t1 = jnp.where(dest[:, 1:2] == ident, 1.0, 0.0)
        eo = eo_all[l]
        rg = rg_all[l]
        e0 = mm(t0.astype(BF16), eo)
        e1 = mm(t1.astype(BF16), eo)
        b = mm((t0 + t1).astype(BF16), rg)
        ep[0] = e0 if ep[0] is None else ep[0] + e0
        ep[1] = e1 if ep[1] is None else ep[1] + e1
        back = b if back is None else back + b

    res = residual[...]
    n_low = normed[...]
    nf = n_low.astype(F32)
    g_low = grad[...]
    g = g_low.astype(F32)
    gate = [tok[:, 0:1], tok[:, 1:2]]
    mw = [[tok[:, 2:3], tok[:, 3:4]], [tok[:, 4:5], tok[:, 5:6]]]
    scale = tok[:, 6:7]
    vec = [small_t[18:19, :], small_t[19:20, :]]
    along_n = jnp.sum(g * nf, axis=1, keepdims=True)
    along_vec = [jnp.sum(g * vec[c], axis=1, keepdims=True) for c in range(2)]
    gate_g = []
    on_n = 0.0
    sel = [0.0, 0.0]
    copy_weight = 0.0
    for t in range(TOP):
        route = routes[:, t : t + 1]
        is_copy = jnp.where(route == experts + 1, 1.0, 0.0)
        is_const = [jnp.where(route == experts + 2 + c, 1.0, 0.0) for c in range(2)]
        a = is_copy + is_const[0] * mw[0][0] + is_const[1] * mw[1][0]
        b = [is_const[c] * mw[c][1] for c in range(2)]
        gate_g.append(
            jnp.sum(g * ep[t], axis=1, keepdims=True)
            + a * along_n
            + b[0] * along_vec[0]
            + b[1] * along_vec[1]
        )
        on_n = on_n + gate[t] * a
        copy_weight = copy_weight + gate[t] * is_copy
        sel = [sel[c] + gate[t] * is_const[c] for c in range(2)]
    vec_w = [sel[c] * mw[c][1] for c in range(2)]
    mixed_out[...] = (
        res + gate[0] * ep[0] + gate[1] * ep[1] + on_n * nf + vec_w[0] * vec[0] + vec_w[1] * vec[1]
    ).astype(BF16)

    centre = gate[0] * gate_g[0] + gate[1] * gate_g[1]
    pair_g = [gate[t] * (gate_g[t] - centre) for t in range(TOP)]
    lane = iota((block, LANES), 1)
    logit_g = jnp.where(lane == routes[:, 0:1], pair_g[0], 0.0)
    logit_g = logit_g + jnp.where(lane == routes[:, 1:2], pair_g[1], 0.0)
    kinds = prev_out.shape[1]
    prev_out[...] = logit_g[:, 0:kinds]
    for c in range(2):
        w0 = sel[c] * along_n
        w1 = sel[c] * along_vec[c]
        mid = mw[c][0] * w0 + mw[c][1] * w1
        logit_g = jnp.where(lane == kinds + 2 * c, mw[c][0] * (w0 - mid), logit_g)
        logit_g = jnp.where(lane == kinds + 2 * c + 1, mw[c][1] * (w1 - mid), logit_g)
    high, low = split_high_low(logit_g)
    table = small_t[...]
    table = jnp.where(iota(table.shape, 0) < 16, table, 0.0).astype(BF16)
    direct = copy_weight + sel[0] * mw[0][0] + sel[1] * mw[1][0]
    normed_g = back + direct * g + mm(high, table) + mm(low, table)
    gain = small_t[17:18, :]
    scaled = normed_g * gain
    second_acc[...] += jnp.sum(
        (normed_g * res * scale).reshape(block // 8, 8, width), axis=0
    )
    resg = g + scale * scaled - res * (scale * scale * scale) * jnp.mean(
        scaled * res, axis=1, keepdims=True
    )
    resg_out[...] = resg
    attn_g = resg.astype(BF16)
    am = mix[...]
    wo_acc[...] += mm_tn(am, attn_g)
    heads_g = mm_nt(attn_g, wo[0]).astype(BF16)
    headg_out[...] = heads_g
    product = heads_g.astype(F32) * am.astype(F32)
    p_high, p_low = split_high_low(product)
    head_of = jnp.where(
        iota((16, width), 1) // HEAD_DIM == iota((16, width), 0), 1.0, 0.0
    ).astype(BF16)
    delta_out[...] = mm_nt(head_of, p_high) + mm_nt(head_of, p_low)
    small_acc[...] += mm_tn(n_low, high) + mm_tn(n_low, low)
    coefficient = jnp.where(lane == 18, vec_w[0], jnp.where(lane == 19, vec_w[1], 0.0))
    c_high, c_low = split_high_low(coefficient)
    small_acc[...] += mm_tn(g_low, c_high) + mm_tn(g_low, c_low)

    @pl.when(step == pl.num_programs(0) - 1)
    def _():
        wo_out[...] = wo_acc[...].astype(BF16)
        second = jnp.sum(second_acc[...], axis=0, keepdims=True)
        row = iota((LANES, width), 0)
        small_out[...] = small_acc[...] + jnp.where(row == 17, second, 0.0).T


def attend_back_kernel(
    start, me, prefix, q, k, v, grad, lse, delta, cosine, sine, normed, output_g,
    dq_out, dk_out, dv_out, grad_out, bias, dq_acc,
):
    length = q.shape[0]
    step = pl.program_id(0)
    pair = step + start
    block = BLOCK
    lane_all = iota((length, LANES), 1)
    lane = iota((block, LANES), 1)

    @pl.when(step == 0)
    def _():
        limit = jnp.maximum(iota((1, length), 1) + 1, prefix[0])
        bias[...] = jnp.where(iota((length, length), 0) < limit, 0.0, NEG).astype(BF16)
        grad_out[me[0] ^ 3] = output_g[...]

    q_pair = q[...]
    g_pair = grad[...]
    zero = jnp.zeros_like(q_pair)
    q_head = []
    g_head = []
    for head in range(2):
        mine = (lane_all // HEAD_DIM) == head
        q_head.append(jnp.where(mine, q_pair, zero))
        g_head.append(jnp.where(mine, g_pair, zero))
    dq_acc[...] = jnp.zeros_like(dq_acc)

    def one_block(index, carry):
        place = pl.ds(pl.multiple_of(index * block, block), block)
        k_pair = k[place, :]
        v_pair = v[place, :]
        dk = None
        dv = None
        for head in range(2):
            mine = (lane // HEAD_DIM) == head
            k_head = jnp.where(mine, k_pair, jnp.zeros_like(k_pair))
            lse_row = lse[pl.ds(2 * pair + head, 1), :]
            delta_row = delta[pl.ds(2 * pair + head, 1), :]
            scores = mm_nt(k_pair, q_head[head]) + bias[place, :].astype(F32)
            weights = jnp.exp(scores - lse_row)
            probs_g = mm_nt(v_pair, g_head[head])
            one_dv = mm(weights.astype(BF16), g_head[head])
            scores_g = (weights * (probs_g - delta_row)).astype(BF16)
            one_dk = mm(scores_g, q_head[head])
            dq_acc[...] += mm_tn(scores_g, k_head)
            dk = one_dk if dk is None else dk + one_dk
            dv = one_dv if dv is None else dv + one_dv
        cos = cosine[place, :]
        sin = sine[place, :]
        dk_out[place, :] = (dk * cos - half_swap(dk) * sin).astype(BF16)
        dv_out[place, :] = dv.astype(BF16)
        return carry

    lax.fori_loop(0, length // block, one_block, 0)
    dq = dq_acc[...] * (HEAD_DIM**-0.5)
    dq_out[...] = (dq * cosine[...] - half_swap(dq) * sine[...]).astype(BF16)
    columns = pl.ds(pl.multiple_of(step * LANES, LANES), LANES)
    three = mm(normed[...], jnp.concatenate([dq_out[...], dk_out[...], dv_out[...]], axis=1))
    for j in range(3):
        grad_out[me[0] ^ j, :, columns] = three[:, j * LANES : (j + 1) * LANES].astype(BF16)


def project_back_kernel(me, x, *refs):
    parts = refs[:-9]
    resg, wq, wk, wv, small_t, small_g, tok_out, small_out, first_acc = refs[-9:]
    step = pl.program_id(0)
    block, width = x.shape

    @pl.when(step == 0)
    def _():
        first_acc[...] = jnp.zeros_like(first_acc)

    rows = x[...].astype(F32)
    scale = lax.rsqrt(jnp.mean(rows * rows, axis=1, keepdims=True) + EPS)
    normed_g = None
    for j, weight in enumerate((wq, wk, wv)):
        part = jnp.concatenate([p[...] for p in parts[j::3]], axis=1)
        one = mm_nt(part, weight[0])
        normed_g = one if normed_g is None else normed_g + one
    first_acc[...] += jnp.sum(
        (normed_g * rows * scale).reshape(block // 8, 8, width), axis=0
    )
    scaled = normed_g * small_t[16:17, :]
    tok_out[...] = resg[...] + scale * scaled - rows * (scale * scale * scale) * jnp.mean(
        scaled * rows, axis=1, keepdims=True
    )

    @pl.when(step == pl.num_programs(0) - 1)
    def _():
        first = jnp.sum(first_acc[...], axis=0, keepdims=True)
        row = iota((LANES, width), 0)
        small_out[...] = (small_g[...] + jnp.where(row == 16, first, 0.0).T).astype(BF16)


def rotary_tables():
    half = HEAD_DIM // 2
    frequency = 10000.0 ** (-np.arange(half) * 2.0 / HEAD_DIM)
    sign = np.tile(np.repeat([-1.0, 1.0], half), LANES // HEAD_DIM)
    tables = []
    for positions in (np.arange(0, LEN, STRIDE), np.arange(STRIDE)):
        angles = np.tile(positions[:, None] * frequency[None, :], (1, LANES // half))
        tables += [np.cos(angles), np.sin(angles)]
    return [t.astype(np.float32) for t in tables + [sign]]


def body(
    tokens, previous_logits, routes, prefix, slot_order, first_gain, query_weight, key_weight,
    value_weight, output_weight, second_gain, router_weight, constant_mix, constant_vectors,
    gate_weight, up_weight, down_weight, cotangent,
):
    owners = lax.axis_size("expert")
    shards = lax.axis_size("shard")
    local_experts, shard_rows, ff = gate_weight.shape
    experts = local_experts * owners
    count, width = tokens.shape
    kinds = experts + ZC
    capacity = count * TOP // kinds // 8 * 8
    stride = -(-capacity // 16) * 16
    tiles = ff // TILE
    down_rows = down_weight.shape[1]
    me = lax.axis_index("expert").astype(jnp.int32).reshape(1)
    packed_width = width + LANES
    cos_a, sin_a, cos_b, sin_b, sign = (jnp.asarray(t) for t in rotary_tables())
    cos_a, sin_a, cos_b, sin_b, me = lax.optimization_barrier((cos_a, sin_a, cos_b, sin_b, me))
    cos_a, sin_a, cos_b, sin_b = cos_a[:, None], sin_a[:, None], cos_b[None], sin_b[None]
    cosine = (cos_a * cos_b - sin_a * sin_b).reshape(LEN, LANES)
    sine = ((sin_a * cos_b + cos_a * sin_b) * sign).reshape(LEN, LANES)
    struct = jax.ShapeDtypeStruct

    packed = call(
        pack_kernel, "pack", (1,),
        [whole((shard_rows, width))] * 4
        + [whole((1, shard_rows))] * 2
        + [whole((kinds, shard_rows)), whole((4, shard_rows)), whole((2, shard_rows))],
        whole((shard_rows, packed_width)),
        struct((shard_rows, packed_width), BF16),
        scratch=[pltpu.VMEM((LANES, LANES), F32)],
        traffic=1 << 20, prefetch=1,
    )(
        me, query_weight, key_weight, value_weight, output_weight, first_gain[None], second_gain[None],
        router_weight.T, constant_mix.T, constant_vectors,
    )

    def send(part, k):
        return lax.ppermute(part, "expert", [(i, i ^ k) for i in range(owners)])

    def add(a, b):
        return (a.astype(F32) + b.astype(F32)).astype(BF16)

    core = (lax.axis_index("shard") % 2).astype(jnp.int32).reshape(1)
    half = width // 2
    own = lax.all_gather(packed, "shard", axis=0, tiled=True)
    top, low = own[None, :half, :width], own[None, half:, :width]
    top = jnp.concatenate([top, send(top, 1)])
    low = jnp.concatenate([low, send(low, 2)])
    top_in, low_in = send(top, 2), send(low, 1)
    weights = jnp.concatenate([
        jnp.concatenate([top, top_in]),
        jnp.stack([low[0], low_in[0], low[1], low_in[1]]),
    ], axis=1)
    aligned = shard_rows % 16 == 0 and down_rows == TILE
    expert_rows = 2 * tiles * shard_rows + width // TILE * down_rows

    def gather_expert(l):
        if aligned:
            one = call(
                pack_expert_kernel, "pack_expert", (1,),
                [pl.BlockSpec((1,) + w.shape[1:], lambda i: (l, 0, 0))
                 for w in (gate_weight, up_weight, down_weight)],
                whole((expert_rows, TILE)), struct((expert_rows, TILE), BF16), traffic=5 << 20,
            )(gate_weight, up_weight, down_weight)
        else:
            one = jnp.concatenate([
                w[l].reshape(w.shape[1], -1, TILE).transpose(1, 0, 2).reshape(-1, TILE)
                for w in (gate_weight, up_weight, down_weight)
            ])
        full = lax.all_gather(one, "shard", axis=0, tiled=True)
        full = full.reshape(shards, expert_rows, TILE)
        if aligned:
            return full, full
        split = 2 * tiles * shard_rows
        gate_up = full[:, :split].reshape(shards, 2 * tiles, shard_rows, TILE)
        down = full[:, split:].reshape(shards, width // TILE, down_rows, TILE)
        down = down.transpose(1, 0, 2, 3).reshape(width // TILE, tiles, TILE, TILE)
        return (
            gate_up.transpose(1, 0, 2, 3).reshape(1, -1, TILE),
            down.transpose(1, 0, 2, 3).reshape(tiles, width, TILE),
        )

    expert_full = [gather_expert(l) for l in range(local_experts)]

    dest_col, dest_row = call(
        functools.partial(slots_kernel, experts, capacity, stride), "slots", (1,),
        [whole((count, TOP)), whole((1, count)), whole((count, 1))],
        [whole((count, LANES)), whole((8, count))],
        [struct((count, LANES), jnp.int32), struct((8, count), jnp.int32)],
        flops=2 * 3 * count * count * LANES, traffic=1 << 20,
    )(routes, slot_order, slot_order.reshape(count, 1))

    steps = count // BLOCK
    weight_block = [
        pl.BlockSpec((1, width, width), lambda i, me, *rest, j=j: (me[0] ^ j, 0, 0))
        for j in range(4)
    ]
    output_block = weight_block.pop()
    small_block = pl.BlockSpec((width, LANES), lambda i, *rest: (0, width // LANES))
    wide = rows_of(BLOCK, width)
    table = rows_of(BLOCK, LANES)
    act = struct((count, width), BF16)
    queries, keys, values, normed_one, small_t = call(
        project_kernel, "project", (steps,),
        [wide] + weight_block + [small_block, table, table],
        [wide] * 3 + [pl.BlockSpec((width, BLOCK), lambda i, *rest: (0, i)), whole((LANES, width))],
        [act] * 3 + [struct((width, count), BF16), struct((LANES, width), F32)],
        flops=6 * count * width * width, traffic=12 << 20, prefetch=1,
    )(me, tokens, weights, weights, weights, own, cosine, sine)

    attn_mix, lse, residual, normed_two, tok = call(
        attend_kernel, "attend", (steps,),
        [wide, whole((count, width)), whole((count, width)), wide, output_block,
         small_block, whole((LANES, width)), rows_of(BLOCK, kinds), rows_of(BLOCK, TOP)],
        [wide, pl.BlockSpec((16, BLOCK), lambda i, *rest: (0, i)), wide, wide, table],
        [act, struct((16, count), F32), struct((count, width), F32), act,
         struct((count, LANES), F32)],
        scratch=[pltpu.VMEM((BLOCK, count), F32), pltpu.VMEM((BLOCK, width), BF16),
                 pltpu.VMEM((BLOCK, LANES), F32)],
        flops=30 << 30, traffic=16 << 20, trans=HEADS * count * count, prefetch=2,
    )(me, prefix, queries, keys, values, tokens, weights, own, small_t,
      previous_logits, routes)

    def exchange(parts):
        return [parts[0]] + [
            lax.ppermute(part, "expert", [(i, i ^ k) for i in range(owners)])
            for k, part in list(enumerate(parts))[1:]
        ]

    pair = whole((2, stride, width))
    pair_shape = struct((2, stride, width), BF16)

    def dispatch(l):
        parts = call(
            functools.partial(dispatch_kernel, local_experts, l), "dispatch", (owners,),
            [whole((count, width)), whole((count, width)), whole((count, LANES)),
             whole((count, TOP)), whole((8, count))],
            [pair] * owners, [pair_shape] * owners,
            scratch=[pltpu.VMEM((count, LANES), BF16)],
            flops=4 * owners * stride * count * width, traffic=6 << 20, prefetch=1,
        )(me, normed_two, cotangent, tok, routes, dest_row)
        return parts

    dispatched = [dispatch(l) for l in range(local_experts)]
    received = [exchange(parts) for parts in dispatched]

    chunks, chunk_rows = (shards, shard_rows) if aligned else (1, width)
    local = owners * stride

    def run_expert(l, rows, after):
        gate_up, down = expert_full[l]
        weights = [
            pl.BlockSpec((chunks, chunk_rows, TILE), lambda f, *rest, j=j: (0, j // 2 * tiles + 2 * f + j % 2, 0))
            for j in range(4)
        ] + [
            pl.BlockSpec((1, width, TILE), lambda f, *rest, j=j: (2 * f + j, 2 if aligned else 0, 0))
            for j in range(2)
        ]
        halves = aligned and l + 1 == local_experts
        if halves:
            grad_shapes = [(shards // 2, expert_rows, TILE)] * 2
        elif aligned:
            grad_shapes = [(shards, expert_rows, TILE)]
        else:
            grad_shapes = [(1, 2 * tiles * width, TILE), (tiles, width, TILE)]
        outs = call(
            functools.partial(expert_kernel, owners, aligned, halves), "expert", (tiles // 2,),
            [pair] * owners + weights,
            [pair] * owners + [whole(g) for g in grad_shapes],
            [pair_shape] * owners + [struct(g, BF16) for g in grad_shapes],
            scratch=[pltpu.VMEM((local, width), BF16)] * 2 + [pltpu.VMEM((width, local), BF16)]
            + [pltpu.VMEM((local, width), F32)] * 2,
            flops=16 * local * width * ff, traffic=24 << 20, trans=local * ff, prefetch=1,
        )(core, *rows, gate_up, gate_up, gate_up, gate_up, down, down)
        grads = outs[owners:]
        if halves:
            keep, give = grads
        elif aligned:
            grad = grads[0]
        else:
            gate_up_g = grads[0].reshape(2 * tiles, shards, shard_rows, TILE).transpose(1, 0, 2, 3)
            down_g = grads[1].reshape(tiles, width // TILE, TILE, TILE).transpose(1, 0, 2, 3)
            down_g = down_g.reshape(width // TILE, shards, down_rows, TILE).transpose(1, 0, 2, 3)
            grad = jnp.concatenate(
                [gate_up_g.reshape(shards, -1, TILE), down_g.reshape(shards, -1, TILE)], axis=1
            )
        if halves:
            grad = add(keep, lax.ppermute(give, "shard", [(i, i ^ 1) for i in range(shards)]))
        grad, after = lax.optimization_barrier((grad, after))
        return outs[:owners], grad.reshape(-1, TILE), after

    def reduce_expert(grad):
        return lax.psum_scatter(
            grad, "shard", scatter_dimension=0, tiled=True,
            axis_index_groups=(
                None if len(grad) == shards * expert_rows
                else [list(range(c, shards, 2)) for c in range(2)]
            ),
        )

    returned = []
    expert_sums = []
    for l in range(local_experts):
        rows, ahead = lax.optimization_barrier((received[l], returned or dispatched[-1]))
        returned = ahead if returned else returned
        back, grad, received[l + 1 :] = run_expert(l, rows, received[l + 1 :])
        back = exchange(back)
        if l + 1 == local_experts:
            back, grad = lax.optimization_barrier((back, grad))
        returned = returned + back
        expert_sums.append(reduce_expert(grad))

    mixed, previous_grad, residual_grad, heads_grad, delta, output_grad, small_grad = call(
        functools.partial(combine_kernel, experts, owners, local_experts), "combine", (steps,),
        [pair] * len(returned)
        + [wide, wide, wide, table, rows_of(BLOCK, TOP), table, wide, output_block,
           whole((LANES, width))],
        [wide, rows_of(BLOCK, kinds), wide, wide, pl.BlockSpec((16, BLOCK), lambda i, *rest: (0, i)),
         whole((width, width)), whole((width, LANES))],
        [act, struct((count, kinds), F32), struct((count, width), F32), act,
         struct((16, count), F32), struct((width, width), BF16), struct((width, LANES), F32)],
        scratch=[pltpu.VMEM((width, width), F32), pltpu.VMEM((width, LANES), F32),
                 pltpu.VMEM((8, width), F32)]
        + [pltpu.VMEM((local_experts, local, width), BF16)] * 2,
        flops=6 * count * 2 * local * width + 4 * count * width * width, traffic=24 << 20, prefetch=1,
    )(me, *returned, residual, normed_two, cotangent, tok,
      routes, dest_col, attn_mix, weights, small_t)

    def first_turn(grad):
        return send(grad[1::2, :half], 1), send(grad[2:, half:], 2)

    def second_turn(grad, came):
        top, low = add(grad[0::2, :half], came[0]), add(grad[:2, half:], came[1])
        return (top[0], low[0]), (send(top[1], 2), send(low[1], 1))

    def join(mine, came):
        return jnp.concatenate([add(a, b) for a, b in zip(mine, came)], axis=0)

    pairs = width // LANES // 2
    columns = pairs * LANES
    half_out = pl.BlockSpec((count, LANES), lambda i, *rest: (0, i))
    parts = []
    dense_grads = []
    moved = ()
    for start in (0, pairs):
        pair_block = pl.BlockSpec((count, LANES), lambda i, *rest, start=start: (0, i + start))
        *three, dense_grad = call(
            functools.partial(attend_back_kernel, start), "attend_back", (pairs,),
            [pair_block] * 4
            + [whole((16, count))] * 2
            + [whole((count, LANES))] * 2
            + [whole((width, count)),
               pl.BlockSpec((width, columns), lambda i, *rest, start=start: (0, start // pairs))],
            [half_out] * 3 + [whole((owners, width, columns))],
            [struct((count, columns), BF16)] * 3 + [struct((owners, width, columns), BF16)],
            scratch=[pltpu.VMEM((count, count), BF16), pltpu.VMEM((count, LANES), F32)],
            flops=30 << 30, traffic=6 << 20, trans=HEADS // 2 * count * count, prefetch=2,
        )(me, prefix, queries, keys, values, heads_grad, lse, delta, cosine, sine, normed_one,
          output_grad)
        if start:
            three, moved, expert_sums[0] = lax.optimization_barrier((three, moved, expert_sums[0]))
        parts += three
        dense_grads.append(dense_grad)
        if start == 0:
            moved = first_turn(dense_grad)
    mine_a, moved_a = second_turn(dense_grads[0], moved)
    moved_b = first_turn(dense_grads[1])

    half_wide = rows_of(BLOCK, columns)
    tokens_grad, small_grad = call(
        project_back_kernel, "project_back", (steps,),
        [wide] + [half_wide] * 6 + [wide] + weight_block
        + [whole((LANES, width)), whole((width, LANES))],
        [wide, whole((width, LANES))],
        [struct((count, width), F32), struct((width, LANES), BF16)],
        scratch=[pltpu.VMEM((8, width), F32)],
        flops=6 * count * width * width, traffic=18 << 20, prefetch=1,
    )(me, tokens, *parts, residual_grad, weights, weights, weights, small_t, small_grad)
    small_grad, moved_a, moved_b = lax.optimization_barrier((small_grad, moved_a, moved_b))
    mine_b, moved_b = second_turn(dense_grads[1], moved_b)
    quarters = [join(mine_a, moved_a), join(mine_b, moved_b)]
    quarter = jnp.concatenate(quarters + [small_grad], axis=1)
    quarter, expert_sums = lax.optimization_barrier((quarter, expert_sums))
    quarter = lax.psum_scatter(quarter, "shard", scatter_dimension=0, tiled=True)
    gathered = jnp.stack([quarter] + [send(quarter, k) for k in range(1, owners)]).astype(F32)
    dense = [
        lax.dynamic_index_in_dim(gathered[:, :, :width], me[0] ^ j, keepdims=False)
        for j in range(4)
    ]
    small = jnp.sum(gathered[:, :, width:], axis=0)
    if aligned:
        out_shapes = [w.shape for w in (gate_weight, up_weight, down_weight)]
        gate_sum, up_sum, down_sum = call(
            unpack_expert_kernel, "unpack", (1,),
            [whole((expert_rows, TILE))] * local_experts,
            [whole(o) for o in out_shapes], [struct(o, F32) for o in out_shapes],
            traffic=8 << 20,
        )(*expert_sums)
    else:
        split = 2 * tiles * shard_rows
        total = jnp.stack(expert_sums).astype(F32)
        gate_sum, up_sum = (
            part.reshape(local_experts, tiles, shard_rows, TILE).transpose(0, 2, 1, 3).reshape(
                local_experts, shard_rows, ff
            )
            for part in (total[:, : split // 2], total[:, split // 2 : split])
        )
        down_sum = total[:, split:].reshape(local_experts, width // TILE, down_rows, TILE)
        down_sum = down_sum.transpose(0, 2, 1, 3).reshape(local_experts, down_rows, width)
    return (
        mixed,
        tokens_grad,
        previous_grad,
        dense[0],
        dense[1],
        dense[2],
        dense[3],
        small[:, 0:kinds],
        small[:, kinds : kinds + 4],
        small[:, 18:20].T,
        small[:, 16],
        small[:, 17],
        gate_sum,
        up_sum,
        down_sum,
    )


def solution(mesh):
    rows = P(("expert", "shard"), None)
    expert = P("expert", "shard", None)
    flat = P("shard", None)
    return jax.shard_map(
        body,
        mesh=mesh,
        in_specs=(
            rows, rows, rows, P(("expert", "shard")), rows, P("shard"), flat, flat, flat, flat,
            P("shard"), flat, flat, P(None, "shard"), expert, expert, expert, rows,
        ),
        out_specs=(
            rows, rows, rows, flat, flat, flat, flat, flat, flat, P(None, "shard"), P("shard"),
            P("shard"), expert, expert, expert,
        ),
        check_vma=False,
    )
```

```python
import functools
import numpy as np
import jax
import jax.numpy as jnp
from jax import lax
from jax.experimental import pallas as pl
from jax.experimental.pallas import tpu as pltpu
from jax.sharding import PartitionSpec as P

HEADS = 12
HEAD_DIM = 64
ZC = 4
TOP = 2
LEN = 1024
EPS = 1e-05
NEG = -1e30
LANES = 128
BLOCK = 256
TILE = 256
STRIDE = 32
F32 = jnp.float32
BF16 = jnp.bfloat16
VMEM_LIMIT = 56 << 20


def call(body, name, grid, in_specs, out_specs, out_shape, scratch=(), flops=0, traffic=0, trans=0, prefetch=0):
    return pl.pallas_call(
        body,
        name=name,
        grid_spec=pltpu.PrefetchScalarGridSpec(
            num_scalar_prefetch=prefetch,
            grid=grid,
            in_specs=in_specs,
            out_specs=out_specs,
            scratch_shapes=scratch,
        ),
        out_shape=out_shape,
        compiler_params=pltpu.CompilerParams(
            dimension_semantics=("arbitrary",) * len(grid), vmem_limit_bytes=VMEM_LIMIT
        ),
        cost_estimate=pl.CostEstimate(flops=flops, transcendentals=trans, bytes_accessed=traffic),
    )


def mm(a, b):
    return lax.dot_general(a, b, (((1,), (0,)), ((), ())), preferred_element_type=F32)


def mm_nt(a, b):
    return lax.dot_general(a, b, (((1,), (1,)), ((), ())), preferred_element_type=F32)


def mm_tn(a, b):
    return lax.dot_general(a, b, (((0,), (0,)), ((), ())), preferred_element_type=F32)


def iota(shape, axis):
    return lax.broadcasted_iota(jnp.int32, shape, axis)


def whole(shape):
    return pl.BlockSpec(shape, lambda *idx: (0,) * len(shape))


def rows_of(block, width):
    return pl.BlockSpec((block, width), lambda i, *rest: (i, 0))


def split_high_low(values):
    high = values.astype(BF16)
    low = (values - high.astype(F32)).astype(BF16)
    return high, low


def pack_kernel(me, q, k, v, o, gain1, gain2, router, mix, vectors, out, scratch):
    rows, width = q.shape
    for j, weight in enumerate((q, k, v, o)):

        @pl.when(me[0] == j)
        def _():
            out[:, 0:width] = weight[...]

    scratch[...] = jnp.zeros_like(scratch)
    n_router = router.shape[0]
    scratch[0:n_router, 0:rows] = router[...].astype(F32)
    scratch[n_router : n_router + mix.shape[0], 0:rows] = mix[...].astype(F32)
    scratch[16:17, 0:rows] = gain1[...].astype(F32)
    scratch[17:18, 0:rows] = gain2[...].astype(F32)
    scratch[18:20, 0:rows] = vectors[...].astype(F32)
    out[:, width : width + LANES] = scratch[...].T[0:rows, :].astype(BF16)


def slots_kernel(experts, capacity, stride, routes, order_row, order_col, dest_col, dest_row):
    tokens = routes.shape[0]
    r0 = routes[:, 0:1]
    r1 = routes[:, 1:2]
    lane = iota((tokens, LANES), 1)
    hot = jnp.where((lane == r0) | (lane == r1), 1.0, 0.0)
    hot = jnp.where(lane < experts, hot, 0.0).astype(BF16)
    row = iota((tokens, tokens), 0)
    col = iota((tokens, tokens), 1)
    to_turn = jnp.where(order_col[...] == col, 1.0, 0.0).astype(BF16)
    hot_turn = mm(to_turn, hot).astype(BF16)
    earlier = mm(jnp.where(col < row, 1.0, 0.0).astype(BF16), hot_turn)
    earlier = jnp.minimum(earlier, 255.0).astype(BF16)
    to_token = jnp.where(order_row[...] == row, 1.0, 0.0).astype(BF16)
    position = mm(to_token, earlier)
    p0 = jnp.sum(jnp.where(lane == r0, position, 0.0), axis=1, keepdims=True)
    p1 = jnp.sum(jnp.where(lane == r1, position, 0.0), axis=1, keepdims=True)
    d0 = jnp.where((r0 < experts) & (p0 < capacity), r0.astype(F32) * stride + p0, -1.0)
    d1 = jnp.where((r1 < experts) & (p1 < capacity), r1.astype(F32) * stride + p1, -1.0)
    both = jnp.where(lane == 0, d0, jnp.where(lane == 1, d1, 0.0))
    dest_col[...] = both.astype(jnp.int32)
    dest_row[...] = both.T[0:8, :].astype(jnp.int32)


def half_swap(values):
    lane = iota(values.shape, 1) % HEAD_DIM
    half = HEAD_DIM // 2
    return jnp.where(
        lane < half, pltpu.roll(values, LANES - half, 1), pltpu.roll(values, half, 1)
    )


def project_kernel(me, x, wq, wk, wv, small, cosine, sine, q_out, k_out, v_out, n_out, small_t):
    @pl.when(pl.program_id(0) == 0)
    def _():
        small_t[...] = small[...].astype(F32).T

    width = x.shape[1]
    rows = x[...].astype(F32)
    scale = lax.rsqrt(jnp.mean(rows * rows, axis=1, keepdims=True) + EPS)
    normed = (rows * scale * small_t[16:17, :]).astype(BF16)
    n_out[...] = normed.T
    cos = cosine[...]
    sin = sine[...]
    for weight, out, factor in ((wq, q_out, HEAD_DIM**-0.5), (wk, k_out, None)):
        lin = mm(normed, weight[0])
        for c in range(width // LANES):
            part = lin[:, c * LANES : (c + 1) * LANES]
            turned = part * cos + half_swap(part) * sin
            if factor is not None:
                turned = turned * factor
            out[:, c * LANES : (c + 1) * LANES] = turned.astype(BF16)
    v_out[...] = mm(normed, wv[0]).astype(BF16)


def attend_kernel(
    me, prefix, q, k, v, x, wo, small, small_t, prev, routes,
    mix_out, lse_out, res_out, n_out, tok_out, bias, mixed, lse,
):
    block, width = q.shape
    length = k.shape[0]
    start = pl.program_id(0) * block
    limit = jnp.maximum(start + iota((block, 1), 0) + 1, prefix[0])
    bias[...] = jnp.where(iota((block, length), 1) < limit, 0.0, NEG)
    lane = iota((block, LANES), 1)
    first = lane < HEAD_DIM
    lse[...] = jnp.zeros_like(lse)

    def one_pair(pair, carry):
        columns = pl.ds(pl.multiple_of(pair * LANES, LANES), LANES)
        q_pair = q[:, columns]
        k_pair = k[:, columns]
        v_pair = v[:, columns]
        outs = []
        for head in range(2):
            mine = first if head == 0 else jnp.logical_not(first)
            q_head = jnp.where(mine, q_pair, jnp.zeros_like(q_pair))
            scores = mm_nt(q_head, k_pair) + bias[...]
            top = jnp.max(scores, axis=1, keepdims=True)
            weights = jnp.exp(scores - top)
            total = jnp.sum(weights, axis=1, keepdims=True)
            outs.append(mm(weights.astype(BF16), v_pair) / total)
            lse[...] = jnp.where(lane == 2 * pair + head, top + jnp.log(total), lse[...])
        mixed[:, columns] = jnp.where(first, outs[0], outs[1]).astype(BF16)
        return carry

    lax.fori_loop(0, width // LANES, one_pair, 0)
    mix_out[...] = mixed[...]
    lse_out[...] = lse[...].T[0:16, :]
    residual = x[...].astype(F32) + mm(mixed[...], wo[0])
    res_out[...] = residual
    scale = lax.rsqrt(jnp.mean(residual * residual, axis=1, keepdims=True) + EPS)
    normed = (residual * scale * small_t[17:18, :]).astype(BF16)
    n_out[...] = normed
    lin = mm(normed, small[...])
    kinds = prev.shape[1]
    logits = lin[:, 0:kinds] + prev[...]
    kind = iota((block, kinds), 1)
    c0 = jnp.sum(jnp.where(kind == routes[:, 0:1], logits, 0.0), axis=1, keepdims=True)
    c1 = jnp.sum(jnp.where(kind == routes[:, 1:2], logits, 0.0), axis=1, keepdims=True)

    def pair_softmax(a, b):
        top = jnp.maximum(a, b)
        ea = jnp.exp(a - top)
        eb = jnp.exp(b - top)
        total = ea + eb
        return ea / total, eb / total

    g0, g1 = pair_softmax(c0, c1)
    m00, m01 = pair_softmax(lin[:, kinds : kinds + 1], lin[:, kinds + 1 : kinds + 2])
    m10, m11 = pair_softmax(lin[:, kinds + 2 : kinds + 3], lin[:, kinds + 3 : kinds + 4])
    packed = jnp.zeros((block, LANES), F32)
    for index, column in enumerate((g0, g1, m00, m01, m10, m11, scale)):
        packed = jnp.where(lane == index, column, packed)
    tok_out[...] = packed


def pack_expert_kernel(gate, up, down, out):
    rows, ff = gate.shape[1:]
    down_rows, width = down.shape[1:]
    tiles = ff // TILE
    for index, ref in enumerate((gate, up)):
        for f in range(tiles):
            start = (index * tiles + f) * rows
            out[start : start + rows, :] = ref[0, :, f * TILE : (f + 1) * TILE]
    base = 2 * tiles * rows
    for c in range(width // TILE):
        out[base + c * down_rows : base + (c + 1) * down_rows, :] = down[
            0, :, c * TILE : (c + 1) * TILE
        ]


def unpack_expert_kernel(*refs):
    gate, up, down = refs[-3:]
    rows, ff = gate.shape[1:]
    down_rows, width = down.shape[1:]
    tiles = ff // TILE
    base = 2 * tiles * rows
    for l, ref in enumerate(refs[:-3]):
        for index, out in enumerate((gate, up)):
            for f in range(tiles):
                start = (index * tiles + f) * rows
                out[l, :, f * TILE : (f + 1) * TILE] = ref[start : start + rows, :].astype(F32)
        for c in range(width // TILE):
            down[l, :, c * TILE : (c + 1) * TILE] = ref[
                base + c * down_rows : base + (c + 1) * down_rows, :
            ].astype(F32)


def dispatch_kernel(local_experts, l, me, normed, grad, tok, routes, dest_row, *rest):
    outs, gates = rest[:-1], rest[-1]
    step = pl.program_id(0)
    tokens = normed.shape[0]
    stride = outs[0].shape[1]
    expert = (me[0] ^ step) * local_experts + l

    @pl.when(step == 0)
    def _():
        lane = iota((tokens, LANES), 1)
        kind = lane % HEAD_DIM
        value = jnp.where(kind == routes[:, 0:1], tok[:, 0:1], 0.0)
        value = value + jnp.where(kind == routes[:, 1:2], tok[:, 1:2], 0.0)
        high = value.astype(BF16).astype(F32)
        gates[...] = jnp.where(lane < HEAD_DIM, high, value - high).astype(BF16)

    slot = expert * stride + iota((stride, tokens), 0)
    hit = (dest_row[0:1, :] == slot) | (dest_row[1:2, :] == slot)
    take = jnp.where(hit, 1.0, 0.0).astype(BF16)
    row = mm(take, normed[...]).astype(BF16)
    slot_gates = mm(take, gates[...])
    mine = iota((stride, LANES), 1) % HEAD_DIM == expert
    slot_gate = jnp.sum(jnp.where(mine, slot_gates, 0.0), axis=1, keepdims=True)
    slot_g = (mm(take, grad[...]) * slot_gate).astype(BF16)
    for k, out in enumerate(outs):

        @pl.when(step == k)
        def _():
            out[0] = row
            out[1] = slot_g


def expert_kernel(owners, merged, halves, core, *refs):
    sent = refs[:owners]
    weights = refs[owners : owners + 6]
    backs = refs[owners + 6 : 2 * owners + 6]
    grads = refs[2 * owners + 6 : -5]
    r_all, s_all, r_turned, out_acc, row_acc = refs[-5:]
    step = pl.program_id(0)
    steps = pl.num_programs(0)
    stride, width = sent[0].shape[1:]
    chunks, chunk_rows = weights[0].shape[:2]

    @pl.when(step == 0)
    def _():
        for k, ref in enumerate(sent):
            r_all[k * stride : (k + 1) * stride, :] = ref[0]
            s_all[k * stride : (k + 1) * stride, :] = ref[1]
        r_turned[...] = r_all[...].T
        out_acc[...] = jnp.zeros_like(out_acc)
        row_acc[...] = jnp.zeros_like(row_acc)

    def tile_pair(a, b):
        return jnp.concatenate([t[...].reshape(width, TILE) for t in (a, b)], axis=1)

    def down_tile(ref):
        parts = [ref[0, c * TILE : (c + 1) * TILE, :] for c in range(width // TILE)]
        return jnp.concatenate(parts, axis=1)

    r = r_all[...]
    s = s_all[...]
    gate = tile_pair(weights[0], weights[1])
    up = tile_pair(weights[2], weights[3])
    d = jnp.concatenate([down_tile(weights[4]), down_tile(weights[5])], axis=0)
    gate_pre = mm(r, gate)
    up_pre = mm(r, up)
    sig = jax.nn.sigmoid(gate_pre)
    silu = gate_pre * sig
    hid = (silu * up_pre).astype(BF16)
    hidden_g = mm_nt(s, d)
    out_acc[...] += mm(hid, d)
    gate_g = (hidden_g * (up_pre * (sig + silu * (1.0 - sig)))).astype(BF16)
    up_g = (hidden_g * silu).astype(BF16)
    both_g = jnp.concatenate([gate_g, up_g], axis=1)
    row_acc[...] += mm_nt(both_g, jnp.concatenate([gate, up], axis=1))
    down_grad = mm_tn(hid, s).astype(BF16)
    gate_grad = mm(r_turned[...], gate_g).astype(BF16)
    up_grad = mm(r_turned[...], up_g).astype(BF16)
    even = core[0] == 0
    for i in range(2):
        tile = 2 * step + i
        for index, value in enumerate((gate_grad, up_grad)):
            start = pl.multiple_of((index * 2 * steps + tile) * chunk_rows, 16)
            place = pl.ds(start, chunk_rows)
            value = value[:, i * TILE : (i + 1) * TILE]
            if halves:
                value = value.reshape(chunks // 2, 2, chunk_rows, TILE)
                for out, flag in zip(grads, (even, jnp.logical_not(even))):
                    out[:, place, :] = jnp.where(flag, value[:, 0], value[:, 1])
            else:
                grads[0][:, place, :] = value.reshape(chunks, chunk_rows, TILE)
    base = 4 * steps * chunk_rows if merged else 0
    for c in range(width // TILE):
        pair = [down_grad[i * TILE : (i + 1) * TILE, c * TILE : (c + 1) * TILE] for i in range(2)]
        place = slice(base + c * TILE, base + (c + 1) * TILE)
        if halves:
            for out, flag in zip(grads, (even, jnp.logical_not(even))):
                out[step, place, :] = jnp.where(flag, pair[0], pair[1])
        else:
            for i in range(2):
                grads[-1][2 * step + i, place, :] = pair[i]

    @pl.when(step == steps - 1)
    def _():
        for k, ref in enumerate(backs):
            ref[0] = out_acc[k * stride : (k + 1) * stride, :].astype(BF16)
            ref[1] = row_acc[k * stride : (k + 1) * stride, :].astype(BF16)


def combine_kernel(experts, owners, local_experts, me, *refs):
    backs = refs[: owners * local_experts]
    (
        residual, normed, grad, tok, routes, dest, mix, wo, small_t,
        mixed_out, prev_out, resg_out, headg_out, delta_out, wo_out, small_out,
        wo_acc, small_acc, second_acc, eo_all, rg_all,
    ) = refs[owners * local_experts :]
    step = pl.program_id(0)
    block, width = residual.shape
    stride = backs[0].shape[1]
    local = owners * stride

    @pl.when(step == 0)
    def _():
        wo_acc[...] = jnp.zeros_like(wo_acc)
        small_acc[...] = jnp.zeros_like(small_acc)
        second_acc[...] = jnp.zeros_like(second_acc)
        for l in range(local_experts):
            for k in range(owners):
                place = slice(k * stride, (k + 1) * stride)
                eo_all[l, place, :] = backs[l * owners + k][0]
                rg_all[l, place, :] = backs[l * owners + k][1]

    slot = iota((1, local), 1)
    owner_slot = ((slot // stride) ^ me[0]) * (local_experts * stride) + slot % stride

    ep = [None, None]
    back = None
    for l in range(local_experts):
        ident = owner_slot + l * stride
        t0 = jnp.where(dest[:, 0:1] == ident, 1.0, 0.0)
        t1 = jnp.where(dest[:, 1:2] == ident, 1.0, 0.0)
        eo = eo_all[l]
        rg = rg_all[l]
        e0 = mm(t0.astype(BF16), eo)
        e1 = mm(t1.astype(BF16), eo)
        b = mm((t0 + t1).astype(BF16), rg)
        ep[0] = e0 if ep[0] is None else ep[0] + e0
        ep[1] = e1 if ep[1] is None else ep[1] + e1
        back = b if back is None else back + b

    res = residual[...]
    n_low = normed[...]
    nf = n_low.astype(F32)
    g_low = grad[...]
    g = g_low.astype(F32)
    gate = [tok[:, 0:1], tok[:, 1:2]]
    mw = [[tok[:, 2:3], tok[:, 3:4]], [tok[:, 4:5], tok[:, 5:6]]]
    scale = tok[:, 6:7]
    vec = [small_t[18:19, :], small_t[19:20, :]]
    along_n = jnp.sum(g * nf, axis=1, keepdims=True)
    along_vec = [jnp.sum(g * vec[c], axis=1, keepdims=True) for c in range(2)]
    gate_g = []
    on_n = 0.0
    sel = [0.0, 0.0]
    copy_weight = 0.0
    for t in range(TOP):
        route = routes[:, t : t + 1]
        is_copy = jnp.where(route == experts + 1, 1.0, 0.0)
        is_const = [jnp.where(route == experts + 2 + c, 1.0, 0.0) for c in range(2)]
        a = is_copy + is_const[0] * mw[0][0] + is_const[1] * mw[1][0]
        b = [is_const[c] * mw[c][1] for c in range(2)]
        gate_g.append(
            jnp.sum(g * ep[t], axis=1, keepdims=True)
            + a * along_n
            + b[0] * along_vec[0]
            + b[1] * along_vec[1]
        )
        on_n = on_n + gate[t] * a
        copy_weight = copy_weight + gate[t] * is_copy
        sel = [sel[c] + gate[t] * is_const[c] for c in range(2)]
    vec_w = [sel[c] * mw[c][1] for c in range(2)]
    mixed_out[...] = (
        res + gate[0] * ep[0] + gate[1] * ep[1] + on_n * nf + vec_w[0] * vec[0] + vec_w[1] * vec[1]
    ).astype(BF16)

    centre = gate[0] * gate_g[0] + gate[1] * gate_g[1]
    pair_g = [gate[t] * (gate_g[t] - centre) for t in range(TOP)]
    lane = iota((block, LANES), 1)
    logit_g = jnp.where(lane == routes[:, 0:1], pair_g[0], 0.0)
    logit_g = logit_g + jnp.where(lane == routes[:, 1:2], pair_g[1], 0.0)
    kinds = prev_out.shape[1]
    prev_out[...] = logit_g[:, 0:kinds]
    for c in range(2):
        w0 = sel[c] * along_n
        w1 = sel[c] * along_vec[c]
        mid = mw[c][0] * w0 + mw[c][1] * w1
        logit_g = jnp.where(lane == kinds + 2 * c, mw[c][0] * (w0 - mid), logit_g)
        logit_g = jnp.where(lane == kinds + 2 * c + 1, mw[c][1] * (w1 - mid), logit_g)
    high, low = split_high_low(logit_g)
    table = small_t[...]
    table = jnp.where(iota(table.shape, 0) < 16, table, 0.0).astype(BF16)
    direct = copy_weight + sel[0] * mw[0][0] + sel[1] * mw[1][0]
    normed_g = back + direct * g + mm(high, table) + mm(low, table)
    gain = small_t[17:18, :]
    scaled = normed_g * gain
    second_acc[...] += jnp.sum(
        (normed_g * res * scale).reshape(block // 8, 8, width), axis=0
    )
    resg = g + scale * scaled - res * (scale * scale * scale) * jnp.mean(
        scaled * res, axis=1, keepdims=True
    )
    resg_out[...] = resg
    attn_g = resg.astype(BF16)
    am = mix[...]
    wo_acc[...] += mm_tn(am, attn_g)
    heads_g = mm_nt(attn_g, wo[0]).astype(BF16)
    headg_out[...] = heads_g
    product = heads_g.astype(F32) * am.astype(F32)
    p_high, p_low = split_high_low(product)
    head_of = jnp.where(
        iota((16, width), 1) // HEAD_DIM == iota((16, width), 0), 1.0, 0.0
    ).astype(BF16)
    delta_out[...] = mm_nt(head_of, p_high) + mm_nt(head_of, p_low)
    small_acc[...] += mm_tn(n_low, high) + mm_tn(n_low, low)
    coefficient = jnp.where(lane == 18, vec_w[0], jnp.where(lane == 19, vec_w[1], 0.0))
    c_high, c_low = split_high_low(coefficient)
    small_acc[...] += mm_tn(g_low, c_high) + mm_tn(g_low, c_low)

    @pl.when(step == pl.num_programs(0) - 1)
    def _():
        wo_out[...] = wo_acc[...].astype(BF16)
        second = jnp.sum(second_acc[...], axis=0, keepdims=True)
        row = iota((LANES, width), 0)
        small_out[...] = small_acc[...] + jnp.where(row == 17, second, 0.0).T


def attend_back_kernel(
    start, me, prefix, q, k, v, grad, lse, delta, cosine, sine, normed, output_g,
    dq_out, dk_out, dv_out, grad_out, bias, dq_acc,
):
    length = q.shape[0]
    step = pl.program_id(0)
    pair = step + start
    block = BLOCK
    lane_all = iota((length, LANES), 1)
    lane = iota((block, LANES), 1)

    @pl.when(step == 0)
    def _():
        limit = jnp.maximum(iota((1, length), 1) + 1, prefix[0])
        bias[...] = jnp.where(iota((length, length), 0) < limit, 0.0, NEG).astype(BF16)
        grad_out[me[0] ^ 3] = output_g[...]

    q_pair = q[...]
    g_pair = grad[...]
    zero = jnp.zeros_like(q_pair)
    q_head = []
    g_head = []
    for head in range(2):
        mine = (lane_all // HEAD_DIM) == head
        q_head.append(jnp.where(mine, q_pair, zero))
        g_head.append(jnp.where(mine, g_pair, zero))
    dq_acc[...] = jnp.zeros_like(dq_acc)

    def one_block(index, carry):
        place = pl.ds(pl.multiple_of(index * block, block), block)
        k_pair = k[place, :]
        v_pair = v[place, :]
        dk = None
        dv = None
        for head in range(2):
            mine = (lane // HEAD_DIM) == head
            k_head = jnp.where(mine, k_pair, jnp.zeros_like(k_pair))
            lse_row = lse[pl.ds(2 * pair + head, 1), :]
            delta_row = delta[pl.ds(2 * pair + head, 1), :]
            scores = mm_nt(k_pair, q_head[head]) + bias[place, :].astype(F32)
            weights = jnp.exp(scores - lse_row)
            probs_g = mm_nt(v_pair, g_head[head])
            one_dv = mm(weights.astype(BF16), g_head[head])
            scores_g = (weights * (probs_g - delta_row)).astype(BF16)
            one_dk = mm(scores_g, q_head[head])
            dq_acc[...] += mm_tn(scores_g, k_head)
            dk = one_dk if dk is None else dk + one_dk
            dv = one_dv if dv is None else dv + one_dv
        cos = cosine[place, :]
        sin = sine[place, :]
        dk_out[place, :] = (dk * cos - half_swap(dk) * sin).astype(BF16)
        dv_out[place, :] = dv.astype(BF16)
        return carry

    lax.fori_loop(0, length // block, one_block, 0)
    dq = dq_acc[...] * (HEAD_DIM**-0.5)
    dq_out[...] = (dq * cosine[...] - half_swap(dq) * sine[...]).astype(BF16)
    columns = pl.ds(pl.multiple_of(step * LANES, LANES), LANES)
    three = mm(normed[...], jnp.concatenate([dq_out[...], dk_out[...], dv_out[...]], axis=1))
    for j in range(3):
        grad_out[me[0] ^ j, :, columns] = three[:, j * LANES : (j + 1) * LANES].astype(BF16)


def project_back_kernel(me, x, *refs):
    parts = refs[:-9]
    resg, wq, wk, wv, small_t, small_g, tok_out, small_out, first_acc = refs[-9:]
    step = pl.program_id(0)
    block, width = x.shape

    @pl.when(step == 0)
    def _():
        first_acc[...] = jnp.zeros_like(first_acc)

    rows = x[...].astype(F32)
    scale = lax.rsqrt(jnp.mean(rows * rows, axis=1, keepdims=True) + EPS)
    normed_g = None
    for j, weight in enumerate((wq, wk, wv)):
        part = jnp.concatenate([p[...] for p in parts[j::3]], axis=1)
        one = mm_nt(part, weight[0])
        normed_g = one if normed_g is None else normed_g + one
    first_acc[...] += jnp.sum(
        (normed_g * rows * scale).reshape(block // 8, 8, width), axis=0
    )
    scaled = normed_g * small_t[16:17, :]
    tok_out[...] = resg[...] + scale * scaled - rows * (scale * scale * scale) * jnp.mean(
        scaled * rows, axis=1, keepdims=True
    )

    @pl.when(step == pl.num_programs(0) - 1)
    def _():
        first = jnp.sum(first_acc[...], axis=0, keepdims=True)
        row = iota((LANES, width), 0)
        small_out[...] = (small_g[...] + jnp.where(row == 16, first, 0.0).T).astype(BF16)


def rotary_tables():
    half = HEAD_DIM // 2
    frequency = 10000.0 ** (-np.arange(half) * 2.0 / HEAD_DIM)
    sign = np.tile(np.repeat([-1.0, 1.0], half), LANES // HEAD_DIM)
    tables = []
    for positions in (np.arange(0, LEN, STRIDE), np.arange(STRIDE)):
        angles = np.tile(positions[:, None] * frequency[None, :], (1, LANES // half))
        tables += [np.cos(angles), np.sin(angles)]
    return [t.astype(np.float32) for t in tables + [sign]]


def body(
    tokens, previous_logits, routes, prefix, slot_order, first_gain, query_weight, key_weight,
    value_weight, output_weight, second_gain, router_weight, constant_mix, constant_vectors,
    gate_weight, up_weight, down_weight, cotangent,
):
    owners = lax.axis_size("expert")
    shards = lax.axis_size("shard")
    local_experts, shard_rows, ff = gate_weight.shape
    experts = local_experts * owners
    count, width = tokens.shape
    kinds = experts + ZC
    capacity = count * TOP // kinds // 8 * 8
    stride = -(-capacity // 16) * 16
    tiles = ff // TILE
    down_rows = down_weight.shape[1]
    me = lax.axis_index("expert").astype(jnp.int32).reshape(1)
    packed_width = width + LANES
    cos_a, sin_a, cos_b, sin_b, sign = (jnp.asarray(t) for t in rotary_tables())
    cos_a, sin_a, cos_b, sin_b, me = lax.optimization_barrier((cos_a, sin_a, cos_b, sin_b, me))
    cos_a, sin_a, cos_b, sin_b = cos_a[:, None], sin_a[:, None], cos_b[None], sin_b[None]
    cosine = (cos_a * cos_b - sin_a * sin_b).reshape(LEN, LANES)
    sine = ((sin_a * cos_b + cos_a * sin_b) * sign).reshape(LEN, LANES)
    struct = jax.ShapeDtypeStruct

    packed = call(
        pack_kernel, "pack", (1,),
        [whole((shard_rows, width))] * 4
        + [whole((1, shard_rows))] * 2
        + [whole((kinds, shard_rows)), whole((4, shard_rows)), whole((2, shard_rows))],
        whole((shard_rows, packed_width)),
        struct((shard_rows, packed_width), BF16),
        scratch=[pltpu.VMEM((LANES, LANES), F32)],
        traffic=1 << 20, prefetch=1,
    )(
        me, query_weight, key_weight, value_weight, output_weight, first_gain[None], second_gain[None],
        router_weight.T, constant_mix.T, constant_vectors,
    )

    def send(part, k):
        return lax.ppermute(part, "expert", [(i, i ^ k) for i in range(owners)])

    def add(a, b):
        return (a.astype(F32) + b.astype(F32)).astype(BF16)

    core = (lax.axis_index("shard") % 2).astype(jnp.int32).reshape(1)
    half = width // 2
    own = lax.all_gather(packed, "shard", axis=0, tiled=True)
    top, low = own[None, :half, :width], own[None, half:, :width]
    top = jnp.concatenate([top, send(top, 1)])
    low = jnp.concatenate([low, send(low, 2)])
    top_in, low_in = send(top, 2), send(low, 1)
    weights = jnp.concatenate([
        jnp.concatenate([top, top_in]),
        jnp.stack([low[0], low_in[0], low[1], low_in[1]]),
    ], axis=1)
    aligned = shard_rows % 16 == 0 and down_rows == TILE
    expert_rows = 2 * tiles * shard_rows + width // TILE * down_rows

    def gather_expert(l):
        if aligned:
            one = call(
                pack_expert_kernel, "pack_expert", (1,),
                [pl.BlockSpec((1,) + w.shape[1:], lambda i: (l, 0, 0))
                 for w in (gate_weight, up_weight, down_weight)],
                whole((expert_rows, TILE)), struct((expert_rows, TILE), BF16), traffic=5 << 20,
            )(gate_weight, up_weight, down_weight)
        else:
            one = jnp.concatenate([
                w[l].reshape(w.shape[1], -1, TILE).transpose(1, 0, 2).reshape(-1, TILE)
                for w in (gate_weight, up_weight, down_weight)
            ])
        full = lax.all_gather(one, "shard", axis=0, tiled=True)
        full = full.reshape(shards, expert_rows, TILE)
        if aligned:
            return full, full
        split = 2 * tiles * shard_rows
        gate_up = full[:, :split].reshape(shards, 2 * tiles, shard_rows, TILE)
        down = full[:, split:].reshape(shards, width // TILE, down_rows, TILE)
        down = down.transpose(1, 0, 2, 3).reshape(width // TILE, tiles, TILE, TILE)
        return (
            gate_up.transpose(1, 0, 2, 3).reshape(1, -1, TILE),
            down.transpose(1, 0, 2, 3).reshape(tiles, width, TILE),
        )

    expert_full = [gather_expert(l) for l in range(local_experts)]

    dest_col, dest_row = call(
        functools.partial(slots_kernel, experts, capacity, stride), "slots", (1,),
        [whole((count, TOP)), whole((1, count)), whole((count, 1))],
        [whole((count, LANES)), whole((8, count))],
        [struct((count, LANES), jnp.int32), struct((8, count), jnp.int32)],
        flops=2 * 3 * count * count * LANES, traffic=1 << 20,
    )(routes, slot_order, slot_order.reshape(count, 1))

    steps = count // BLOCK
    weight_block = [
        pl.BlockSpec((1, width, width), lambda i, me, *rest, j=j: (me[0] ^ j, 0, 0))
        for j in range(4)
    ]
    output_block = weight_block.pop()
    small_block = pl.BlockSpec((width, LANES), lambda i, *rest: (0, width // LANES))
    wide = rows_of(BLOCK, width)
    table = rows_of(BLOCK, LANES)
    act = struct((count, width), BF16)
    queries, keys, values, normed_one, small_t = call(
        project_kernel, "project", (steps,),
        [wide] + weight_block + [small_block, table, table],
        [wide] * 3 + [pl.BlockSpec((width, BLOCK), lambda i, *rest: (0, i)), whole((LANES, width))],
        [act] * 3 + [struct((width, count), BF16), struct((LANES, width), F32)],
        flops=6 * count * width * width, traffic=12 << 20, prefetch=1,
    )(me, tokens, weights, weights, weights, own, cosine, sine)

    attn_mix, lse, residual, normed_two, tok = call(
        attend_kernel, "attend", (steps,),
        [wide, whole((count, width)), whole((count, width)), wide, output_block,
         small_block, whole((LANES, width)), rows_of(BLOCK, kinds), rows_of(BLOCK, TOP)],
        [wide, pl.BlockSpec((16, BLOCK), lambda i, *rest: (0, i)), wide, wide, table],
        [act, struct((16, count), F32), struct((count, width), F32), act,
         struct((count, LANES), F32)],
        scratch=[pltpu.VMEM((BLOCK, count), F32), pltpu.VMEM((BLOCK, width), BF16),
                 pltpu.VMEM((BLOCK, LANES), F32)],
        flops=30 << 30, traffic=16 << 20, trans=HEADS * count * count, prefetch=2,
    )(me, prefix, queries, keys, values, tokens, weights, own, small_t,
      previous_logits, routes)

    def exchange(parts):
        return [parts[0]] + [
            lax.ppermute(part, "expert", [(i, i ^ k) for i in range(owners)])
            for k, part in list(enumerate(parts))[1:]
        ]

    pair = whole((2, stride, width))
    pair_shape = struct((2, stride, width), BF16)

    def dispatch(l):
        parts = call(
            functools.partial(dispatch_kernel, local_experts, l), "dispatch", (owners,),
            [whole((count, width)), whole((count, width)), whole((count, LANES)),
             whole((count, TOP)), whole((8, count))],
            [pair] * owners, [pair_shape] * owners,
            scratch=[pltpu.VMEM((count, LANES), BF16)],
            flops=4 * owners * stride * count * width, traffic=6 << 20, prefetch=1,
        )(me, normed_two, cotangent, tok, routes, dest_row)
        return parts

    dispatched = [dispatch(l) for l in range(local_experts)]
    received = [exchange(parts) for parts in dispatched]

    chunks, chunk_rows = (shards, shard_rows) if aligned else (1, width)
    local = owners * stride

    def run_expert(l, rows, after):
        gate_up, down = expert_full[l]
        weights = [
            pl.BlockSpec((chunks, chunk_rows, TILE), lambda f, *rest, j=j: (0, j // 2 * tiles + 2 * f + j % 2, 0))
            for j in range(4)
        ] + [
            pl.BlockSpec((1, width, TILE), lambda f, *rest, j=j: (2 * f + j, 2 if aligned else 0, 0))
            for j in range(2)
        ]
        halves = aligned
        if halves:
            grad_shapes = [(shards // 2, expert_rows, TILE)] * 2
        elif aligned:
            grad_shapes = [(shards, expert_rows, TILE)]
        else:
            grad_shapes = [(1, 2 * tiles * width, TILE), (tiles, width, TILE)]
        *outs, = call(
            functools.partial(expert_kernel, owners, aligned, halves), "expert", (tiles // 2,),
            [pair] * owners + weights,
            [pair] * owners + [whole(g) for g in grad_shapes],
            [pair_shape] * owners + [struct(g, BF16) for g in grad_shapes],
            scratch=[pltpu.VMEM((local, width), BF16)] * 2 + [pltpu.VMEM((width, local), BF16)]
            + [pltpu.VMEM((local, width), F32)] * 2,
            flops=16 * local * width * ff, traffic=24 << 20, trans=local * ff, prefetch=1,
        )(core, *rows, gate_up, gate_up, gate_up, gate_up, down, down)
        grads = outs[owners:]
        if halves:
            keep, give = grads
        elif aligned:
            grad = grads[0]
        else:
            gate_up_g = grads[0].reshape(2 * tiles, shards, shard_rows, TILE).transpose(1, 0, 2, 3)
            down_g = grads[1].reshape(tiles, width // TILE, TILE, TILE).transpose(1, 0, 2, 3)
            down_g = down_g.reshape(width // TILE, shards, down_rows, TILE).transpose(1, 0, 2, 3)
            grad = jnp.concatenate(
                [gate_up_g.reshape(shards, -1, TILE), down_g.reshape(shards, -1, TILE)], axis=1
            )
        if halves:
            outs[:owners], keep, give, after = lax.optimization_barrier(
                (outs[:owners], keep, give, after)
            )
            grad = add(keep, lax.ppermute(give, "shard", [(i, i ^ 1) for i in range(shards)]))
        return outs[:owners], grad.reshape(-1, TILE), after

    def reduce_expert(grad):
        return lax.psum_scatter(
            grad, "shard", scatter_dimension=0, tiled=True,
            axis_index_groups=(
                None if len(grad) == shards * expert_rows
                else [list(range(c, shards, 2)) for c in range(2)]
            ),
        )

    returned = []
    expert_sums = []
    for l in range(local_experts):
        rows, _ = lax.optimization_barrier((received[l], dispatched[-1]))
        back, grad, ahead = run_expert(l, rows, (received[l + 1 :], returned))
        received[l + 1 :], returned = ahead
        back = exchange(back)
        if l + 1 == local_experts:
            back, grad = lax.optimization_barrier((back, grad))
        returned = returned + back
        expert_sums.append(reduce_expert(grad))

    mixed, previous_grad, residual_grad, heads_grad, delta, output_grad, small_grad = call(
        functools.partial(combine_kernel, experts, owners, local_experts), "combine", (steps,),
        [pair] * len(returned)
        + [wide, wide, wide, table, rows_of(BLOCK, TOP), table, wide, output_block,
           whole((LANES, width))],
        [wide, rows_of(BLOCK, kinds), wide, wide, pl.BlockSpec((16, BLOCK), lambda i, *rest: (0, i)),
         whole((width, width)), whole((width, LANES))],
        [act, struct((count, kinds), F32), struct((count, width), F32), act,
         struct((16, count), F32), struct((width, width), BF16), struct((width, LANES), F32)],
        scratch=[pltpu.VMEM((width, width), F32), pltpu.VMEM((width, LANES), F32),
                 pltpu.VMEM((8, width), F32)]
        + [pltpu.VMEM((local_experts, local, width), BF16)] * 2,
        flops=6 * count * 2 * local * width + 4 * count * width * width, traffic=24 << 20, prefetch=1,
    )(me, *returned, residual, normed_two, cotangent, tok,
      routes, dest_col, attn_mix, weights, small_t)

    def first_turn(grad):
        return send(grad[1::2, :half], 1), send(grad[2:, half:], 2)

    def second_turn(grad, came):
        top, low = add(grad[0::2, :half], came[0]), add(grad[:2, half:], came[1])
        return (top[0], low[0]), (send(top[1], 2), send(low[1], 1))

    def join(mine, came):
        return jnp.concatenate([add(a, b) for a, b in zip(mine, came)], axis=0)

    pairs = width // LANES // 2
    columns = pairs * LANES
    half_out = pl.BlockSpec((count, LANES), lambda i, *rest: (0, i))
    parts = []
    dense_grads = []
    moved = ()
    for start in (0, pairs):
        pair_block = pl.BlockSpec((count, LANES), lambda i, *rest, start=start: (0, i + start))
        *three, dense_grad = call(
            functools.partial(attend_back_kernel, start), "attend_back", (pairs,),
            [pair_block] * 4
            + [whole((16, count))] * 2
            + [whole((count, LANES))] * 2
            + [whole((width, count)),
               pl.BlockSpec((width, columns), lambda i, *rest, start=start: (0, start // pairs))],
            [half_out] * 3 + [whole((owners, width, columns))],
            [struct((count, columns), BF16)] * 3 + [struct((owners, width, columns), BF16)],
            scratch=[pltpu.VMEM((count, count), BF16), pltpu.VMEM((count, LANES), F32)],
            flops=30 << 30, traffic=6 << 20, trans=HEADS // 2 * count * count, prefetch=2,
        )(me, prefix, queries, keys, values, heads_grad, lse, delta, cosine, sine, normed_one,
          output_grad)
        if start:
            three, moved, expert_sums[0] = lax.optimization_barrier((three, moved, expert_sums[0]))
        parts += three
        dense_grads.append(dense_grad)
        if start == 0:
            moved = first_turn(dense_grad)
    mine_a, moved_a = second_turn(dense_grads[0], moved)
    moved_b = first_turn(dense_grads[1])

    half_wide = rows_of(BLOCK, columns)
    tokens_grad, small_grad = call(
        project_back_kernel, "project_back", (steps,),
        [wide] + [half_wide] * 6 + [wide] + weight_block
        + [whole((LANES, width)), whole((width, LANES))],
        [wide, whole((width, LANES))],
        [struct((count, width), F32), struct((width, LANES), BF16)],
        scratch=[pltpu.VMEM((8, width), F32)],
        flops=6 * count * width * width, traffic=18 << 20, prefetch=1,
    )(me, tokens, *parts, residual_grad, weights, weights, weights, small_t, small_grad)
    small_grad, moved_a, moved_b = lax.optimization_barrier((small_grad, moved_a, moved_b))
    mine_b, moved_b = second_turn(dense_grads[1], moved_b)
    quarters = [join(mine_a, moved_a), join(mine_b, moved_b)]
    quarter = jnp.concatenate(quarters + [small_grad], axis=1)
    quarter, expert_sums = lax.optimization_barrier((quarter, expert_sums))
    quarter = lax.psum_scatter(quarter, "shard", scatter_dimension=0, tiled=True)
    gathered = jnp.stack([quarter] + [send(quarter, k) for k in range(1, owners)]).astype(F32)
    dense = [
        lax.dynamic_index_in_dim(gathered[:, :, :width], me[0] ^ j, keepdims=False)
        for j in range(4)
    ]
    small = jnp.sum(gathered[:, :, width:], axis=0)
    if aligned:
        out_shapes = [w.shape for w in (gate_weight, up_weight, down_weight)]
        gate_sum, up_sum, down_sum = call(
            unpack_expert_kernel, "unpack", (1,),
            [whole((expert_rows, TILE))] * local_experts,
            [whole(o) for o in out_shapes], [struct(o, F32) for o in out_shapes],
            traffic=8 << 20,
        )(*expert_sums)
    else:
        split = 2 * tiles * shard_rows
        total = jnp.stack(expert_sums).astype(F32)
        gate_sum, up_sum = (
            part.reshape(local_experts, tiles, shard_rows, TILE).transpose(0, 2, 1, 3).reshape(
                local_experts, shard_rows, ff
            )
            for part in (total[:, : split // 2], total[:, split // 2 : split])
        )
        down_sum = total[:, split:].reshape(local_experts, width // TILE, down_rows, TILE)
        down_sum = down_sum.transpose(0, 2, 1, 3).reshape(local_experts, down_rows, width)
    return (
        mixed,
        tokens_grad,
        previous_grad,
        dense[0],
        dense[1],
        dense[2],
        dense[3],
        small[:, 0:kinds],
        small[:, kinds : kinds + 4],
        small[:, 18:20].T,
        small[:, 16],
        small[:, 17],
        gate_sum,
        up_sum,
        down_sum,
    )


def solution(mesh):
    rows = P(("expert", "shard"), None)
    expert = P("expert", "shard", None)
    flat = P("shard", None)
    return jax.shard_map(
        body,
        mesh=mesh,
        in_specs=(
            rows, rows, rows, P(("expert", "shard")), rows, P("shard"), flat, flat, flat, flat,
            P("shard"), flat, flat, P(None, "shard"), expert, expert, expert, rows,
        ),
        out_specs=(
            rows, rows, rows, flat, flat, flat, flat, flat, flat, P(None, "shard"), P("shard"),
            P("shard"), expert, expert, expert,
        ),
        check_vma=False,
    )
```

```python
import functools
import numpy as np
import jax
import jax.numpy as jnp
from jax import lax
from jax.experimental import pallas as pl
from jax.experimental.pallas import tpu as pltpu
from jax.sharding import PartitionSpec as P

HEADS = 12
HEAD_DIM = 64
ZC = 4
TOP = 2
LEN = 1024
EPS = 1e-05
NEG = -1e30
LANES = 128
BLOCK = 256
TILE = 256
STRIDE = 32
F32 = jnp.float32
BF16 = jnp.bfloat16
VMEM_LIMIT = 56 << 20


def call(body, name, grid, in_specs, out_specs, out_shape, scratch=(), flops=0, traffic=0, trans=0, prefetch=0):
    return pl.pallas_call(
        body,
        name=name,
        grid_spec=pltpu.PrefetchScalarGridSpec(
            num_scalar_prefetch=prefetch,
            grid=grid,
            in_specs=in_specs,
            out_specs=out_specs,
            scratch_shapes=scratch,
        ),
        out_shape=out_shape,
        compiler_params=pltpu.CompilerParams(
            dimension_semantics=("arbitrary",) * len(grid), vmem_limit_bytes=VMEM_LIMIT
        ),
        cost_estimate=pl.CostEstimate(flops=flops, transcendentals=trans, bytes_accessed=traffic),
    )


def mm(a, b):
    return lax.dot_general(a, b, (((1,), (0,)), ((), ())), preferred_element_type=F32)


def mm_nt(a, b):
    return lax.dot_general(a, b, (((1,), (1,)), ((), ())), preferred_element_type=F32)


def mm_tn(a, b):
    return lax.dot_general(a, b, (((0,), (0,)), ((), ())), preferred_element_type=F32)


def iota(shape, axis):
    return lax.broadcasted_iota(jnp.int32, shape, axis)


def whole(shape):
    return pl.BlockSpec(shape, lambda *idx: (0,) * len(shape))


def rows_of(block, width):
    return pl.BlockSpec((block, width), lambda i, *rest: (i, 0))


def split_high_low(values):
    high = values.astype(BF16)
    low = (values - high.astype(F32)).astype(BF16)
    return high, low


def pack_kernel(me, q, k, v, o, gain1, gain2, router, mix, vectors, out, scratch):
    rows, width = q.shape
    for j, weight in enumerate((q, k, v, o)):

        @pl.when(me[0] == j)
        def _():
            out[:, 0:width] = weight[...]

    scratch[...] = jnp.zeros_like(scratch)
    n_router = router.shape[0]
    scratch[0:n_router, 0:rows] = router[...].astype(F32)
    scratch[n_router : n_router + mix.shape[0], 0:rows] = mix[...].astype(F32)
    scratch[16:17, 0:rows] = gain1[...].astype(F32)
    scratch[17:18, 0:rows] = gain2[...].astype(F32)
    scratch[18:20, 0:rows] = vectors[...].astype(F32)
    out[:, width : width + LANES] = scratch[...].T[0:rows, :].astype(BF16)


def slots_kernel(experts, capacity, stride, routes, order_row, order_col, dest_col, dest_row):
    tokens = routes.shape[0]
    r0 = routes[:, 0:1]
    r1 = routes[:, 1:2]
    lane = iota((tokens, LANES), 1)
    hot = jnp.where((lane == r0) | (lane == r1), 1.0, 0.0)
    hot = jnp.where(lane < experts, hot, 0.0).astype(BF16)
    row = iota((tokens, tokens), 0)
    col = iota((tokens, tokens), 1)
    to_turn = jnp.where(order_col[...] == col, 1.0, 0.0).astype(BF16)
    hot_turn = mm(to_turn, hot).astype(BF16)
    earlier = mm(jnp.where(col < row, 1.0, 0.0).astype(BF16), hot_turn)
    earlier = jnp.minimum(earlier, 255.0).astype(BF16)
    to_token = jnp.where(order_row[...] == row, 1.0, 0.0).astype(BF16)
    position = mm(to_token, earlier)
    p0 = jnp.sum(jnp.where(lane == r0, position, 0.0), axis=1, keepdims=True)
    p1 = jnp.sum(jnp.where(lane == r1, position, 0.0), axis=1, keepdims=True)
    d0 = jnp.where((r0 < experts) & (p0 < capacity), r0.astype(F32) * stride + p0, -1.0)
    d1 = jnp.where((r1 < experts) & (p1 < capacity), r1.astype(F32) * stride + p1, -1.0)
    both = jnp.where(lane == 0, d0, jnp.where(lane == 1, d1, 0.0))
    dest_col[...] = both.astype(jnp.int32)
    dest_row[...] = both.T[0:8, :].astype(jnp.int32)


def half_swap(values):
    lane = iota(values.shape, 1) % HEAD_DIM
    half = HEAD_DIM // 2
    return jnp.where(
        lane < half, pltpu.roll(values, LANES - half, 1), pltpu.roll(values, half, 1)
    )


def project_kernel(me, x, wq, wk, wv, small, cosine, sine, q_out, k_out, v_out, n_out, small_t):
    @pl.when(pl.program_id(0) == 0)
    def _():
        small_t[...] = small[...].astype(F32).T

    width = x.shape[1]
    rows = x[...].astype(F32)
    scale = lax.rsqrt(jnp.mean(rows * rows, axis=1, keepdims=True) + EPS)
    normed = (rows * scale * small_t[16:17, :]).astype(BF16)
    n_out[...] = normed.T
    cos = cosine[...]
    sin = sine[...]
    for weight, out, factor in ((wq, q_out, HEAD_DIM**-0.5), (wk, k_out, None)):
        lin = mm(normed, weight[0])
        for c in range(width // LANES):
            part = lin[:, c * LANES : (c + 1) * LANES]
            turned = part * cos + half_swap(part) * sin
            if factor is not None:
                turned = turned * factor
            out[:, c * LANES : (c + 1) * LANES] = turned.astype(BF16)
    v_out[...] = mm(normed, wv[0]).astype(BF16)


def attend_kernel(
    me, prefix, q, k, v, x, wo, small, small_t, prev, routes,
    mix_out, lse_out, res_out, n_out, tok_out, bias, mixed, lse,
):
    block, width = q.shape
    length = k.shape[0]
    start = pl.program_id(0) * block
    limit = jnp.maximum(start + iota((block, 1), 0) + 1, prefix[0])
    bias[...] = jnp.where(iota((block, length), 1) < limit, 0.0, NEG)
    lane = iota((block, LANES), 1)
    first = lane < HEAD_DIM
    lse[...] = jnp.zeros_like(lse)

    def one_pair(pair, carry):
        columns = pl.ds(pl.multiple_of(pair * LANES, LANES), LANES)
        q_pair = q[:, columns]
        k_pair = k[:, columns]
        v_pair = v[:, columns]
        outs = []
        for head in range(2):
            mine = first if head == 0 else jnp.logical_not(first)
            q_head = jnp.where(mine, q_pair, jnp.zeros_like(q_pair))
            scores = mm_nt(q_head, k_pair) + bias[...]
            top = jnp.max(scores, axis=1, keepdims=True)
            weights = jnp.exp(scores - top)
            total = jnp.sum(weights, axis=1, keepdims=True)
            outs.append(mm(weights.astype(BF16), v_pair) / total)
            lse[...] = jnp.where(lane == 2 * pair + head, top + jnp.log(total), lse[...])
        mixed[:, columns] = jnp.where(first, outs[0], outs[1]).astype(BF16)
        return carry

    lax.fori_loop(0, width // LANES, one_pair, 0)
    mix_out[...] = mixed[...]
    lse_out[...] = lse[...].T[0:16, :]
    residual = x[...].astype(F32) + mm(mixed[...], wo[0])
    res_out[...] = residual
    scale = lax.rsqrt(jnp.mean(residual * residual, axis=1, keepdims=True) + EPS)
    normed = (residual * scale * small_t[17:18, :]).astype(BF16)
    n_out[...] = normed
    lin = mm(normed, small[...])
    kinds = prev.shape[1]
    logits = lin[:, 0:kinds] + prev[...]
    kind = iota((block, kinds), 1)
    c0 = jnp.sum(jnp.where(kind == routes[:, 0:1], logits, 0.0), axis=1, keepdims=True)
    c1 = jnp.sum(jnp.where(kind == routes[:, 1:2], logits, 0.0), axis=1, keepdims=True)

    def pair_softmax(a, b):
        top = jnp.maximum(a, b)
        ea = jnp.exp(a - top)
        eb = jnp.exp(b - top)
        total = ea + eb
        return ea / total, eb / total

    g0, g1 = pair_softmax(c0, c1)
    m00, m01 = pair_softmax(lin[:, kinds : kinds + 1], lin[:, kinds + 1 : kinds + 2])
    m10, m11 = pair_softmax(lin[:, kinds + 2 : kinds + 3], lin[:, kinds + 3 : kinds + 4])
    packed = jnp.zeros((block, LANES), F32)
    for index, column in enumerate((g0, g1, m00, m01, m10, m11, scale)):
        packed = jnp.where(lane == index, column, packed)
    tok_out[...] = packed


def pack_expert_kernel(gate, up, down, out):
    rows, ff = gate.shape[1:]
    down_rows, width = down.shape[1:]
    tiles = ff // TILE
    for index, ref in enumerate((gate, up)):
        for f in range(tiles):
            start = (index * tiles + f) * rows
            out[start : start + rows, :] = ref[0, :, f * TILE : (f + 1) * TILE]
    base = 2 * tiles * rows
    for c in range(width // TILE):
        out[base + c * down_rows : base + (c + 1) * down_rows, :] = down[
            0, :, c * TILE : (c + 1) * TILE
        ]


def unpack_expert_kernel(*refs):
    gate, up, down = refs[-3:]
    rows, ff = gate.shape[1:]
    down_rows, width = down.shape[1:]
    tiles = ff // TILE
    base = 2 * tiles * rows
    for l, ref in enumerate(refs[:-3]):
        for index, out in enumerate((gate, up)):
            for f in range(tiles):
                start = (index * tiles + f) * rows
                out[l, :, f * TILE : (f + 1) * TILE] = ref[start : start + rows, :].astype(F32)
        for c in range(width // TILE):
            down[l, :, c * TILE : (c + 1) * TILE] = ref[
                base + c * down_rows : base + (c + 1) * down_rows, :
            ].astype(F32)


def dispatch_kernel(local_experts, l, me, normed, grad, tok, routes, dest_row, *rest):
    outs, gates = rest[:-1], rest[-1]
    step = pl.program_id(0)
    tokens = normed.shape[0]
    stride = outs[0].shape[1]
    expert = (me[0] ^ step) * local_experts + l

    @pl.when(step == 0)
    def _():
        lane = iota((tokens, LANES), 1)
        kind = lane % HEAD_DIM
        value = jnp.where(kind == routes[:, 0:1], tok[:, 0:1], 0.0)
        value = value + jnp.where(kind == routes[:, 1:2], tok[:, 1:2], 0.0)
        high = value.astype(BF16).astype(F32)
        gates[...] = jnp.where(lane < HEAD_DIM, high, value - high).astype(BF16)

    slot = expert * stride + iota((stride, tokens), 0)
    hit = (dest_row[0:1, :] == slot) | (dest_row[1:2, :] == slot)
    take = jnp.where(hit, 1.0, 0.0).astype(BF16)
    row = mm(take, normed[...]).astype(BF16)
    slot_gates = mm(take, gates[...])
    mine = iota((stride, LANES), 1) % HEAD_DIM == expert
    slot_gate = jnp.sum(jnp.where(mine, slot_gates, 0.0), axis=1, keepdims=True)
    slot_g = (mm(take, grad[...]) * slot_gate).astype(BF16)
    for k, out in enumerate(outs):

        @pl.when(step == k)
        def _():
            out[0] = row
            out[1] = slot_g


def expert_kernel(owners, merged, halves, core, *refs):
    sent = refs[:owners]
    weights = refs[owners : owners + 6]
    backs = refs[owners + 6 : 2 * owners + 6]
    grads = refs[2 * owners + 6 : -5]
    r_all, s_all, r_turned, out_acc, row_acc = refs[-5:]
    step = pl.program_id(0)
    steps = pl.num_programs(0)
    stride, width = sent[0].shape[1:]
    chunks, chunk_rows = weights[0].shape[:2]

    @pl.when(step == 0)
    def _():
        for k, ref in enumerate(sent):
            r_all[k * stride : (k + 1) * stride, :] = ref[0]
            s_all[k * stride : (k + 1) * stride, :] = ref[1]
        r_turned[...] = r_all[...].T
        out_acc[...] = jnp.zeros_like(out_acc)
        row_acc[...] = jnp.zeros_like(row_acc)

    def tile_pair(a, b):
        return jnp.concatenate([t[...].reshape(width, TILE) for t in (a, b)], axis=1)

    def down_tile(ref):
        parts = [ref[0, c * TILE : (c + 1) * TILE, :] for c in range(width // TILE)]
        return jnp.concatenate(parts, axis=1)

    r = r_all[...]
    s = s_all[...]
    gate = tile_pair(weights[0], weights[1])
    up = tile_pair(weights[2], weights[3])
    d = jnp.concatenate([down_tile(weights[4]), down_tile(weights[5])], axis=0)
    gate_pre = mm(r, gate)
    up_pre = mm(r, up)
    sig = jax.nn.sigmoid(gate_pre)
    silu = gate_pre * sig
    hid = (silu * up_pre).astype(BF16)
    hidden_g = mm_nt(s, d)
    out_acc[...] += mm(hid, d)
    gate_g = (hidden_g * (up_pre * (sig + silu * (1.0 - sig)))).astype(BF16)
    up_g = (hidden_g * silu).astype(BF16)
    both_g = jnp.concatenate([gate_g, up_g], axis=1)
    row_acc[...] += mm_nt(both_g, jnp.concatenate([gate, up], axis=1))
    down_grad = mm_tn(hid, s).astype(BF16)
    gate_grad = mm(r_turned[...], gate_g).astype(BF16)
    up_grad = mm(r_turned[...], up_g).astype(BF16)
    even = core[0] == 0
    for i in range(2):
        tile = 2 * step + i
        for index, value in enumerate((gate_grad, up_grad)):
            start = pl.multiple_of((index * 2 * steps + tile) * chunk_rows, 16)
            place = pl.ds(start, chunk_rows)
            value = value[:, i * TILE : (i + 1) * TILE]
            if halves:
                value = value.reshape(chunks // 2, 2, chunk_rows, TILE)
                for out, flag in zip(grads, (even, jnp.logical_not(even))):
                    out[:, place, :] = jnp.where(flag, value[:, 0], value[:, 1])
            else:
                grads[0][:, place, :] = value.reshape(chunks, chunk_rows, TILE)
    base = 4 * steps * chunk_rows if merged else 0
    for c in range(width // TILE):
        pair = [down_grad[i * TILE : (i + 1) * TILE, c * TILE : (c + 1) * TILE] for i in range(2)]
        place = slice(base + c * TILE, base + (c + 1) * TILE)
        if halves:
            for out, flag in zip(grads, (even, jnp.logical_not(even))):
                out[step, place, :] = jnp.where(flag, pair[0], pair[1])
        else:
            for i in range(2):
                grads[-1][2 * step + i, place, :] = pair[i]

    @pl.when(step == steps - 1)
    def _():
        for k, ref in enumerate(backs):
            ref[0] = out_acc[k * stride : (k + 1) * stride, :].astype(BF16)
            ref[1] = row_acc[k * stride : (k + 1) * stride, :].astype(BF16)


def combine_kernel(experts, owners, local_experts, me, *refs):
    backs = refs[: owners * local_experts]
    (
        residual, normed, grad, tok, routes, dest, mix, wo, small_t,
        mixed_out, prev_out, resg_out, headg_out, delta_out, wo_out, small_out,
        wo_acc, small_acc, second_acc, eo_all, rg_all,
    ) = refs[owners * local_experts :]
    step = pl.program_id(0)
    block, width = residual.shape
    stride = backs[0].shape[1]
    local = owners * stride

    @pl.when(step == 0)
    def _():
        wo_acc[...] = jnp.zeros_like(wo_acc)
        small_acc[...] = jnp.zeros_like(small_acc)
        second_acc[...] = jnp.zeros_like(second_acc)
        for l in range(local_experts):
            for k in range(owners):
                place = slice(k * stride, (k + 1) * stride)
                eo_all[l, place, :] = backs[l * owners + k][0]
                rg_all[l, place, :] = backs[l * owners + k][1]

    slot = iota((1, local), 1)
    owner_slot = ((slot // stride) ^ me[0]) * (local_experts * stride) + slot % stride

    ep = [None, None]
    back = None
    for l in range(local_experts):
        ident = owner_slot + l * stride
        t0 = jnp.where(dest[:, 0:1] == ident, 1.0, 0.0)
        t1 = jnp.where(dest[:, 1:2] == ident, 1.0, 0.0)
        eo = eo_all[l]
        rg = rg_all[l]
        e0 = mm(t0.astype(BF16), eo)
        e1 = mm(t1.astype(BF16), eo)
        b = mm((t0 + t1).astype(BF16), rg)
        ep[0] = e0 if ep[0] is None else ep[0] + e0
        ep[1] = e1 if ep[1] is None else ep[1] + e1
        back = b if back is None else back + b

    res = residual[...]
    n_low = normed[...]
    nf = n_low.astype(F32)
    g_low = grad[...]
    g = g_low.astype(F32)
    gate = [tok[:, 0:1], tok[:, 1:2]]
    mw = [[tok[:, 2:3], tok[:, 3:4]], [tok[:, 4:5], tok[:, 5:6]]]
    scale = tok[:, 6:7]
    vec = [small_t[18:19, :], small_t[19:20, :]]
    along_n = jnp.sum(g * nf, axis=1, keepdims=True)
    along_vec = [jnp.sum(g * vec[c], axis=1, keepdims=True) for c in range(2)]
    gate_g = []
    on_n = 0.0
    sel = [0.0, 0.0]
    copy_weight = 0.0
    for t in range(TOP):
        route = routes[:, t : t + 1]
        is_copy = jnp.where(route == experts + 1, 1.0, 0.0)
        is_const = [jnp.where(route == experts + 2 + c, 1.0, 0.0) for c in range(2)]
        a = is_copy + is_const[0] * mw[0][0] + is_const[1] * mw[1][0]
        b = [is_const[c] * mw[c][1] for c in range(2)]
        gate_g.append(
            jnp.sum(g * ep[t], axis=1, keepdims=True)
            + a * along_n
            + b[0] * along_vec[0]
            + b[1] * along_vec[1]
        )
        on_n = on_n + gate[t] * a
        copy_weight = copy_weight + gate[t] * is_copy
        sel = [sel[c] + gate[t] * is_const[c] for c in range(2)]
    vec_w = [sel[c] * mw[c][1] for c in range(2)]
    mixed_out[...] = (
        res + gate[0] * ep[0] + gate[1] * ep[1] + on_n * nf + vec_w[0] * vec[0] + vec_w[1] * vec[1]
    ).astype(BF16)

    centre = gate[0] * gate_g[0] + gate[1] * gate_g[1]
    pair_g = [gate[t] * (gate_g[t] - centre) for t in range(TOP)]
    lane = iota((block, LANES), 1)
    logit_g = jnp.where(lane == routes[:, 0:1], pair_g[0], 0.0)
    logit_g = logit_g + jnp.where(lane == routes[:, 1:2], pair_g[1], 0.0)
    kinds = prev_out.shape[1]
    prev_out[...] = logit_g[:, 0:kinds]
    for c in range(2):
        w0 = sel[c] * along_n
        w1 = sel[c] * along_vec[c]
        mid = mw[c][0] * w0 + mw[c][1] * w1
        logit_g = jnp.where(lane == kinds + 2 * c, mw[c][0] * (w0 - mid), logit_g)
        logit_g = jnp.where(lane == kinds + 2 * c + 1, mw[c][1] * (w1 - mid), logit_g)
    high, low = split_high_low(logit_g)
    table = small_t[...]
    table = jnp.where(iota(table.shape, 0) < 16, table, 0.0).astype(BF16)
    direct = copy_weight + sel[0] * mw[0][0] + sel[1] * mw[1][0]
    normed_g = back + direct * g + mm(high, table) + mm(low, table)
    gain = small_t[17:18, :]
    scaled = normed_g * gain
    second_acc[...] += jnp.sum(
        (normed_g * res * scale).reshape(block // 8, 8, width), axis=0
    )
    resg = g + scale * scaled - res * (scale * scale * scale) * jnp.mean(
        scaled * res, axis=1, keepdims=True
    )
    resg_out[...] = resg
    attn_g = resg.astype(BF16)
    am = mix[...]
    wo_acc[...] += mm_tn(am, attn_g)
    heads_g = mm_nt(attn_g, wo[0]).astype(BF16)
    headg_out[...] = heads_g
    product = heads_g.astype(F32) * am.astype(F32)
    p_high, p_low = split_high_low(product)
    head_of = jnp.where(
        iota((16, width), 1) // HEAD_DIM == iota((16, width), 0), 1.0, 0.0
    ).astype(BF16)
    delta_out[...] = mm_nt(head_of, p_high) + mm_nt(head_of, p_low)
    small_acc[...] += mm_tn(n_low, high) + mm_tn(n_low, low)
    coefficient = jnp.where(lane == 18, vec_w[0], jnp.where(lane == 19, vec_w[1], 0.0))
    c_high, c_low = split_high_low(coefficient)
    small_acc[...] += mm_tn(g_low, c_high) + mm_tn(g_low, c_low)

    @pl.when(step == pl.num_programs(0) - 1)
    def _():
        wo_out[...] = wo_acc[...].astype(BF16)
        second = jnp.sum(second_acc[...], axis=0, keepdims=True)
        row = iota((LANES, width), 0)
        small_out[...] = small_acc[...] + jnp.where(row == 17, second, 0.0).T


def attend_back_kernel(
    start, me, prefix, q, k, v, grad, lse, delta, cosine, sine, normed, output_g,
    dq_out, dk_out, dv_out, grad_out, bias, dq_acc,
):
    length = q.shape[0]
    step = pl.program_id(0)
    pair = step + start
    block = BLOCK
    lane_all = iota((length, LANES), 1)
    lane = iota((block, LANES), 1)

    @pl.when(step == 0)
    def _():
        limit = jnp.maximum(iota((1, length), 1) + 1, prefix[0])
        bias[...] = jnp.where(iota((length, length), 0) < limit, 0.0, NEG).astype(BF16)
        grad_out[me[0] ^ 3] = output_g[...]

    q_pair = q[...]
    g_pair = grad[...]
    zero = jnp.zeros_like(q_pair)
    q_head = []
    g_head = []
    for head in range(2):
        mine = (lane_all // HEAD_DIM) == head
        q_head.append(jnp.where(mine, q_pair, zero))
        g_head.append(jnp.where(mine, g_pair, zero))
    dq_acc[...] = jnp.zeros_like(dq_acc)

    def one_block(index, carry):
        place = pl.ds(pl.multiple_of(index * block, block), block)
        k_pair = k[place, :]
        v_pair = v[place, :]
        dk = None
        dv = None
        for head in range(2):
            mine = (lane // HEAD_DIM) == head
            k_head = jnp.where(mine, k_pair, jnp.zeros_like(k_pair))
            lse_row = lse[pl.ds(2 * pair + head, 1), :]
            delta_row = delta[pl.ds(2 * pair + head, 1), :]
            scores = mm_nt(k_pair, q_head[head]) + bias[place, :].astype(F32)
            weights = jnp.exp(scores - lse_row)
            probs_g = mm_nt(v_pair, g_head[head])
            one_dv = mm(weights.astype(BF16), g_head[head])
            scores_g = (weights * (probs_g - delta_row)).astype(BF16)
            one_dk = mm(scores_g, q_head[head])
            dq_acc[...] += mm_tn(scores_g, k_head)
            dk = one_dk if dk is None else dk + one_dk
            dv = one_dv if dv is None else dv + one_dv
        cos = cosine[place, :]
        sin = sine[place, :]
        dk_out[place, :] = (dk * cos - half_swap(dk) * sin).astype(BF16)
        dv_out[place, :] = dv.astype(BF16)
        return carry

    lax.fori_loop(0, length // block, one_block, 0)
    dq = dq_acc[...] * (HEAD_DIM**-0.5)
    dq_out[...] = (dq * cosine[...] - half_swap(dq) * sine[...]).astype(BF16)
    columns = pl.ds(pl.multiple_of(step * LANES, LANES), LANES)
    three = mm(normed[...], jnp.concatenate([dq_out[...], dk_out[...], dv_out[...]], axis=1))
    for j in range(3):
        grad_out[me[0] ^ j, :, columns] = three[:, j * LANES : (j + 1) * LANES].astype(BF16)


def project_back_kernel(me, x, *refs):
    parts = refs[:-9]
    resg, wq, wk, wv, small_t, small_g, tok_out, small_out, first_acc = refs[-9:]
    step = pl.program_id(0)
    block, width = x.shape

    @pl.when(step == 0)
    def _():
        first_acc[...] = jnp.zeros_like(first_acc)

    rows = x[...].astype(F32)
    scale = lax.rsqrt(jnp.mean(rows * rows, axis=1, keepdims=True) + EPS)
    normed_g = None
    for j, weight in enumerate((wq, wk, wv)):
        part = jnp.concatenate([p[...] for p in parts[j::3]], axis=1)
        one = mm_nt(part, weight[0])
        normed_g = one if normed_g is None else normed_g + one
    first_acc[...] += jnp.sum(
        (normed_g * rows * scale).reshape(block // 8, 8, width), axis=0
    )
    scaled = normed_g * small_t[16:17, :]
    tok_out[...] = resg[...] + scale * scaled - rows * (scale * scale * scale) * jnp.mean(
        scaled * rows, axis=1, keepdims=True
    )

    @pl.when(step == pl.num_programs(0) - 1)
    def _():
        first = jnp.sum(first_acc[...], axis=0, keepdims=True)
        row = iota((LANES, width), 0)
        small_out[...] = (small_g[...] + jnp.where(row == 16, first, 0.0).T).astype(BF16)


def rotary_tables():
    half = HEAD_DIM // 2
    frequency = 10000.0 ** (-np.arange(half) * 2.0 / HEAD_DIM)
    sign = np.tile(np.repeat([-1.0, 1.0], half), LANES // HEAD_DIM)
    tables = []
    for positions in (np.arange(0, LEN, STRIDE), np.arange(STRIDE)):
        angles = np.tile(positions[:, None] * frequency[None, :], (1, LANES // half))
        tables += [np.cos(angles), np.sin(angles)]
    return [t.astype(np.float32) for t in tables + [sign]]


def body(
    tokens, previous_logits, routes, prefix, slot_order, first_gain, query_weight, key_weight,
    value_weight, output_weight, second_gain, router_weight, constant_mix, constant_vectors,
    gate_weight, up_weight, down_weight, cotangent,
):
    owners = lax.axis_size("expert")
    shards = lax.axis_size("shard")
    local_experts, shard_rows, ff = gate_weight.shape
    experts = local_experts * owners
    count, width = tokens.shape
    kinds = experts + ZC
    capacity = count * TOP // kinds // 8 * 8
    stride = -(-capacity // 16) * 16
    tiles = ff // TILE
    down_rows = down_weight.shape[1]
    me = lax.axis_index("expert").astype(jnp.int32).reshape(1)
    packed_width = width + LANES
    cos_a, sin_a, cos_b, sin_b, sign = (jnp.asarray(t) for t in rotary_tables())
    cos_a, sin_a, cos_b, sin_b, me = lax.optimization_barrier((cos_a, sin_a, cos_b, sin_b, me))
    cos_a, sin_a, cos_b, sin_b = cos_a[:, None], sin_a[:, None], cos_b[None], sin_b[None]
    cosine = (cos_a * cos_b - sin_a * sin_b).reshape(LEN, LANES)
    sine = ((sin_a * cos_b + cos_a * sin_b) * sign).reshape(LEN, LANES)
    struct = jax.ShapeDtypeStruct

    packed = call(
        pack_kernel, "pack", (1,),
        [whole((shard_rows, width))] * 4
        + [whole((1, shard_rows))] * 2
        + [whole((kinds, shard_rows)), whole((4, shard_rows)), whole((2, shard_rows))],
        whole((shard_rows, packed_width)),
        struct((shard_rows, packed_width), BF16),
        scratch=[pltpu.VMEM((LANES, LANES), F32)],
        traffic=1 << 20, prefetch=1,
    )(
        me, query_weight, key_weight, value_weight, output_weight, first_gain[None], second_gain[None],
        router_weight.T, constant_mix.T, constant_vectors,
    )

    def send(part, k):
        return lax.ppermute(part, "expert", [(i, i ^ k) for i in range(owners)])

    def add(a, b):
        return (a.astype(F32) + b.astype(F32)).astype(BF16)

    core = (lax.axis_index("shard") % 2).astype(jnp.int32).reshape(1)
    half = width // 2
    own = lax.all_gather(packed, "shard", axis=0, tiled=True)
    top, low = own[None, :half, :width], own[None, half:, :width]
    top = jnp.concatenate([top, send(top, 1)])
    low = jnp.concatenate([low, send(low, 2)])
    top_in, low_in = send(top, 2), send(low, 1)
    weights = jnp.concatenate([
        jnp.concatenate([top, top_in]),
        jnp.stack([low[0], low_in[0], low[1], low_in[1]]),
    ], axis=1)
    aligned = shard_rows % 16 == 0 and down_rows == TILE
    expert_rows = 2 * tiles * shard_rows + width // TILE * down_rows

    def gather_expert(l):
        if aligned:
            one = call(
                pack_expert_kernel, "pack_expert", (1,),
                [pl.BlockSpec((1,) + w.shape[1:], lambda i: (l, 0, 0))
                 for w in (gate_weight, up_weight, down_weight)],
                whole((expert_rows, TILE)), struct((expert_rows, TILE), BF16), traffic=5 << 20,
            )(gate_weight, up_weight, down_weight)
        else:
            one = jnp.concatenate([
                w[l].reshape(w.shape[1], -1, TILE).transpose(1, 0, 2).reshape(-1, TILE)
                for w in (gate_weight, up_weight, down_weight)
            ])
        full = lax.all_gather(one, "shard", axis=0, tiled=True)
        full = full.reshape(shards, expert_rows, TILE)
        if aligned:
            return full, full
        split = 2 * tiles * shard_rows
        gate_up = full[:, :split].reshape(shards, 2 * tiles, shard_rows, TILE)
        down = full[:, split:].reshape(shards, width // TILE, down_rows, TILE)
        down = down.transpose(1, 0, 2, 3).reshape(width // TILE, tiles, TILE, TILE)
        return (
            gate_up.transpose(1, 0, 2, 3).reshape(1, -1, TILE),
            down.transpose(1, 0, 2, 3).reshape(tiles, width, TILE),
        )

    expert_full = [gather_expert(l) for l in range(local_experts)]

    dest_col, dest_row = call(
        functools.partial(slots_kernel, experts, capacity, stride), "slots", (1,),
        [whole((count, TOP)), whole((1, count)), whole((count, 1))],
        [whole((count, LANES)), whole((8, count))],
        [struct((count, LANES), jnp.int32), struct((8, count), jnp.int32)],
        flops=2 * 3 * count * count * LANES, traffic=1 << 20,
    )(routes, slot_order, slot_order.reshape(count, 1))

    steps = count // BLOCK
    weight_block = [
        pl.BlockSpec((1, width, width), lambda i, me, *rest, j=j: (me[0] ^ j, 0, 0))
        for j in range(4)
    ]
    output_block = weight_block.pop()
    small_block = pl.BlockSpec((width, LANES), lambda i, *rest: (0, width // LANES))
    wide = rows_of(BLOCK, width)
    table = rows_of(BLOCK, LANES)
    act = struct((count, width), BF16)
    queries, keys, values, normed_one, small_t = call(
        project_kernel, "project", (steps,),
        [wide] + weight_block + [small_block, table, table],
        [wide] * 3 + [pl.BlockSpec((width, BLOCK), lambda i, *rest: (0, i)), whole((LANES, width))],
        [act] * 3 + [struct((width, count), BF16), struct((LANES, width), F32)],
        flops=6 * count * width * width, traffic=12 << 20, prefetch=1,
    )(me, tokens, weights, weights, weights, own, cosine, sine)

    attn_mix, lse, residual, normed_two, tok = call(
        attend_kernel, "attend", (steps,),
        [wide, whole((count, width)), whole((count, width)), wide, output_block,
         small_block, whole((LANES, width)), rows_of(BLOCK, kinds), rows_of(BLOCK, TOP)],
        [wide, pl.BlockSpec((16, BLOCK), lambda i, *rest: (0, i)), wide, wide, table],
        [act, struct((16, count), F32), struct((count, width), F32), act,
         struct((count, LANES), F32)],
        scratch=[pltpu.VMEM((BLOCK, count), F32), pltpu.VMEM((BLOCK, width), BF16),
                 pltpu.VMEM((BLOCK, LANES), F32)],
        flops=30 << 30, traffic=16 << 20, trans=HEADS * count * count, prefetch=2,
    )(me, prefix, queries, keys, values, tokens, weights, own, small_t,
      previous_logits, routes)

    def exchange(parts):
        return [parts[0]] + [
            lax.ppermute(part, "expert", [(i, i ^ k) for i in range(owners)])
            for k, part in list(enumerate(parts))[1:]
        ]

    pair = whole((2, stride, width))
    pair_shape = struct((2, stride, width), BF16)

    def dispatch(l):
        parts = call(
            functools.partial(dispatch_kernel, local_experts, l), "dispatch", (owners,),
            [whole((count, width)), whole((count, width)), whole((count, LANES)),
             whole((count, TOP)), whole((8, count))],
            [pair] * owners, [pair_shape] * owners,
            scratch=[pltpu.VMEM((count, LANES), BF16)],
            flops=4 * owners * stride * count * width, traffic=6 << 20, prefetch=1,
        )(me, normed_two, cotangent, tok, routes, dest_row)
        return parts

    dispatched = [dispatch(l) for l in range(local_experts)]
    received = [exchange(parts) for parts in dispatched]

    chunks, chunk_rows = (shards, shard_rows) if aligned else (1, width)
    local = owners * stride

    def run_expert(l, rows, after):
        gate_up, down = expert_full[l]
        weights = [
            pl.BlockSpec((chunks, chunk_rows, TILE), lambda f, *rest, j=j: (0, j // 2 * tiles + 2 * f + j % 2, 0))
            for j in range(4)
        ] + [
            pl.BlockSpec((1, width, TILE), lambda f, *rest, j=j: (2 * f + j, 2 if aligned else 0, 0))
            for j in range(2)
        ]
        halves = aligned
        if halves:
            grad_shapes = [(shards // 2, expert_rows, TILE)] * 2
        elif aligned:
            grad_shapes = [(shards, expert_rows, TILE)]
        else:
            grad_shapes = [(1, 2 * tiles * width, TILE), (tiles, width, TILE)]
        *outs, = call(
            functools.partial(expert_kernel, owners, aligned, halves), "expert", (tiles // 2,),
            [pair] * owners + weights,
            [pair] * owners + [whole(g) for g in grad_shapes],
            [pair_shape] * owners + [struct(g, BF16) for g in grad_shapes],
            scratch=[pltpu.VMEM((local, width), BF16)] * 2 + [pltpu.VMEM((width, local), BF16)]
            + [pltpu.VMEM((local, width), F32)] * 2,
            flops=16 * local * width * ff, traffic=24 << 20, trans=local * ff, prefetch=1,
        )(core, *rows, gate_up, gate_up, gate_up, gate_up, down, down)
        grads = outs[owners:]
        if halves:
            keep, give = grads
        elif aligned:
            grad = grads[0]
        else:
            gate_up_g = grads[0].reshape(2 * tiles, shards, shard_rows, TILE).transpose(1, 0, 2, 3)
            down_g = grads[1].reshape(tiles, width // TILE, TILE, TILE).transpose(1, 0, 2, 3)
            down_g = down_g.reshape(width // TILE, shards, down_rows, TILE).transpose(1, 0, 2, 3)
            grad = jnp.concatenate(
                [gate_up_g.reshape(shards, -1, TILE), down_g.reshape(shards, -1, TILE)], axis=1
            )
        if halves:
            outs[:owners], keep, give, after = lax.optimization_barrier(
                (outs[:owners], keep, give, after)
            )
            grad = add(keep, lax.ppermute(give, "shard", [(i, i ^ 1) for i in range(shards)]))
        return outs[:owners], grad.reshape(-1, TILE), after

    def reduce_expert(grad):
        return lax.psum_scatter(
            grad, "shard", scatter_dimension=0, tiled=True,
            axis_index_groups=(
                None if len(grad) == shards * expert_rows
                else [list(range(c, shards, 2)) for c in range(2)]
            ),
        )

    returned = []
    expert_sums = []
    for l in range(local_experts):
        rows, _ = lax.optimization_barrier((received[l], dispatched[-1]))
        back, grad, ahead = run_expert(l, rows, (received[l + 1 :], returned))
        received[l + 1 :], returned = ahead
        back = exchange(back)
        if l + 1 == local_experts:
            back, grad = lax.optimization_barrier((back, grad))
        returned = returned + back
        expert_sums.append(reduce_expert(grad))

    mixed, previous_grad, residual_grad, heads_grad, delta, output_grad, small_grad = call(
        functools.partial(combine_kernel, experts, owners, local_experts), "combine", (steps,),
        [pair] * len(returned)
        + [wide, wide, wide, table, rows_of(BLOCK, TOP), table, wide, output_block,
           whole((LANES, width))],
        [wide, rows_of(BLOCK, kinds), wide, wide, pl.BlockSpec((16, BLOCK), lambda i, *rest: (0, i)),
         whole((width, width)), whole((width, LANES))],
        [act, struct((count, kinds), F32), struct((count, width), F32), act,
         struct((16, count), F32), struct((width, width), BF16), struct((width, LANES), F32)],
        scratch=[pltpu.VMEM((width, width), F32), pltpu.VMEM((width, LANES), F32),
                 pltpu.VMEM((8, width), F32)]
        + [pltpu.VMEM((local_experts, local, width), BF16)] * 2,
        flops=6 * count * 2 * local * width + 4 * count * width * width, traffic=24 << 20, prefetch=1,
    )(me, *returned, residual, normed_two, cotangent, tok,
      routes, dest_col, attn_mix, weights, small_t)

    def first_turn(grad):
        return send(grad[1::2, :half], 1), send(grad[2:, half:], 2)

    def second_turn(grad, came):
        top, low = add(grad[0::2, :half], came[0]), add(grad[:2, half:], came[1])
        return (top[0], low[0]), (send(top[1], 2), send(low[1], 1))

    def join(mine, came):
        return jnp.concatenate([add(a, b) for a, b in zip(mine, came)], axis=0)

    pairs = width // LANES // 2
    columns = pairs * LANES
    half_out = pl.BlockSpec((count, LANES), lambda i, *rest: (0, i))
    parts = []
    dense_grads = []
    moved = ()
    for start in (0, pairs):
        pair_block = pl.BlockSpec((count, LANES), lambda i, *rest, start=start: (0, i + start))
        *three, dense_grad = call(
            functools.partial(attend_back_kernel, start), "attend_back", (pairs,),
            [pair_block] * 4
            + [whole((16, count))] * 2
            + [whole((count, LANES))] * 2
            + [whole((width, count)),
               pl.BlockSpec((width, columns), lambda i, *rest, start=start: (0, start // pairs))],
            [half_out] * 3 + [whole((owners, width, columns))],
            [struct((count, columns), BF16)] * 3 + [struct((owners, width, columns), BF16)],
            scratch=[pltpu.VMEM((count, count), BF16), pltpu.VMEM((count, LANES), F32)],
            flops=30 << 30, traffic=6 << 20, trans=HEADS // 2 * count * count, prefetch=2,
        )(me, prefix, queries, keys, values, heads_grad, lse, delta, cosine, sine, normed_one,
          output_grad)
        if start:
            three, moved, expert_sums[0] = lax.optimization_barrier((three, moved, expert_sums[0]))
        parts += three
        dense_grads.append(dense_grad)
        if start == 0:
            moved = first_turn(dense_grad)
    mine_a, moved_a = second_turn(dense_grads[0], moved)
    moved_b = first_turn(dense_grads[1])

    half_wide = rows_of(BLOCK, columns)
    tokens_grad, small_grad = call(
        project_back_kernel, "project_back", (steps,),
        [wide] + [half_wide] * 6 + [wide] + weight_block
        + [whole((LANES, width)), whole((width, LANES))],
        [wide, whole((width, LANES))],
        [struct((count, width), F32), struct((width, LANES), BF16)],
        scratch=[pltpu.VMEM((8, width), F32)],
        flops=6 * count * width * width, traffic=18 << 20, prefetch=1,
    )(me, tokens, *parts, residual_grad, weights, weights, weights, small_t, small_grad)
    small_grad, moved_a, moved_b = lax.optimization_barrier((small_grad, moved_a, moved_b))
    mine_b, moved_b = second_turn(dense_grads[1], moved_b)
    quarters = [join(mine_a, moved_a), join(mine_b, moved_b)]
    quarter = jnp.concatenate(quarters + [small_grad], axis=1)
    by_core = quarter.reshape(shards // 2, 2, shard_rows, width + LANES)
    keep, give = (
        lax.dynamic_index_in_dim(by_core, c, axis=1, keepdims=False) for c in (core[0], 1 - core[0])
    )
    quarter = add(keep, lax.ppermute(give, "shard", [(i, i ^ 1) for i in range(shards)]))
    quarter, expert_sums = lax.optimization_barrier((quarter, expert_sums))
    quarter = lax.psum_scatter(
        quarter.reshape(width // 2, width + LANES), "shard", scatter_dimension=0, tiled=True,
        axis_index_groups=[list(range(c, shards, 2)) for c in range(2)],
    )
    gathered = jnp.stack([quarter] + [send(quarter, k) for k in range(1, owners)]).astype(F32)
    dense = [
        lax.dynamic_index_in_dim(gathered[:, :, :width], me[0] ^ j, keepdims=False)
        for j in range(4)
    ]
    small = jnp.sum(gathered[:, :, width:], axis=0)
    if aligned:
        out_shapes = [w.shape for w in (gate_weight, up_weight, down_weight)]
        gate_sum, up_sum, down_sum = call(
            unpack_expert_kernel, "unpack", (1,),
            [whole((expert_rows, TILE))] * local_experts,
            [whole(o) for o in out_shapes], [struct(o, F32) for o in out_shapes],
            traffic=8 << 20,
        )(*expert_sums)
    else:
        split = 2 * tiles * shard_rows
        total = jnp.stack(expert_sums).astype(F32)
        gate_sum, up_sum = (
            part.reshape(local_experts, tiles, shard_rows, TILE).transpose(0, 2, 1, 3).reshape(
                local_experts, shard_rows, ff
            )
            for part in (total[:, : split // 2], total[:, split // 2 : split])
        )
        down_sum = total[:, split:].reshape(local_experts, width // TILE, down_rows, TILE)
        down_sum = down_sum.transpose(0, 2, 1, 3).reshape(local_experts, down_rows, width)
    return (
        mixed,
        tokens_grad,
        previous_grad,
        dense[0],
        dense[1],
        dense[2],
        dense[3],
        small[:, 0:kinds],
        small[:, kinds : kinds + 4],
        small[:, 18:20].T,
        small[:, 16],
        small[:, 17],
        gate_sum,
        up_sum,
        down_sum,
    )


def solution(mesh):
    rows = P(("expert", "shard"), None)
    expert = P("expert", "shard", None)
    flat = P("shard", None)
    return jax.shard_map(
        body,
        mesh=mesh,
        in_specs=(
            rows, rows, rows, P(("expert", "shard")), rows, P("shard"), flat, flat, flat, flat,
            P("shard"), flat, flat, P(None, "shard"), expert, expert, expert, rows,
        ),
        out_specs=(
            rows, rows, rows, flat, flat, flat, flat, flat, flat, P(None, "shard"), P("shard"),
            P("shard"), expert, expert, expert,
        ),
        check_vma=False,
    )
```
